32 devices in a mesh: row: 2 (over y), col: 16 (over z, x, core).
Axes of the slice: x: 2, y: 2, z: 4, core: 2. Of those that a mesh axis runs over, the one named last changes fastest.
Arguments:
- right_side: float32 [2048, 4096], P('row', 'col'), may hold values from -8 to 8
- factor_panels: float32 [4, 256, 2048], P(None, 'col', 'row'), may hold values from -0.1875 to 0.1875
- inverses: float32 [4, 256, 256], P(None, 'col'), may hold values from -0.5 to 1.6, as said below
Outputs:
- solved: float32 [2048, 4096], P('row', 'col')
The draws below stay inside these ranges and needn't reach their ends.
Inputs may be any that keep to these rules, and one draw needn't show every extreme that they name: inverses[k] is lower triangular with a diagonal between 0.6 and 1.6 and independent entries below it.
All inputs are finite; a program needn't handle non-finite values.
Results may differ from the reference program's by a relative error of at most 0.0001.
Values sent between devices are 32-bit elements; how exact they have to be, the bound alone decides.
No kernel may reach another device: no remote copies, remote signals or barrier semaphores. Data moves between devices by JAX's collectives and lax.ppermute only.
A program may use at most 64 MiB of HBM per device.

```python
import jax
import jax.numpy as jnp
from jax import lax

NB = 256
PANELS = 4
ROW_DEV = 1024
RHS_DEV = 256
ROWS = 2048
RHS = 4096
N_ROW = 2


def draw_inverses(key, part):
    first, second = jax.random.split(jax.random.fold_in(key, 7))
    diagonal = jax.random.uniform(first, (PANELS, NB), jnp.float32, 0.6, 1.6)
    below = jax.random.normal(second, (PANELS, NB, NB), jnp.float32) * (0.6 / NB ** 0.5)
    below = jnp.clip(below, -0.5, 0.5)
    row_index = jnp.arange(NB)[:, None]
    col_index = jnp.arange(NB)[None, :]
    lower = jnp.where(row_index > col_index, below, 0.0)
    eye = (row_index == col_index).astype(jnp.float32)
    return lower + diagonal[:, :, None] * eye


def level_of(rng, extent, shards, low, largest):
    gain, own = 1.0, jax.random.fold_in(rng, 6)
    for axis_at, shards_of in shards:
        steps = jnp.exp(jax.random.uniform(jax.random.fold_in(own, axis_at), (shards_of,), jnp.float32, low / len(shards), largest / len(shards)))
        gain = gain * jnp.repeat(steps, extent[axis_at] // shards_of).reshape([-1 if axis == axis_at else 1 for axis in range(len(extent))])
    return gain


def centred(rng, dims, scale, reach, pieces=(), held_as=jnp.bfloat16):
    level = level_of(rng, dims, pieces, -0.22, 0.18) if pieces else 1.0
    entries = jax.random.normal(rng, dims, jnp.float32) * scale * level
    return jnp.minimum(jnp.maximum(entries, -reach), reach).astype(held_as)


def setup_inputs(seed: int = 0) -> dict:
    arg_keys = jax.random.split(jax.random.key(seed), 4)
    return {
        "right_side": centred(arg_keys[0], (ROWS, RHS), 1.0, 8.0, ((0, 2), (1, 16)), jnp.float32),
        "factor_panels": centred(arg_keys[1], (PANELS, NB, ROWS), (PANELS * NB) ** -0.5, 0.1875, ((1, 16), (2, 2)), jnp.float32),
        "inverses": draw_inverses(jax.random.fold_in(arg_keys[3], 71), 0),
    }


def solve_columns(columns, factor_panels, inverses):
    blocks_dev = ROW_DEV // NB
    stored_block = jnp.arange(ROWS, dtype=jnp.int32) // NB
    rank = (stored_block % blocks_dev) * N_ROW + stored_block // blocks_dev
    work = columns
    for panel in range(PANELS):
        stored = (panel % N_ROW) * blocks_dev + panel // N_ROW
        current = work[stored * NB:(stored + 1) * NB]
        answer = jnp.dot(inverses[panel], current, precision=lax.Precision.HIGHEST, preferred_element_type=jnp.float32)
        work = work.at[stored * NB:(stored + 1) * NB].set(answer)
        update = lax.dot_general(factor_panels[panel], answer, (((0,), (0,)), ((), ())), precision=lax.Precision.HIGHEST, preferred_element_type=jnp.float32)
        work = work - jnp.where((rank > panel)[:, None], update, jnp.zeros_like(update))
    return work


def reference(right_side, factor_panels, inverses):
    width = RHS_DEV
    stacked = right_side.reshape(ROWS, RHS // width, width).transpose(1, 0, 2)
    result = lax.map(lambda columns: solve_columns(columns, factor_panels, inverses), stacked)
    return result.transpose(1, 0, 2).reshape(ROWS, RHS)
```

```python
import functools

import jax
import jax.numpy as jnp
from jax import lax
from jax.experimental import pallas as pl
from jax.experimental.pallas import tpu as pltpu
from jax.sharding import PartitionSpec as P


def ring_place(chip, chips):
    return jnp.where(chip % 2 == 0, chip // 2, chips - 1 - chip // 2)


def ring_chip(place, chips):
    up = 2 * place
    down = 2 * (chips - 1 - place) + 1
    if isinstance(place, int):
        return up if place < chips // 2 else down
    return jnp.where(place < chips // 2, up, down)


def split(value):
    high = value.astype(jnp.bfloat16)
    low = (value - high.astype(jnp.float32)).astype(jnp.bfloat16)
    return high, low


def dot3(left, right, dims):
    mult = functools.partial(
        lax.dot_general, dimension_numbers=(dims, ((), ())), preferred_element_type=jnp.float32
    )
    return mult(left[0], right[0]) + (mult(left[0], right[1]) + mult(left[1], right[0]))


def ring(first, half_core, chips):
    steps = chips // 2
    nearest = []
    for place in range(chips):
        here = ring_chip(place, chips)
        nearest.append((2 * here, 2 * ring_chip((place + 1) % chips, chips)))
        nearest.append((2 * here + 1, 2 * ring_chip((place - 1) % chips, chips) + 1))
    swap = [(i, i ^ 1) for i in range(2 * chips)]
    moving = first
    pieces = []
    for step in range(1, steps + 1):
        last = step == steps
        pairs = [p for p in nearest if not last or p[0] % 2 == half_core]
        moving = lax.ppermute(moving, "col", pairs)
        across = [p for p in swap if not last or p[0] % 2 == half_core]
        pieces.append((moving, lax.ppermute(moving, "col", across)))
    return pieces


def streams(chips):
    core = lax.axis_index("col") % 2
    here = ring_place(lax.axis_index("col") // 2, chips)
    found = [(lax.axis_index("col") // 2, core)]
    steps = chips // 2
    for step in range(1, steps + 1):
        turn = step * (1 - 2 * core)
        mine = ring_chip((here - turn + chips) % chips, chips)
        other = ring_chip((here + turn + chips) % chips, chips)
        if step < steps:
            found.append((mine, core))
            found.append((other, 1 - core))
        else:
            found.append((mine, None))
    return found


def assemble(piece_refs, mat_ref, chips, half_core):
    depth = piece_refs[0].shape[2]

    def put(row, value):
        mat_ref[:, pl.ds(pl.multiple_of(row, value.shape[1]), value.shape[1]), :] = value

    for at, (chip, core) in enumerate(streams(chips)):
        halves = []
        for half in range(2):
            if core is None:
                halves.append(piece_refs[at][half ^ half_core] + piece_refs[at + 1][half ^ half_core])
            elif depth % 8 == 0:
                halves.append(piece_refs[at][jnp.where(core == 0, half, 1 - half)])
            else:
                halves.append(jnp.where(core == 0, piece_refs[at][half], piece_refs[at][1 - half]))
        if depth % 8 == 0:
            for half in range(2):
                put((2 * chip + half) * depth, halves[half])
        else:
            put(2 * chip * depth, jnp.concatenate(halves, axis=1))


def solve_kernel(panels, group_count, locals_, chips, *refs):
    piece_refs, right_ref = refs[: chips + 1], refs[chips + 1]
    received = refs[chips + 2 : -3]
    x_ref, mat_ref, work_ref = refs[-3:]
    nb = right_ref.shape[0] // locals_
    me = lax.axis_index("row")
    assemble(piece_refs, mat_ref, chips, 0)
    for shift in range(group_count):
        owner = (me + shift) % group_count
        source = right_ref if shift == 0 else received[shift - 1]
        for local in range(locals_):
            rank = local * group_count + owner

            @pl.when(rank < panels)
            def _(rank=rank, local=local, source=source):
                work_ref[rank] = source[local * nb : (local + 1) * nb]

    solved = []
    for panel in range(panels):
        current = work_ref[panel]
        for before in range(panel):
            tri = panels + panel * (panel - 1) // 2 + before
            current = current - dot3(split(mat_ref[tri]), solved[before], ((0,), (0,)))
        answer = dot3(split(mat_ref[panel]), split(current), ((1,), (0,)))
        x_ref[panel] = answer
        solved.append(split(answer))


def update_kernel(panels, group_count, locals_, chips, *refs):
    *piece_refs, right_ref, x_ref, out_ref, mat_ref = refs
    nb = x_ref.shape[1]
    sure = panels // group_count
    me = lax.axis_index("row")
    assemble(piece_refs, mat_ref, chips, 1)
    total = right_ref[sure * nb :]
    for panel in range(panels):
        total = total - dot3(split(mat_ref[panel]), split(x_ref[panel]), ((0,), (0,)))
    out_ref[sure * nb :] = total
    for local in range(locals_):
        rank = local * group_count + me

        @pl.when(rank < panels)
        def _(rank=rank, local=local):
            out_ref[local * nb : (local + 1) * nb] = x_ref[rank]


def per_device(right_side, factor_panels, inverses):
    group_count = lax.axis_size("row")
    chips = lax.axis_size("col") // 2
    me = lax.axis_index("row")
    panels, depth, rows = factor_panels.shape
    nb = inverses.shape[2]
    columns = right_side.shape[1]
    locals_ = -(-panels // group_count)
    swap = [(i, i ^ 1) for i in range(2 * chips)]
    shifts = [
        [((g + shift) % group_count, g) for g in range(group_count)] for shift in range(1, group_count)
    ]

    factor_other = lax.ppermute(factor_panels, "col", swap)
    wanted = [
        (local, panel)
        for local in range(locals_)
        for panel in range(min(local * group_count + group_count - 1, panels - 1))
    ]
    tri_own = jnp.stack([factor_panels[k, :, l * nb : (l + 1) * nb] for l, k in wanted])
    tri = [tri_own] + [lax.ppermute(tri_own, "row", pairs) for pairs in shifts]
    above = right_side[: locals_ * nb]
    received = [lax.ppermute(above, "row", pairs) for pairs in shifts]

    sure = panels // group_count * nb
    trail_first = jnp.stack([factor_panels[:, :, sure:], factor_other[:, :, sure:]])
    blocks = []
    for rank in range(1, panels):
        local, owner = divmod(rank, group_count)
        for panel in range(rank):
            at = wanted.index((local, panel))
            value = tri[0][at]
            for shift in range(1, group_count):
                value = jnp.where((me + shift) % group_count == owner, tri[shift][at], value)
            blocks.append(value)
    near_own = jnp.concatenate([inverses, jnp.stack(blocks)])
    near_first = jnp.stack([near_own, lax.ppermute(near_own, "col", swap)])

    near = ring(near_first, 0, chips)
    trail = ring(trail_first, 1, chips)

    near_pieces = [near_first] + [p for pair in near for p in pair]
    trail_pieces = [trail_first] + [p for pair in trail for p in pair]
    vmem = pl.BlockSpec(memory_space=pltpu.VMEM)
    sizes = (panels, group_count, locals_, chips)
    count = near_first.shape[1]
    solved = pl.pallas_call(
        functools.partial(solve_kernel, *sizes),
        out_shape=jax.ShapeDtypeStruct((panels, nb, columns), jnp.float32),
        in_specs=[vmem] * (len(near_pieces) + group_count),
        out_specs=vmem,
        scratch_shapes=[
            pltpu.VMEM((count, nb, nb), jnp.float32),
            pltpu.VMEM((panels, nb, columns), jnp.float32),
        ],
        cost_estimate=pl.CostEstimate(flops=6 * count * nb * nb * columns, bytes_accessed=6 << 20, transcendentals=0),
        name="solve",
    )(*near_pieces, above, *received)
    return pl.pallas_call(
        functools.partial(update_kernel, *sizes),
        out_shape=jax.ShapeDtypeStruct(right_side.shape, jnp.float32),
        in_specs=[vmem] * (len(trail_pieces) + 2),
        out_specs=vmem,
        scratch_shapes=[pltpu.VMEM((panels, nb, rows - sure), jnp.float32)],
        cost_estimate=pl.CostEstimate(
            flops=6 * panels * nb * columns * (rows - sure), bytes_accessed=6 << 20, transcendentals=0
        ),
        name="update",
    )(*trail_pieces, right_side, solved)


def solution(mesh):
    in_specs = (P("row", "col"), P(None, "col", "row"), P(None, "col", None))
    out_specs = P("row", "col")
    return jax.shard_map(
        per_device, mesh=mesh, in_specs=in_specs, out_specs=out_specs, check_vma=False
    )
```

```python
import functools

import jax
import jax.numpy as jnp
from jax import lax
from jax.experimental import pallas as pl
from jax.experimental.pallas import tpu as pltpu
from jax.sharding import PartitionSpec as P


def ring_place(chip, chips):
    return jnp.where(chip % 2 == 0, chip // 2, chips - 1 - chip // 2)


def ring_chip(place, chips):
    up = 2 * place
    down = 2 * (chips - 1 - place) + 1
    if isinstance(place, int):
        return up if place < chips // 2 else down
    return jnp.where(place < chips // 2, up, down)


def split(value):
    high = value.astype(jnp.bfloat16)
    low = (value - high.astype(jnp.float32)).astype(jnp.bfloat16)
    return high, low


def dot3(left, right, dims):
    mult = functools.partial(
        lax.dot_general, dimension_numbers=(dims, ((), ())), preferred_element_type=jnp.float32
    )
    return mult(left[0], right[0]) + (mult(left[0], right[1]) + mult(left[1], right[0]))


def ring(first, half_core, chips):
    steps = chips // 2
    nearest = []
    for place in range(chips):
        here = ring_chip(place, chips)
        nearest.append((2 * here, 2 * ring_chip((place + 1) % chips, chips)))
        nearest.append((2 * here + 1, 2 * ring_chip((place - 1) % chips, chips) + 1))
    swap = [(i, i ^ 1) for i in range(2 * chips)]
    moving = first
    pieces = []
    for step in range(1, steps + 1):
        last = step == steps
        pairs = [p for p in nearest if not last or p[0] % 2 == half_core]
        moving = lax.ppermute(moving, "col", pairs)
        across = [p for p in swap if not last or p[0] % 2 == half_core]
        pieces.append((moving, lax.ppermute(moving, "col", across)))
    return pieces


def streams(chips):
    core = lax.axis_index("col") % 2
    here = ring_place(lax.axis_index("col") // 2, chips)
    found = [(lax.axis_index("col") // 2, core)]
    steps = chips // 2
    for step in range(1, steps + 1):
        turn = step * (1 - 2 * core)
        mine = ring_chip((here - turn + chips) % chips, chips)
        other = ring_chip((here + turn + chips) % chips, chips)
        if step < steps:
            found.append((mine, core))
            found.append((other, 1 - core))
        else:
            found.append((mine, None))
    return found


def assemble(piece_refs, mat_ref, chips, half_core):
    depth = piece_refs[0].shape[2]

    def put(row, value):
        mat_ref[:, pl.ds(pl.multiple_of(row, value.shape[1]), value.shape[1]), :] = value

    for at, (chip, core) in enumerate(streams(chips)):
        halves = []
        for half in range(2):
            if core is None:
                halves.append(piece_refs[at][half ^ half_core] + piece_refs[at + 1][half ^ half_core])
            elif depth % 8 == 0:
                halves.append(piece_refs[at][jnp.where(core == 0, half, 1 - half)])
            else:
                halves.append(jnp.where(core == 0, piece_refs[at][half], piece_refs[at][1 - half]))
        if depth % 8 == 0:
            for half in range(2):
                put((2 * chip + half) * depth, halves[half])
        else:
            put(2 * chip * depth, jnp.concatenate(halves, axis=1))


def solve_kernel(panels, group_count, locals_, chips, *refs):
    piece_refs, right_ref = refs[: chips + 1], refs[chips + 1]
    received = refs[chips + 2 : -3]
    x_ref, mat_ref, work_ref = refs[-3:]
    nb = right_ref.shape[0] // locals_
    me = lax.axis_index("row")
    assemble(piece_refs, mat_ref, chips, 0)
    for shift in range(group_count):
        owner = (me + shift) % group_count
        source = right_ref if shift == 0 else received[shift - 1]
        for local in range(locals_):
            rank = local * group_count + owner

            @pl.when(rank < panels)
            def _(rank=rank, local=local, source=source):
                work_ref[rank] = source[local * nb : (local + 1) * nb]

    solved = []
    for panel in range(panels):
        current = work_ref[panel]
        for before in range(panel):
            tri = panels + panel * (panel - 1) // 2 + before
            current = current - dot3(split(mat_ref[tri]), solved[before], ((0,), (0,)))
        answer = dot3(split(mat_ref[panel]), split(current), ((1,), (0,)))
        x_ref[panel] = answer
        solved.append(split(answer))


def update_kernel(panels, group_count, locals_, chips, *refs):
    *piece_refs, right_ref, x_ref, out_ref, mat_ref = refs
    nb = x_ref.shape[1]
    sure = panels // group_count
    me = lax.axis_index("row")
    assemble(piece_refs, mat_ref, chips, 1)
    total = right_ref[sure * nb :]
    for panel in range(panels):
        total = total - dot3(split(mat_ref[panel]), split(x_ref[panel]), ((0,), (0,)))
    out_ref[sure * nb :] = total
    for local in range(locals_):
        rank = local * group_count + me

        @pl.when(rank < panels)
        def _(rank=rank, local=local):
            out_ref[local * nb : (local + 1) * nb] = x_ref[rank]


def per_device(right_side, factor_panels, inverses):
    group_count = lax.axis_size("row")
    chips = lax.axis_size("col") // 2
    me = lax.axis_index("row")
    panels, _, rows = factor_panels.shape
    nb = inverses.shape[2]
    columns = right_side.shape[1]
    locals_ = -(-panels // group_count)
    swap = [(i, i ^ 1) for i in range(2 * chips)]
    shifts = [
        [((g + shift) % group_count, g) for g in range(group_count)] for shift in range(1, group_count)
    ]

    factor_other = lax.ppermute(factor_panels, "col", swap)
    wanted = [
        (local, panel)
        for local in range(locals_)
        for panel in range(min(local * group_count + group_count - 1, panels - 1))
    ]
    tri_own = jnp.stack([factor_panels[k, :, l * nb : (l + 1) * nb] for l, k in wanted])
    tri = [tri_own] + [lax.ppermute(tri_own, "row", pairs) for pairs in shifts]
    above = right_side[: locals_ * nb]
    received = [lax.ppermute(above, "row", pairs) for pairs in shifts]

    sure = panels // group_count * nb
    trail_first = jnp.stack([factor_panels[:, :, sure:], factor_other[:, :, sure:]])
    blocks = []
    for rank in range(1, panels):
        local, owner = divmod(rank, group_count)
        for panel in range(rank):
            at = wanted.index((local, panel))
            value = tri[0][at]
            for shift in range(1, group_count):
                value = jnp.where((me + shift) % group_count == owner, tri[shift][at], value)
            blocks.append(value)
    near_own = jnp.concatenate([inverses, jnp.stack(blocks)])
    near_first = jnp.stack([near_own, lax.ppermute(near_own, "col", swap)])

    near = ring(near_first, 0, chips)
    trail = ring(trail_first, 1, chips)

    near_pieces = [near_first] + [p for pair in near for p in pair]
    trail_pieces = [trail_first] + [p for pair in trail for p in pair]
    vmem = pl.BlockSpec(memory_space=pltpu.VMEM)
    sizes = (panels, group_count, locals_, chips)
    count = near_first.shape[1]
    solved = pl.pallas_call(
        functools.partial(solve_kernel, *sizes),
        out_shape=jax.ShapeDtypeStruct((panels, nb, columns), jnp.float32),
        in_specs=[vmem] * (len(near_pieces) + group_count),
        out_specs=vmem,
        scratch_shapes=[
            pltpu.VMEM((count, nb, nb), jnp.float32),
            pltpu.VMEM((panels, nb, columns), jnp.float32),
        ],
        cost_estimate=pl.CostEstimate(flops=6 * count * nb * nb * columns, bytes_accessed=6 << 20, transcendentals=0),
        compiler_params=pltpu.CompilerParams(vmem_limit_bytes=16 << 20),
        name="solve",
    )(*near_pieces, above, *received)
    return pl.pallas_call(
        functools.partial(update_kernel, *sizes),
        out_shape=jax.ShapeDtypeStruct(right_side.shape, jnp.float32),
        in_specs=[vmem] * (len(trail_pieces) + 2),
        out_specs=vmem,
        scratch_shapes=[pltpu.VMEM((panels, nb, rows - sure), jnp.float32)],
        cost_estimate=pl.CostEstimate(
            flops=6 * panels * nb * columns * (rows - sure), bytes_accessed=6 << 20, transcendentals=0
        ),
        compiler_params=pltpu.CompilerParams(vmem_limit_bytes=16 << 20),
        name="update",
    )(*trail_pieces, right_side, solved)


def solution(mesh):
    in_specs = (P("row", "col"), P(None, "col", "row"), P(None, "col", None))
    out_specs = P("row", "col")

    return jax.shard_map(per_device, mesh=mesh, in_specs=in_specs, out_specs=out_specs, check_vma=False)
```

```python
import functools

import jax
import jax.numpy as jnp
from jax import lax
from jax.experimental import pallas as pl
from jax.experimental.pallas import tpu as pltpu
from jax.sharding import PartitionSpec as P


def ring_place(chip, chips):
    return jnp.where(chip % 2 == 0, chip // 2, chips - 1 - chip // 2)


def ring_chip(place, chips):
    up = 2 * place
    down = 2 * (chips - 1 - place) + 1
    if isinstance(place, int):
        return up if place < chips // 2 else down
    return jnp.where(place < chips // 2, up, down)


def split(value):
    high = value.astype(jnp.bfloat16)
    low = (value - high.astype(jnp.float32)).astype(jnp.bfloat16)
    return high, low


def dot3(left, right, dims):
    mult = functools.partial(
        lax.dot_general, dimension_numbers=(dims, ((), ())), preferred_element_type=jnp.float32
    )
    return mult(left[0], right[0]) + (mult(left[0], right[1]) + mult(left[1], right[0]))


def ring(first, chips):
    steps = chips // 2
    nearest = []
    for place in range(chips):
        here = ring_chip(place, chips)
        nearest.append((2 * here, 2 * ring_chip((place + 1) % chips, chips)))
        nearest.append((2 * here + 1, 2 * ring_chip((place - 1) % chips, chips) + 1))
    swap = [(i, i ^ 1) for i in range(2 * chips)]
    moving = first
    pieces = [first]
    for step in range(1, steps + 1):
        moving = lax.ppermute(moving if step < steps else moving[0], "col", nearest)
        pieces += [moving, lax.ppermute(moving, "col", swap)]
    return pieces


def streams(chips):
    core = lax.axis_index("col") % 2
    here = ring_place(lax.axis_index("col") // 2, chips)
    found = [(lax.axis_index("col") // 2, core)]
    for step in range(1, chips // 2 + 1):
        turn = step * (1 - 2 * core)
        found.append((ring_chip((here - turn + chips) % chips, chips), core))
        found.append((ring_chip((here + turn + chips) % chips, chips), 1 - core))
    return found


def assemble(piece_refs, mat_ref, chips):
    depth = piece_refs[0].shape[2]

    def put(row, value):
        mat_ref[:, pl.ds(pl.multiple_of(row, value.shape[1]), value.shape[1]), :] = value

    table = streams(chips)
    for at, (chip, core) in enumerate(table):
        ref = piece_refs[at]
        if at < chips - 1:
            if depth % 8 == 0:
                for half in range(2):
                    put((2 * chip + half) * depth, ref[jnp.where(core == 0, half, 1 - half)])
                continue
            pair = [ref[0], ref[1]]
        else:
            if depth % 8 == 0:
                put((2 * chip + core) * depth, ref[...])
                continue
            if at == chips:
                continue
            pair = [ref[...], piece_refs[at + 1][...]]
        low, high = jnp.where(core == 0, pair[0], pair[1]), jnp.where(core == 0, pair[1], pair[0])
        put(2 * chip * depth, jnp.concatenate([low, high], axis=1))


def solve_kernel(panels, group_count, locals_, chips, *refs):
    count = chips + 1
    inverse_refs, tri_refs, right_ref = refs[:count], refs[count : 2 * count], refs[2 * count]
    received = refs[2 * count + 1 : -4]
    x_ref, inv_ref, tri_ref, work_ref = refs[-4:]
    nb = right_ref.shape[0] // locals_
    me = lax.axis_index("row")
    assemble(inverse_refs, inv_ref, chips)
    assemble(tri_refs, tri_ref, chips)
    for shift in range(group_count):
        owner = (me + shift) % group_count
        source = right_ref if shift == 0 else received[shift - 1]
        for local in range(locals_):
            rank = local * group_count + owner

            @pl.when(rank < panels)
            def _(rank=rank, local=local, source=source):
                work_ref[rank] = source[local * nb : (local + 1) * nb]

    solved = []
    for panel in range(panels):
        current = work_ref[panel]
        for before in range(panel):
            tri = panel * (panel - 1) // 2 + before
            current = current - dot3(split(tri_ref[tri]), solved[before], ((0,), (0,)))
        answer = dot3(split(inv_ref[panel]), split(current), ((1,), (0,)))
        x_ref[panel] = answer
        solved.append(split(answer))


def update_kernel(panels, group_count, locals_, chips, *refs):
    *piece_refs, right_ref, x_ref, out_ref, mat_ref = refs
    nb = x_ref.shape[1]
    sure = panels // group_count
    me = lax.axis_index("row")
    assemble(piece_refs, mat_ref, chips)
    total = right_ref[sure * nb :]
    for panel in range(panels):
        total = total - dot3(split(mat_ref[panel]), split(x_ref[panel]), ((0,), (0,)))
    out_ref[sure * nb :] = total
    for local in range(locals_):
        rank = local * group_count + me

        @pl.when(rank < panels)
        def _(rank=rank, local=local):
            out_ref[local * nb : (local + 1) * nb] = x_ref[rank]


def per_device(right_side, factor_panels, inverses):
    group_count = lax.axis_size("row")
    chips = lax.axis_size("col") // 2
    me = lax.axis_index("row")
    panels, _, rows = factor_panels.shape
    nb = inverses.shape[2]
    columns = right_side.shape[1]
    locals_ = -(-panels // group_count)
    swap = [(i, i ^ 1) for i in range(2 * chips)]
    shifts = [
        [((g + shift) % group_count, g) for g in range(group_count)] for shift in range(1, group_count)
    ]

    inverse_pieces = jnp.stack([inverses, lax.ppermute(inverses, "col", swap)])
    factor_other = lax.ppermute(factor_panels, "col", swap)
    deep = min((locals_ - 1) * group_count + group_count - 1, panels - 1)
    tri_own = factor_panels[:deep, :, : locals_ * nb]
    tri = [tri_own] + [lax.ppermute(tri_own, "row", pairs) for pairs in shifts]
    above = right_side[: locals_ * nb]
    received = [lax.ppermute(above, "row", pairs) for pairs in shifts]

    sure = panels // group_count * nb
    trail_first = jnp.stack([factor_panels[:, :, sure:], factor_other[:, :, sure:]])
    blocks = []
    for rank in range(1, panels):
        local, owner = divmod(rank, group_count)
        for panel in range(rank):
            value = tri[0]
            for shift in range(1, group_count):
                value = jnp.where((me + shift) % group_count == owner, tri[shift], value)
            blocks.append(value[panel, :, local * nb : (local + 1) * nb])
    tri_half = jnp.stack(blocks)
    tri_first = jnp.stack([tri_half, lax.ppermute(tri_half, "col", swap)])

    inverse_pieces = ring(inverse_pieces, chips)
    tri_pieces = ring(tri_first, chips)
    trail_pieces = ring(trail_first, chips)
    vmem = pl.BlockSpec(memory_space=pltpu.VMEM)
    sizes = (panels, group_count, locals_, chips)
    count = panels + len(blocks)
    solved = pl.pallas_call(
        functools.partial(solve_kernel, *sizes),
        out_shape=jax.ShapeDtypeStruct((panels, nb, columns), jnp.float32),
        in_specs=[vmem] * (len(inverse_pieces) + len(tri_pieces) + group_count),
        out_specs=vmem,
        scratch_shapes=[
            pltpu.VMEM((panels, nb, nb), jnp.float32),
            pltpu.VMEM((len(blocks), nb, nb), jnp.float32),
            pltpu.VMEM((panels, nb, columns), jnp.float32),
        ],
        cost_estimate=pl.CostEstimate(flops=6 * count * nb * nb * columns, bytes_accessed=6 << 20, transcendentals=0),
        compiler_params=pltpu.CompilerParams(vmem_limit_bytes=16 << 20),
        name="solve",
    )(*inverse_pieces, *tri_pieces, above, *received)
    return pl.pallas_call(
        functools.partial(update_kernel, *sizes),
        out_shape=jax.ShapeDtypeStruct(right_side.shape, jnp.float32),
        in_specs=[vmem] * (len(trail_pieces) + 2),
        out_specs=vmem,
        scratch_shapes=[pltpu.VMEM((panels, nb, rows - sure), jnp.float32)],
        cost_estimate=pl.CostEstimate(
            flops=6 * panels * nb * columns * (rows - sure), bytes_accessed=6 << 20, transcendentals=0
        ),
        compiler_params=pltpu.CompilerParams(vmem_limit_bytes=16 << 20),
        name="update",
    )(*trail_pieces, right_side, solved)


def solution(mesh):
    in_specs = (P("row", "col"), P(None, "col", "row"), P(None, "col", None))
    out_specs = P("row", "col")

    return jax.shard_map(per_device, mesh=mesh, in_specs=in_specs, out_specs=out_specs, check_vma=False)
```

```python
import functools

import jax
import jax.numpy as jnp
from jax import lax
from jax.experimental import pallas as pl
from jax.experimental.pallas import tpu as pltpu
from jax.sharding import PartitionSpec as P

ROWS = ((0,), (0,))
PLAIN = ((1,), (0,))


def ring_place(chip, chips):
    return jnp.where(chip % 2 == 0, chip // 2, chips - 1 - chip // 2)


def ring_chip(place, chips):
    up = 2 * place
    down = 2 * (chips - 1 - place) + 1
    if isinstance(place, int):
        return up if place < chips // 2 else down
    return jnp.where(place < chips // 2, up, down)


def split(value):
    high = value.astype(jnp.bfloat16)
    low = (value - high.astype(jnp.float32)).astype(jnp.bfloat16)
    return high, low


def dot3(left, right, dims):
    mult = functools.partial(
        lax.dot_general, dimension_numbers=(dims, ((), ())), preferred_element_type=jnp.float32
    )
    return mult(left[0], right[0]) + (mult(left[0], right[1]) + mult(left[1], right[0]))


def kernel_call(body, out_shapes, scratch, operands, flops=0):
    vmem = pl.BlockSpec(memory_space=pltpu.VMEM)
    return pl.pallas_call(
        body,
        out_shape=out_shapes,
        in_specs=[vmem] * len(operands),
        out_specs=jax.tree.map(lambda _: vmem, out_shapes),
        scratch_shapes=scratch,
        cost_estimate=pl.CostEstimate(flops=flops, bytes_accessed=4 << 20, transcendentals=0),
        compiler_params=pltpu.CompilerParams(vmem_limit_bytes=20 << 20),
    )(*operands)


def ring(first, chips):
    steps = chips // 2
    nearest = []
    for place in range(chips):
        here = ring_chip(place, chips)
        nearest.append((2 * here, 2 * ring_chip((place + 1) % chips, chips)))
        nearest.append((2 * here + 1, 2 * ring_chip((place - 1) % chips, chips) + 1))
    swap = [(i, i ^ 1) for i in range(2 * chips)]
    moving = first
    pieces = [first]
    for step in range(1, steps + 1):
        moving = lax.ppermute(moving if step < steps else moving[0], "col", nearest)
        pieces += [moving, lax.ppermute(moving, "col", swap)]
    return pieces


def streams(chips):
    core = lax.axis_index("col") % 2
    here = ring_place(lax.axis_index("col") // 2, chips)
    found = [(lax.axis_index("col") // 2, core)]
    for step in range(1, chips // 2 + 1):
        turn = step * (1 - 2 * core)
        found.append((ring_chip((here - turn + chips) % chips, chips), core))
        found.append((ring_chip((here + turn + chips) % chips, chips), 1 - core))
    return found


def assemble(piece_refs, high_ref, low_ref, whole_ref, chips):
    depth = piece_refs[0].shape[2]

    def put(row, value):
        rows = pl.ds(pl.multiple_of(row, value.shape[1]), value.shape[1])
        if depth % 16 == 0:
            high_ref[:, rows, :], low_ref[:, rows, :] = split(value)
        else:
            whole_ref[:, rows, :] = value

    for at, (chip, core) in enumerate(streams(chips)):
        ref = piece_refs[at]
        if depth % 16 == 0:
            if at < chips - 1:
                for half in range(2):
                    put((2 * chip + half) * depth, ref[jnp.where(core == 0, half, 1 - half)])
            else:
                put((2 * chip + core) * depth, ref[...])
            continue
        if at == chips:
            continue
        pair = [ref[0], ref[1]] if at < chips - 1 else [ref[...], piece_refs[at + 1][...]]
        low, high = jnp.where(core == 0, pair[0], pair[1]), jnp.where(core == 0, pair[1], pair[0])
        put(2 * chip * depth, jnp.concatenate([low, high], axis=1))
    if depth % 16 != 0:
        high_ref[...], low_ref[...] = split(whole_ref[...])


def split_scratch(count, nb, depth):
    whole = (count, nb, nb) if depth % 16 != 0 else (1, 8, nb)
    return [
        pltpu.VMEM((count, nb, nb), jnp.bfloat16),
        pltpu.VMEM((count, nb, nb), jnp.bfloat16),
        pltpu.VMEM(whole, jnp.float32),
    ]


class Plan:
    def __init__(self, group_count, chips, panels, nb, rows):
        self.group_count, self.chips, self.panels, self.nb = group_count, chips, panels, nb
        self.held = -(-panels // group_count)
        self.sure = panels // group_count
        self.wide = rows // nb - self.sure
        self.tri = [(rank, panel) for rank in range(1, panels) for panel in range(rank)]
        self.deep = max(
            min(rank, panels - 1) for rank in range((self.held - 1) * group_count, self.held * group_count)
        )
        sizes = [
            max(panels + self.wide * s, len(self.tri) + self.wide * (panels - s)) for s in range(panels + 1)
        ]
        self.early = panels - sizes[::-1].index(min(sizes))
        self.first = panels + self.wide * self.early
        self.second = len(self.tri) + self.wide * (panels - self.early)

    def chosen(self, owner, sources):
        me = lax.axis_index("row")
        value = sources[0]
        for shift in range(1, self.group_count):
            value = jnp.where((me + shift) % self.group_count == owner, sources[shift], value)
        return value

    def panel_rows(self, rank, right_ref, received):
        local, owner = divmod(rank, self.group_count)
        rows = slice(local * self.nb, (local + 1) * self.nb)
        return self.chosen(owner, [right_ref[rows]] + [r[rows] for r in received])


def first_kernel(plan, inv_ref, inv_other, factor_ref, factor_other, out_ref):
    for side, (inv, factor) in enumerate(((inv_ref, factor_ref), (inv_other, factor_other))):
        out_ref[side, : plan.panels] = inv[...]
        for panel in range(plan.early):
            for block in range(plan.wide):
                at = (plan.sure + block) * plan.nb
                to = plan.panels + panel * plan.wide + block
                out_ref[side, to] = factor[panel, :, at : at + plan.nb]


def tri_kernel(plan, *refs):
    *sources, out_ref = refs
    for at, (rank, panel) in enumerate(plan.tri):
        local, owner = divmod(rank, plan.group_count)
        part = slice(local * plan.nb, (local + 1) * plan.nb)
        out_ref[at] = plan.chosen(owner, [source[panel, :, part] for source in sources])


def second_kernel(plan, tri_ref, tri_other, factor_ref, factor_other, out_ref):
    for side, (tri, factor) in enumerate(((tri_ref, factor_ref), (tri_other, factor_other))):
        out_ref[side, : len(plan.tri)] = tri[...]
        for panel in range(plan.early, plan.panels):
            for block in range(plan.wide):
                at = (plan.sure + block) * plan.nb
                to = len(plan.tri) + (panel - plan.early) * plan.wide + block
                out_ref[side, to] = factor[panel, :, at : at + plan.nb]


def below(plan, panel, block, mats, start):
    at = start + panel * plan.wide + block
    return mats[0][at], mats[1][at]


def prep_kernel(plan, *refs):
    pieces, right_ref = refs[: plan.chips + 1], refs[plan.chips + 1]
    received = refs[plan.chips + 2 : -5]
    high_ref, low_ref, x_ref, total_ref, whole_ref = refs[-5:]
    assemble(pieces, high_ref, low_ref, whole_ref, plan.chips)
    answer = dot3(
        (high_ref[0], low_ref[0]), split(plan.panel_rows(0, right_ref, received)), PLAIN
    )
    x_ref[...] = answer
    solved = split(answer)
    for block in range(plan.wide):
        rows = slice(block * plan.nb, (block + 1) * plan.nb)
        total = right_ref[plan.sure * plan.nb + block * plan.nb : plan.sure * plan.nb + (block + 1) * plan.nb]
        total_ref[rows] = total - dot3(below(plan, 0, block, (high_ref, low_ref), plan.panels), solved, ROWS)


def final_kernel(plan, *refs):
    pieces = refs[: plan.chips + 1]
    first_high, first_low, x_first, total_ref, right_ref = refs[plan.chips + 1 : plan.chips + 6]
    received = refs[plan.chips + 6 : -5]
    out_ref, x_ref, high_ref, low_ref, whole_ref = refs[-5:]
    panels, nb, wide = plan.panels, plan.nb, plan.wide
    assemble(pieces, high_ref, low_ref, whole_ref, plan.chips)
    x_ref[0] = x_first[...]
    solved = [split(x_first[...])]
    for panel in range(1, panels):
        current = plan.panel_rows(panel, right_ref, received)
        for before in range(panel):
            tri = plan.tri.index((panel, before))
            current = current - dot3((high_ref[tri], low_ref[tri]), solved[before], ROWS)
        answer = dot3((first_high[panel], first_low[panel]), split(current), PLAIN)
        x_ref[panel] = answer
        solved.append(split(answer))
    for block in range(wide):
        total = total_ref[block * nb : (block + 1) * nb]
        for panel in range(1, panels):
            if panel < plan.early:
                mat = below(plan, panel, block, (first_high, first_low), panels)
            else:
                mat = below(plan, panel - plan.early, block, (high_ref, low_ref), len(plan.tri))
            total = total - dot3(mat, solved[panel], ROWS)
        out_ref[(plan.sure + block) * nb : (plan.sure + block + 1) * nb] = total
    for local in range(plan.held):
        rank = local * plan.group_count + lax.axis_index("row")

        @pl.when(rank < panels)
        def _(rank=rank, local=local):
            out_ref[local * nb : (local + 1) * nb] = x_ref[rank]


def per_device(right_side, factor_panels, inverses):
    group_count = lax.axis_size("row")
    chips = lax.axis_size("col") // 2
    panels, depth, rows = factor_panels.shape
    nb = inverses.shape[2]
    columns = right_side.shape[1]
    plan = Plan(group_count, chips, panels, nb, rows)
    swap = [(i, i ^ 1) for i in range(2 * chips)]
    shifts = [
        [((g + shift) % group_count, g) for g in range(group_count)] for shift in range(1, group_count)
    ]
    f32, bf16 = jnp.float32, jnp.bfloat16
    shape = jax.ShapeDtypeStruct
    bound = functools.partial

    inverses_other = lax.ppermute(inverses, "col", swap)
    factor_other = lax.ppermute(factor_panels, "col", swap)
    own = factor_panels[: plan.deep, :, : plan.held * nb]
    tri = [own] + [lax.ppermute(own, "row", pairs) for pairs in shifts]
    above = right_side[: plan.held * nb]
    received = [lax.ppermute(above, "row", pairs) for pairs in shifts]

    first = kernel_call(
        bound(first_kernel, plan),
        shape((2, plan.first, depth, nb), f32),
        [],
        (inverses, inverses_other, factor_panels, factor_other),
    )
    half = kernel_call(bound(tri_kernel, plan), shape((len(plan.tri), depth, nb), f32), [], tri)
    half_other = lax.ppermute(half, "col", swap)
    second = kernel_call(
        bound(second_kernel, plan),
        shape((2, plan.second, depth, nb), f32),
        [],
        (half, half_other, factor_panels, factor_other),
    )
    first_pieces = ring(first, chips)
    second_pieces = ring(second, chips)

    high, low, x_first, total = kernel_call(
        bound(prep_kernel, plan),
        [
            shape((plan.first, nb, nb), bf16),
            shape((plan.first, nb, nb), bf16),
            shape((nb, columns), f32),
            shape((plan.wide * nb, columns), f32),
        ],
        split_scratch(plan.first, nb, depth)[2:],
        (*first_pieces, right_side, *received),
        flops=6 * 3 * nb * nb * columns,
    )
    return kernel_call(
        bound(final_kernel, plan),
        shape(right_side.shape, f32),
        [pltpu.VMEM((panels, nb, columns), f32)] + split_scratch(plan.second, nb, depth),
        (*second_pieces, high, low, x_first, total, right_side, *received),
        flops=6 * 15 * nb * nb * columns,
    )


def solution(mesh):
    in_specs = (P("row", "col"), P(None, "col", "row"), P(None, "col", None))
    out_specs = P("row", "col")

    return jax.shard_map(per_device, mesh=mesh, in_specs=in_specs, out_specs=out_specs, check_vma=False)
```

```python
import functools

import jax
import jax.numpy as jnp
from jax import lax
from jax.experimental import pallas as pl
from jax.experimental.pallas import tpu as pltpu
from jax.sharding import PartitionSpec as P

CHUNKS = 2
ROWS = ((0,), (0,))
PLAIN = ((1,), (0,))


def ring_place(chip, chips):
    return jnp.where(chip % 2 == 0, chip // 2, chips - 1 - chip // 2)


def ring_chip(place, chips):
    up = 2 * place
    down = 2 * (chips - 1 - place) + 1
    if isinstance(place, int):
        return up if place < chips // 2 else down
    return jnp.where(place < chips // 2, up, down)


def split(value):
    high = value.astype(jnp.bfloat16)
    low = (value - high.astype(jnp.float32)).astype(jnp.bfloat16)
    return high, low


def dot3(left, right, dims):
    mult = functools.partial(
        lax.dot_general, dimension_numbers=(dims, ((), ())), preferred_element_type=jnp.float32
    )
    return mult(left[0], right[0]) + (mult(left[0], right[1]) + mult(left[1], right[0]))


def kernel_call(body, out_shapes, scratch, operands, flops=0, in_hbm=0, out_hbm=0, aliases={}):
    vmem, hbm = pl.BlockSpec(memory_space=pltpu.VMEM), pl.BlockSpec(memory_space=pltpu.HBM)
    return pl.pallas_call(
        body,
        out_shape=out_shapes,
        in_specs=[hbm] * in_hbm + [vmem] * (len(operands) - in_hbm),
        out_specs=jax.tree.map(lambda _: vmem, out_shapes)
        if not out_hbm
        else [hbm] * out_hbm + [vmem] * (len(out_shapes) - out_hbm),
        input_output_aliases=aliases,
        scratch_shapes=scratch,
        cost_estimate=pl.CostEstimate(flops=flops, bytes_accessed=4 << 20, transcendentals=0),
        compiler_params=pltpu.CompilerParams(vmem_limit_bytes=20 << 20),
    )(*operands)


def ring(first, chips):
    steps = chips // 2
    nearest = []
    for place in range(chips):
        here = ring_chip(place, chips)
        nearest.append((2 * here, 2 * ring_chip((place + 1) % chips, chips)))
        nearest.append((2 * here + 1, 2 * ring_chip((place - 1) % chips, chips) + 1))
    swap = [(i, i ^ 1) for i in range(2 * chips)]
    moving = first
    pieces = [first]
    for step in range(1, steps + 1):
        moving = lax.ppermute(moving if step < steps else moving[0], "col", nearest)
        pieces += [moving, lax.ppermute(moving, "col", swap)]
    return pieces


def streams(chips):
    core = lax.axis_index("col") % 2
    here = ring_place(lax.axis_index("col") // 2, chips)
    found = [(lax.axis_index("col") // 2, core)]
    for step in range(1, chips // 2 + 1):
        turn = step * (1 - 2 * core)
        found.append((ring_chip((here - turn + chips) % chips, chips), core))
        found.append((ring_chip((here + turn + chips) % chips, chips), 1 - core))
    return found


def assemble(piece_refs, high_ref, low_ref, whole_ref, chips, chosen=slice(None)):
    depth = piece_refs[0].shape[-2]

    def put(row, value):
        rows = pl.ds(pl.multiple_of(row, value.shape[1]), value.shape[1])
        if depth % 16 == 0:
            high_ref[:, rows, :], low_ref[:, rows, :] = split(value)
        else:
            whole_ref[:, rows, :] = value

    table = list(enumerate(streams(chips)))[chosen]
    for ref, (at, (chip, core)) in zip(piece_refs, table):
        if depth % 16 == 0:
            if at < chips - 1:
                for half in range(2):
                    put((2 * chip + half) * depth, ref[jnp.where(core == 0, half, 1 - half)])
            else:
                put((2 * chip + core) * depth, ref[...])
            continue
        if at == chips:
            continue
        pair = [ref[0], ref[1]] if at < chips - 1 else [ref[...], piece_refs[-1][...]]
        low, high = jnp.where(core == 0, pair[0], pair[1]), jnp.where(core == 0, pair[1], pair[0])
        put(2 * chip * depth, jnp.concatenate([low, high], axis=1))
    if depth % 16 != 0:
        high_ref[...], low_ref[...] = split(whole_ref[...])


def whole_scratch(count, nb, depth):
    return pltpu.VMEM((count, nb, nb) if depth % 16 != 0 else (1, 8, nb), jnp.float32)


class Plan:
    def __init__(self, group_count, chips, panels, nb, rows):
        self.group_count, self.chips, self.panels, self.nb = group_count, chips, panels, nb
        self.held = -(-panels // group_count)
        self.sure = panels // group_count
        self.wide = rows // nb - self.sure
        self.tri = [(rank, panel) for rank in range(1, panels) for panel in range(rank)]
        self.deep = max(
            min(rank, panels - 1) for rank in range((self.held - 1) * group_count, self.held * group_count)
        )
        low = [(panel, block) for panel in range(panels) for block in range(self.wide)]
        total = panels + len(self.tri) + len(low)
        inv = [("inv", panel) for panel in range(panels)]
        tri = [("tri", at) for at in range(len(self.tri))]
        low = [("low", *pair) for pair in low]
        last = max(total // CHUNKS, len(tri))
        rest = inv + low[: total - panels - last]
        size = -(-len(rest) // (CHUNKS - 1))
        self.chunks = [rest[at : at + size] for at in range(0, len(rest), size)]
        self.chunks.append(tri + low[total - panels - last :])
        self.where = {b: (c, at) for c, chunk in enumerate(self.chunks) for at, b in enumerate(chunk)}

    def mat(self, mats, *block):
        chunk, at = self.where[block]
        high, low = mats[chunk]
        return high[at], low[at]

    def chosen(self, owner, sources):
        me = lax.axis_index("row")
        value = sources[0]
        for shift in range(1, self.group_count):
            value = jnp.where((me + shift) % self.group_count == owner, sources[shift], value)
        return value

    def panel_rows(self, rank, right_ref, received):
        local, owner = divmod(rank, self.group_count)
        rows = slice(local * self.nb, (local + 1) * self.nb)
        return self.chosen(owner, [right_ref[rows]] + [r[rows] for r in received])


def load_kernel(factor_hbm, inv_hbm, factor_ref, inv_ref, own_ref, sems):
    deep, _, part = own_ref.shape
    copies = [
        pltpu.make_async_copy(factor_hbm.at[:deep, :, :part], own_ref, sems.at[0]),
        pltpu.make_async_copy(factor_hbm, factor_ref, sems.at[1]),
        pltpu.make_async_copy(inv_hbm, inv_ref, sems.at[2]),
    ]
    for copy in copies:
        copy.start()
    for copy in copies:
        copy.wait()


def pack_kernel(plan, chunk, *refs):
    out_ref = refs[-1]
    for side in range(2):
        head, factor = refs[2 * side : 2 * side + 2]
        for to, (kind, *which) in enumerate(plan.chunks[chunk]):
            if kind == "low":
                panel, block = which
                at = (plan.sure + block) * plan.nb
                out_ref[side, to] = factor[panel, :, at : at + plan.nb]
            else:
                out_ref[side, to] = head[which[0]]


def tri_kernel(plan, *refs):
    *sources, out_ref = refs
    for at, (rank, panel) in enumerate(plan.tri):
        local, owner = divmod(rank, plan.group_count)
        part = slice(local * plan.nb, (local + 1) * plan.nb)
        out_ref[at] = plan.chosen(owner, [source[panel, :, part] for source in sources])


def prep_kernel(plan, *refs):
    count, early = plan.chips + 1, len(plan.chunks) - 1
    pieces = [refs[c * count : (c + 1) * count] for c in range(early)]
    right_ref = refs[early * count]
    outs = refs[-3 * early - 2 :]
    received = refs[early * count + 1 : -3 * early - 2]
    mats = [outs[2 * c : 2 * c + 2] for c in range(early)]
    x_ref, total_ref = outs[2 * early : 2 * early + 2]
    for c in range(early):
        assemble(pieces[c], *mats[c], outs[2 * early + 2 + c], plan.chips)
    nb = plan.nb
    answer = dot3(plan.mat(mats, "inv", 0), split(plan.panel_rows(0, right_ref, received)), PLAIN)
    x_ref[...] = answer
    solved = split(answer)
    for block in range(plan.wide):
        at = (plan.sure + block) * nb
        total = right_ref[at : at + nb] - dot3(plan.mat(mats, "low", 0, block), solved, ROWS)
        total_ref[block * nb : (block + 1) * nb] = total


def place_kernel(plan, *refs):
    high_ref, low_ref, whole_ref = refs[-3:]
    assemble(refs[:-3], high_ref, low_ref, whole_ref, plan.chips, slice(0, plan.chips - 1))


def final_kernel(plan, late, *refs):
    early = len(plan.chunks) - 1
    pieces, at = refs[:late], late
    mats = [refs[at + 2 * c : at + 2 * c + 2] for c in range(early)]
    at += 2 * early
    x_first, total_ref, right_ref = refs[at + 2 : at + 5]
    received = refs[at + 5 : -7]
    out_hbm, high_ref, low_ref, x_ref, low_rows, whole_ref, sems = refs[-7:]
    panels, nb, wide = plan.panels, plan.nb, plan.wide
    me = lax.axis_index("row")
    fresh = slice(plan.chips - 1, None) if late == 2 else slice(None)
    assemble(pieces, high_ref, low_ref, whole_ref, plan.chips, fresh)
    mats.append((high_ref, low_ref))

    def copy_out(rank, local):
        rows = pl.ds(local * nb, nb)
        return pltpu.make_async_copy(x_ref.at[rank], out_hbm.at[rows], sems.at[local])

    x_ref[0] = x_first[...]
    solved = [split(x_first[...])]
    currents = [plan.panel_rows(panel, right_ref, received) for panel in range(panels)]
    totals = [total_ref[block * nb : (block + 1) * nb] for block in range(wide)]
    for panel in range(1, panels):
        for after in range(panel, panels):
            mat = plan.mat(mats, "tri", plan.tri.index((after, panel - 1)))
            currents[after] = currents[after] - dot3(mat, solved[panel - 1], ROWS)
        answer = dot3(plan.mat(mats, "inv", panel), split(currents[panel]), PLAIN)
        x_ref[panel] = answer
        if panel > 1:
            for block in range(wide):
                mat = plan.mat(mats, "low", panel - 1, block)
                totals[block] = totals[block] - dot3(mat, solved[panel - 1], ROWS)
        solved.append(split(answer))
    for local in range(plan.held):
        rank = local * plan.group_count + me

        @pl.when(rank < panels)
        def _(rank=rank, local=local):
            copy_out(rank, local).start()

    outs = []
    for block in range(wide):
        mat = plan.mat(mats, "low", panels - 1, block)
        low_rows[block] = totals[block] - dot3(mat, solved[panels - 1], ROWS)
        local = plan.sure + block
        out = pltpu.make_async_copy(
            low_rows.at[block], out_hbm.at[pl.ds(local * nb, nb)], sems.at[local]
        )
        if local < plan.held:
            below = local * plan.group_count + me >= panels
            pl.when(below)(out.start)
            pl.when(below)(out.wait)
        else:
            out.start()
            outs.append(out)
    for local in range(plan.held):
        rank = local * plan.group_count + me

        @pl.when(rank < panels)
        def _(rank=rank, local=local):
            copy_out(rank, local).wait()

    for out in outs:
        out.wait()


def per_device(right_side, factor_panels, inverses):
    group_count = lax.axis_size("row")
    chips = lax.axis_size("col") // 2
    panels, depth, rows = factor_panels.shape
    nb = inverses.shape[2]
    columns = right_side.shape[1]
    plan = Plan(group_count, chips, panels, nb, rows)
    swap = [(i, i ^ 1) for i in range(2 * chips)]
    shifts = [
        [((g + shift) % group_count, g) for g in range(group_count)] for shift in range(1, group_count)
    ]
    f32, bf16 = jnp.float32, jnp.bfloat16
    shape = jax.ShapeDtypeStruct
    bound = functools.partial

    factor, inv, own = kernel_call(
        load_kernel,
        [
            shape(factor_panels.shape, f32),
            shape(inverses.shape, f32),
            shape((plan.deep, depth, plan.held * nb), f32),
        ],
        [pltpu.SemaphoreType.DMA((3,))],
        (factor_panels, inverses),
        in_hbm=2,
    )
    inv_other = lax.ppermute(inv, "col", swap)
    factor_other = lax.ppermute(factor, "col", swap)
    tri = [own] + [lax.ppermute(own, "row", pairs) for pairs in shifts]
    above = right_side[: plan.held * nb]
    received = [lax.ppermute(above, "row", pairs) for pairs in shifts]
    half = kernel_call(bound(tri_kernel, plan), shape((len(plan.tri), depth, nb), f32), [], tri)
    half_other = lax.ppermute(half, "col", swap)

    pieces = []
    last = len(plan.chunks) - 1
    for chunk in range(last + 1):
        heads = (half, half_other) if chunk == last else (inv, inv_other)
        packed = kernel_call(
            bound(pack_kernel, plan, chunk),
            shape((2, len(plan.chunks[chunk]), depth, nb), f32),
            [],
            (heads[0], factor, heads[1], factor_other),
        )
        pieces.append(ring(packed, chips))

    split_shapes = [[shape((len(chunk), nb, nb), bf16)] * 2 for chunk in plan.chunks]
    *mats, x_first, total = kernel_call(
        bound(prep_kernel, plan),
        [s for pair in split_shapes[:-1] for s in pair]
        + [shape((nb, columns), f32), shape((plan.wide * nb, columns), f32)],
        [whole_scratch(len(chunk), nb, depth) for chunk in plan.chunks[:-1]],
        (*(piece for chunk in pieces[:-1] for piece in chunk), right_side, *received),
        flops=6 * 3 * nb * nb * columns,
    )
    whole = whole_scratch(len(plan.chunks[-1]), nb, depth)
    aligned = depth % 16 == 0
    if aligned:
        placed = kernel_call(
            bound(place_kernel, plan), split_shapes[-1], [whole], pieces[-1][: chips - 1]
        )
        late = pieces[-1][chips - 1 :]
    else:
        placed = [jnp.zeros(s.shape, s.dtype) for s in split_shapes[-1]]
        late = pieces[-1]
    at = len(late) + len(mats)
    out, _, _ = kernel_call(
        bound(final_kernel, plan, len(late)),
        [shape(right_side.shape, f32), *split_shapes[-1]],
        [
            pltpu.VMEM((panels, nb, columns), f32),
            pltpu.VMEM((plan.wide, nb, columns), f32),
            whole,
            pltpu.SemaphoreType.DMA((rows // nb,)),
        ],
        (*late, *mats, *placed, x_first, total, right_side, *received),
        flops=6 * 15 * nb * nb * columns,
        out_hbm=1,
        aliases={at: 1, at + 1: 2},
    )
    return out


def solution(mesh):
    in_specs = (P("row", "col"), P(None, "col", "row"), P(None, "col", None))
    out_specs = P("row", "col")

    return jax.shard_map(per_device, mesh=mesh, in_specs=in_specs, out_specs=out_specs, check_vma=False)
```

```python
import functools

import jax
import jax.numpy as jnp
from jax import lax
from jax.experimental import pallas as pl
from jax.experimental.pallas import tpu as pltpu
from jax.sharding import PartitionSpec as P

ROWS = ((0,), (0,))
PLAIN = ((1,), (0,))


def ring_place(chip, chips):
    return jnp.where(chip % 2 == 0, chip // 2, chips - 1 - chip // 2)


def ring_chip(place, chips):
    up = 2 * place
    down = 2 * (chips - 1 - place) + 1
    if isinstance(place, int):
        return up if place < chips // 2 else down
    return jnp.where(place < chips // 2, up, down)


def split(value):
    high = value.astype(jnp.bfloat16)
    low = (value - high.astype(jnp.float32)).astype(jnp.bfloat16)
    return high, low


def dot3(left, right, dims):
    mult = functools.partial(
        lax.dot_general, dimension_numbers=(dims, ((), ())), preferred_element_type=jnp.float32
    )
    return mult(left[0], right[0]) + (mult(left[0], right[1]) + mult(left[1], right[0]))


def kernel_call(body, out_shapes, scratch, operands, flops=0, in_hbm=0, out_hbm=0, aliases={}):
    near, hbm = pl.BlockSpec(memory_space=pltpu.VMEM), pl.BlockSpec(memory_space=pltpu.HBM)
    return pl.pallas_call(
        body,
        out_shape=out_shapes,
        in_specs=[hbm] * in_hbm + [near] * (len(operands) - in_hbm),
        out_specs=jax.tree.map(lambda _: near, out_shapes)
        if not out_hbm
        else [hbm] * out_hbm + [near] * (len(out_shapes) - out_hbm),
        input_output_aliases=aliases,
        scratch_shapes=scratch,
        cost_estimate=pl.CostEstimate(flops=flops, bytes_accessed=4 << 20, transcendentals=0),
        compiler_params=pltpu.CompilerParams(vmem_limit_bytes=20 << 20),
    )(*operands)


def ring(first, chips):
    steps = chips // 2
    nearest = []
    for place in range(chips):
        here = ring_chip(place, chips)
        nearest.append((2 * here, 2 * ring_chip((place + 1) % chips, chips)))
        nearest.append((2 * here + 1, 2 * ring_chip((place - 1) % chips, chips) + 1))
    swap = [(i, i ^ 1) for i in range(2 * chips)]
    moving = first
    pieces = [first]
    for step in range(1, steps + 1):
        moving = lax.ppermute(moving if step < steps else moving[0], "col", nearest)
        pieces += [moving, lax.ppermute(moving, "col", swap)]
    return pieces


def streams(chips):
    core = lax.axis_index("col") % 2
    here = ring_place(lax.axis_index("col") // 2, chips)
    found = [(lax.axis_index("col") // 2, core)]
    for step in range(1, chips // 2 + 1):
        turn = step * (1 - 2 * core)
        found.append((ring_chip((here - turn + chips) % chips, chips), core))
        found.append((ring_chip((here + turn + chips) % chips, chips), 1 - core))
    return found


def assemble(piece_refs, high_ref, low_ref, whole_ref, chips, chosen=slice(None)):
    depth = piece_refs[0].shape[-2]

    def put(row, value):
        rows = pl.ds(pl.multiple_of(row, value.shape[1]), value.shape[1])
        if depth % 16 == 0:
            high_ref[:, rows, :], low_ref[:, rows, :] = split(value)
        else:
            whole_ref[:, rows, :] = value

    table = list(enumerate(streams(chips)))[chosen]
    for ref, (at, (chip, core)) in zip(piece_refs, table):
        if depth % 16 == 0:
            if at < chips - 1:
                for half in range(2):
                    put((2 * chip + half) * depth, ref[jnp.where(core == 0, half, 1 - half)])
            else:
                put((2 * chip + core) * depth, ref[...])
            continue
        if at == chips:
            continue
        pair = [ref[0], ref[1]] if at < chips - 1 else [ref[...], piece_refs[-1][...]]
        low, high = jnp.where(core == 0, pair[0], pair[1]), jnp.where(core == 0, pair[1], pair[0])
        put(2 * chip * depth, jnp.concatenate([low, high], axis=1))
    if depth % 16 != 0:
        high_ref[...], low_ref[...] = split(whole_ref[...])


def whole_scratch(count, nb, depth):
    return pltpu.VMEM((count, nb, nb) if depth % 16 != 0 else (1, 8, nb), jnp.float32)


class Plan:
    def __init__(self, group_count, chips, panels, nb, rows):
        self.group_count, self.chips, self.panels, self.nb = group_count, chips, panels, nb
        self.held = -(-panels // group_count)
        self.sure = panels // group_count
        self.wide = rows // nb - self.sure
        self.tri = [(rank, panel) for rank in range(1, panels) for panel in range(rank)]
        self.deep = max(
            min(rank, panels - 1) for rank in range((self.held - 1) * group_count, self.held * group_count)
        )
        low = [("low", panel, block) for panel in range(panels) for block in range(self.wide)]
        self.chunks = [
            [("inv", panel) for panel in range(panels)] + low[: self.wide],
            low[self.wide :],
            [("tri", at) for at in range(len(self.tri))],
        ]
        self.where = {b: (c, at) for c, chunk in enumerate(self.chunks) for at, b in enumerate(chunk)}

    def mat(self, mats, *block):
        chunk, at = self.where[block]
        high, low = mats[chunk]
        return high[at], low[at]

    def chosen(self, owner, sources):
        me = lax.axis_index("row")
        value = sources[0]
        for shift in range(1, self.group_count):
            value = jnp.where((me + shift) % self.group_count == owner, sources[shift], value)
        return value

    def panel_rows(self, rank, right_ref, received):
        local, owner = divmod(rank, self.group_count)
        rows = slice(local * self.nb, (local + 1) * self.nb)
        return self.chosen(owner, [right_ref[rows]] + [r[rows] for r in received])


def load_kernel(factor_hbm, inv_hbm, factor_ref, inv_ref, own_ref, sems):
    deep, _, part = own_ref.shape
    copies = [
        pltpu.make_async_copy(factor_hbm.at[:deep, :, :part], own_ref, sems.at[0]),
        pltpu.make_async_copy(factor_hbm, factor_ref, sems.at[1]),
        pltpu.make_async_copy(inv_hbm, inv_ref, sems.at[2]),
    ]
    for copy in copies:
        copy.start()
    for copy in copies:
        copy.wait()


def pack_kernel(plan, chunk, *refs):
    out_ref = refs[-1]
    for side in range(2):
        head, factor = refs[2 * side : 2 * side + 2]
        for to, (kind, *which) in enumerate(plan.chunks[chunk]):
            if kind == "low":
                panel, block = which
                at = (plan.sure + block) * plan.nb
                out_ref[side, to] = factor[panel, :, at : at + plan.nb]
            else:
                out_ref[side, to] = head[which[0]]


def tri_kernel(plan, *refs):
    *sources, out_ref = refs
    for at, (rank, panel) in enumerate(plan.tri):
        local, owner = divmod(rank, plan.group_count)
        part = slice(local * plan.nb, (local + 1) * plan.nb)
        out_ref[at] = plan.chosen(owner, [source[panel, :, part] for source in sources])


def prep_kernel(plan, *refs):
    pieces, right_ref = refs[: plan.chips + 1], refs[plan.chips + 1]
    received = refs[plan.chips + 2 : -5]
    high_ref, low_ref, x_ref, total_ref, whole_ref = refs[-5:]
    assemble(pieces, high_ref, low_ref, whole_ref, plan.chips)
    mats, nb = [(high_ref, low_ref)], plan.nb
    answer = dot3(plan.mat(mats, "inv", 0), split(plan.panel_rows(0, right_ref, received)), PLAIN)
    x_ref[...] = answer
    solved = split(answer)
    for block in range(plan.wide):
        at = (plan.sure + block) * nb
        total = right_ref[at : at + nb] - dot3(plan.mat(mats, "low", 0, block), solved, ROWS)
        total_ref[block * nb : (block + 1) * nb] = total


def place_kernel(plan, *refs):
    high_ref, low_ref, whole_ref = refs[-3:]
    assemble(refs[:-3], high_ref, low_ref, whole_ref, plan.chips, slice(0, plan.chips - 1))


def late_pieces(plan, late):
    return slice(plan.chips - 1, None) if late == 2 else slice(None)


def solve_kernel(plan, late, *refs):
    pieces = refs[:late]
    inv_high, inv_low, x_first, right_ref = refs[late + 2 : late + 6]
    received = refs[late + 6 : -6]
    x_ref, x_high, x_low, high_ref, low_ref, whole_ref = refs[-6:]
    assemble(pieces, high_ref, low_ref, whole_ref, plan.chips, late_pieces(plan, late))
    mats = [(inv_high, inv_low), None, (high_ref, low_ref)]
    panels = plan.panels
    currents = [plan.panel_rows(panel, right_ref, received) for panel in range(panels)]
    answer = x_first[...]
    for panel in range(panels):
        if panel > 0:
            answer = dot3(plan.mat(mats, "inv", panel), split(currents[panel]), PLAIN)
        x_ref[panel] = answer
        solved = split(answer)
        x_high[panel], x_low[panel] = solved
        for after in range(panel + 1, panels):
            mat = plan.mat(mats, "tri", plan.tri.index((after, panel)))
            currents[after] = currents[after] - dot3(mat, solved, ROWS)


def final_kernel(plan, late, *refs):
    pieces = refs[:late]
    x_ref, x_high, x_low, total_ref = refs[late + 2 : late + 6]
    out_hbm, high_ref, low_ref, low_rows, whole_ref, sems = refs[-6:]
    panels, nb = plan.panels, plan.nb
    me = lax.axis_index("row")

    def panel_out(rank, local):
        rows = pl.ds(local * nb, nb)
        return pltpu.make_async_copy(x_ref.at[rank], out_hbm.at[rows], sems.at[local])

    def for_panels(act):
        for local in range(plan.held):
            rank = local * plan.group_count + me

            @pl.when(rank < panels)
            def _(rank=rank, local=local):
                act(panel_out(rank, local))

    for_panels(lambda copy: copy.start())
    assemble(pieces, high_ref, low_ref, whole_ref, plan.chips, late_pieces(plan, late))
    mats = [None, (high_ref, low_ref)]
    outs = []
    for block in range(plan.wide):
        total = total_ref[block * nb : (block + 1) * nb]
        for panel in range(1, panels):
            mat = plan.mat(mats, "low", panel, block)
            total = total - dot3(mat, (x_high[panel], x_low[panel]), ROWS)
        low_rows[block] = total
        local = plan.sure + block
        out = pltpu.make_async_copy(
            low_rows.at[block], out_hbm.at[pl.ds(local * nb, nb)], sems.at[local]
        )
        if local < plan.held:
            mine = local * plan.group_count + me >= panels
            pl.when(mine)(out.start)
            pl.when(mine)(out.wait)
        else:
            out.start()
            outs.append(out)
    for_panels(lambda copy: copy.wait())
    for out in outs:
        out.wait()


def per_device(right_side, factor_panels, inverses):
    group_count = lax.axis_size("row")
    chips = lax.axis_size("col") // 2
    panels, depth, rows = factor_panels.shape
    nb = inverses.shape[2]
    columns = right_side.shape[1]
    plan = Plan(group_count, chips, panels, nb, rows)
    swap = [(i, i ^ 1) for i in range(2 * chips)]
    shifts = [
        [((g + shift) % group_count, g) for g in range(group_count)] for shift in range(1, group_count)
    ]
    f32, bf16 = jnp.float32, jnp.bfloat16
    shape = jax.ShapeDtypeStruct
    bound = functools.partial

    factor, inv, own = kernel_call(
        load_kernel,
        [
            shape(factor_panels.shape, f32),
            shape(inverses.shape, f32),
            shape((plan.deep, depth, plan.held * nb), f32),
        ],
        [pltpu.SemaphoreType.DMA((3,))],
        [pltpu.with_memory_space_constraint(a, pltpu.HBM) for a in (factor_panels, inverses)],
        in_hbm=2,
    )
    inv_other = lax.ppermute(inv, "col", swap)
    factor_other = lax.ppermute(factor, "col", swap)
    tri = [own] + [lax.ppermute(own, "row", pairs) for pairs in shifts]
    above = right_side[: plan.held * nb]
    received = [lax.ppermute(above, "row", pairs) for pairs in shifts]
    half = kernel_call(bound(tri_kernel, plan), shape((len(plan.tri), depth, nb), f32), [], tri)
    half_other = lax.ppermute(half, "col", swap)

    pieces = []
    for chunk, blocks in enumerate(plan.chunks):
        heads = (half, half_other) if chunk == len(plan.chunks) - 1 else (inv, inv_other)
        packed = kernel_call(
            bound(pack_kernel, plan, chunk),
            shape((2, len(blocks), depth, nb), f32),
            [],
            (heads[0], factor, heads[1], factor_other),
        )
        pieces.append(ring(packed, chips))

    pairs = [[shape((len(blocks), nb, nb), bf16)] * 2 for blocks in plan.chunks]
    wholes = [whole_scratch(len(blocks), nb, depth) for blocks in plan.chunks]

    def place(chunk):
        if depth % 16 != 0:
            return [jnp.zeros(s.shape, s.dtype) for s in pairs[chunk]], pieces[chunk]
        done = kernel_call(
            bound(place_kernel, plan), pairs[chunk], [wholes[chunk]], pieces[chunk][: chips - 1]
        )
        return done, pieces[chunk][chips - 1 :]

    inv_high, inv_low, x_first, total = kernel_call(
        bound(prep_kernel, plan),
        [*pairs[0], shape((nb, columns), f32), shape((plan.wide * nb, columns), f32)],
        [wholes[0]],
        (*pieces[0], right_side, *received),
        flops=6 * 3 * nb * nb * columns,
    )
    placed, late = place(2)
    answers = [shape((panels, nb, columns), t) for t in (f32, bf16, bf16)]
    x, x_high, x_low, _, _ = kernel_call(
        bound(solve_kernel, plan, len(late)),
        [*answers, *pairs[2]],
        [wholes[2]],
        (*late, *placed, inv_high, inv_low, x_first, right_side, *received),
        flops=6 * 9 * nb * nb * columns,
        aliases={len(late): 3, len(late) + 1: 4},
    )
    placed, late = place(1)
    out, _, _ = kernel_call(
        bound(final_kernel, plan, len(late)),
        [shape(right_side.shape, f32), *pairs[1]],
        [
            pltpu.VMEM((plan.wide, nb, columns), f32),
            wholes[1],
            pltpu.SemaphoreType.DMA((rows // nb,)),
        ],
        (*late, *placed, x, x_high, x_low, total),
        flops=6 * 6 * nb * nb * columns,
        out_hbm=1,
        aliases={len(late): 1, len(late) + 1: 2},
    )
    return out


def solution(mesh):
    in_specs = (P("row", "col"), P(None, "col", "row"), P(None, "col", None))
    out_specs = P("row", "col")

    return jax.shard_map(per_device, mesh=mesh, in_specs=in_specs, out_specs=out_specs, check_vma=False)
```

```python
import functools

import jax
import jax.numpy as jnp
from jax import lax
from jax.experimental import pallas as pl
from jax.experimental.pallas import tpu as pltpu
from jax.sharding import PartitionSpec as P

ROWS = ((0,), (0,))
PLAIN = ((1,), (0,))


def ring_place(chip, chips):
    return jnp.where(chip % 2 == 0, chip // 2, chips - 1 - chip // 2)


def ring_chip(place, chips):
    up = 2 * place
    down = 2 * (chips - 1 - place) + 1
    if isinstance(place, int):
        return up if place < chips // 2 else down
    return jnp.where(place < chips // 2, up, down)


def split(value):
    high = value.astype(jnp.bfloat16)
    low = (value - high.astype(jnp.float32)).astype(jnp.bfloat16)
    return high, low


def dot3(left, right, dims):
    mult = functools.partial(
        lax.dot_general, dimension_numbers=(dims, ((), ())), preferred_element_type=jnp.float32
    )
    return mult(left[0], right[0]) + (mult(left[0], right[1]) + mult(left[1], right[0]))


def kernel_call(body, out_shapes, scratch, operands, flops=0, in_hbm=0, out_hbm=0, aliases={}):
    near, hbm = pl.BlockSpec(memory_space=pltpu.VMEM), pl.BlockSpec(memory_space=pltpu.HBM)
    return pl.pallas_call(
        body,
        out_shape=out_shapes,
        in_specs=[hbm] * in_hbm + [near] * (len(operands) - in_hbm),
        out_specs=jax.tree.map(lambda _: near, out_shapes)
        if not out_hbm
        else [hbm] * out_hbm + [near] * (len(out_shapes) - out_hbm),
        input_output_aliases=aliases,
        scratch_shapes=scratch,
        cost_estimate=pl.CostEstimate(flops=flops, bytes_accessed=4 << 20, transcendentals=0),
        compiler_params=pltpu.CompilerParams(vmem_limit_bytes=20 << 20),
    )(*operands)


def ring(first, chips):
    steps = chips // 2
    nearest = []
    for place in range(chips):
        here = ring_chip(place, chips)
        nearest.append((2 * here, 2 * ring_chip((place + 1) % chips, chips)))
        nearest.append((2 * here + 1, 2 * ring_chip((place - 1) % chips, chips) + 1))
    swap = [(i, i ^ 1) for i in range(2 * chips)]
    moving = first
    pieces = [first]
    for step in range(1, steps + 1):
        moving = lax.ppermute(moving if step < steps else moving[0], "col", nearest)
        pieces += [moving, lax.ppermute(moving, "col", swap)]
    return pieces


def streams(chips):
    core = lax.axis_index("col") % 2
    here = ring_place(lax.axis_index("col") // 2, chips)
    found = [(lax.axis_index("col") // 2, core)]
    for step in range(1, chips // 2 + 1):
        turn = step * (1 - 2 * core)
        found.append((ring_chip((here - turn + chips) % chips, chips), core))
        found.append((ring_chip((here + turn + chips) % chips, chips), 1 - core))
    return found


def assemble(piece_refs, high_ref, low_ref, whole_ref, chips, chosen=slice(None)):
    depth = piece_refs[0].shape[-2]

    def put(row, value):
        rows = pl.ds(pl.multiple_of(row, value.shape[1]), value.shape[1])
        if depth % 16 == 0:
            high_ref[:, rows, :], low_ref[:, rows, :] = split(value)
        else:
            whole_ref[:, rows, :] = value

    table = list(enumerate(streams(chips)))[chosen]
    for ref, (at, (chip, core)) in zip(piece_refs, table):
        if depth % 16 == 0:
            if at < chips - 1:
                for half in range(2):
                    put((2 * chip + half) * depth, ref[jnp.where(core == 0, half, 1 - half)])
            else:
                put((2 * chip + core) * depth, ref[...])
            continue
        if at == chips:
            continue
        pair = [ref[0], ref[1]] if at < chips - 1 else [ref[...], piece_refs[-1][...]]
        low, high = jnp.where(core == 0, pair[0], pair[1]), jnp.where(core == 0, pair[1], pair[0])
        put(2 * chip * depth, jnp.concatenate([low, high], axis=1))
    if depth % 16 != 0:
        high_ref[...], low_ref[...] = split(whole_ref[...])


def whole_scratch(count, nb, depth):
    return pltpu.VMEM((count, nb, nb) if depth % 16 != 0 else (1, 8, nb), jnp.float32)


class Plan:
    def __init__(self, group_count, chips, panels, nb, rows):
        self.group_count, self.chips, self.panels, self.nb = group_count, chips, panels, nb
        self.held = -(-panels // group_count)
        self.sure = panels // group_count
        self.wide = rows // nb - self.sure
        self.tri = [(rank, panel) for rank in range(1, panels) for panel in range(rank)]
        self.deep = max(
            min(rank, panels - 1) for rank in range((self.held - 1) * group_count, self.held * group_count)
        )
        low = [("low", panel, block) for panel in range(panels) for block in range(self.wide)]
        self.chunks = [
            [("inv", panel) for panel in range(panels)] + low[: self.wide],
            low[self.wide :],
            [("tri", at) for at in range(len(self.tri))],
        ]
        self.where = {b: (c, at) for c, chunk in enumerate(self.chunks) for at, b in enumerate(chunk)}

    def mat(self, mats, *block):
        chunk, at = self.where[block]
        high, low = mats[chunk]
        return high[at], low[at]

    def chosen(self, owner, sources):
        me = lax.axis_index("row")
        value = sources[0]
        for shift in range(1, self.group_count):
            value = jnp.where((me + shift) % self.group_count == owner, sources[shift], value)
        return value

    def panel_rows(self, rank, right_ref, received):
        local, owner = divmod(rank, self.group_count)
        rows = slice(local * self.nb, (local + 1) * self.nb)
        return self.chosen(owner, [right_ref[rows]] + [r[rows] for r in received])


def load_kernel(factor_hbm, inv_hbm, factor_ref, inv_ref, own_ref, sems):
    deep, _, part = own_ref.shape
    copies = [
        pltpu.make_async_copy(factor_hbm.at[:deep, :, :part], own_ref, sems.at[0]),
        pltpu.make_async_copy(factor_hbm, factor_ref, sems.at[1]),
        pltpu.make_async_copy(inv_hbm, inv_ref, sems.at[2]),
    ]
    for copy in copies:
        copy.start()
    for copy in copies:
        copy.wait()


def pack_kernel(plan, chunk, *refs):
    out_ref = refs[-1]
    for side in range(2):
        head, factor = refs[2 * side : 2 * side + 2]
        for to, (kind, *which) in enumerate(plan.chunks[chunk]):
            if kind == "low":
                panel, block = which
                at = (plan.sure + block) * plan.nb
                out_ref[side, to] = factor[panel, :, at : at + plan.nb]
            else:
                out_ref[side, to] = head[which[0]]


def tri_kernel(plan, *refs):
    *sources, out_ref = refs
    for at, (rank, panel) in enumerate(plan.tri):
        local, owner = divmod(rank, plan.group_count)
        part = slice(local * plan.nb, (local + 1) * plan.nb)
        out_ref[at] = plan.chosen(owner, [source[panel, :, part] for source in sources])


def prep_kernel(plan, *refs):
    pieces, right_ref = refs[: plan.chips + 1], refs[plan.chips + 1]
    received = refs[plan.chips + 2 : -5]
    high_ref, low_ref, x_ref, total_ref, whole_ref = refs[-5:]
    assemble(pieces, high_ref, low_ref, whole_ref, plan.chips)
    mats, nb = [(high_ref, low_ref)], plan.nb
    answer = dot3(plan.mat(mats, "inv", 0), split(plan.panel_rows(0, right_ref, received)), PLAIN)
    x_ref[...] = answer
    solved = split(answer)
    for block in range(plan.wide):
        at = (plan.sure + block) * nb
        total = right_ref[at : at + nb] - dot3(plan.mat(mats, "low", 0, block), solved, ROWS)
        total_ref[block * nb : (block + 1) * nb] = total


def place_kernel(plan, *refs):
    high_ref, low_ref, whole_ref = refs[-3:]
    assemble(refs[:-3], high_ref, low_ref, whole_ref, plan.chips, slice(0, len(refs) - 3))


def late_pieces(plan, late):
    return slice(plan.chips - 1, None) if late == 2 else slice(None)


def final_kernel(plan, late, *refs):
    pieces, at = refs[:late], late + 2
    mats = [refs[at : at + 2], refs[at + 2 : at + 4]]
    x_first, total_ref, right_ref = refs[at + 4 : at + 7]
    received = refs[at + 7 : -7]
    out_hbm, high_ref, low_ref, x_ref, low_rows, whole_ref, sems = refs[-7:]
    panels, nb = plan.panels, plan.nb
    me = lax.axis_index("row")
    assemble(pieces, high_ref, low_ref, whole_ref, plan.chips, late_pieces(plan, late))
    mats.append((high_ref, low_ref))
    currents = [plan.panel_rows(panel, right_ref, received) for panel in range(panels)]
    totals = [total_ref[block * nb : (block + 1) * nb] for block in range(plan.wide)]

    def panel_out(local):
        rank = local * plan.group_count + me
        rows = pl.ds(local * nb, nb)
        return pltpu.make_async_copy(x_ref.at[rank], out_hbm.at[rows], sems.at[local])

    def rows_out(block):
        local = plan.sure + block
        rows = pl.ds(local * nb, nb)
        return pltpu.make_async_copy(low_rows.at[block], out_hbm.at[rows], sems.at[local])

    def each_out(act):
        for local in range(plan.sure):
            act(panel_out(local))
        for local in range(plan.sure, plan.held):
            pl.when(local * plan.group_count + me < panels)(functools.partial(act, panel_out(local)))

    answer = x_first[...]
    for panel in range(panels):
        if panel > 0:
            answer = dot3(plan.mat(mats, "inv", panel), split(currents[panel]), PLAIN)
        x_ref[panel] = answer
        solved = split(answer)
        for after in range(panel + 1, panels):
            mat = plan.mat(mats, "tri", plan.tri.index((after, panel)))
            currents[after] = currents[after] - dot3(mat, solved, ROWS)
        if panel == panels - 1:
            each_out(lambda copy: copy.start())
        for block in range(plan.wide):
            if panel > 0:
                mat = plan.mat(mats, "low", panel, block)
                totals[block] = totals[block] - dot3(mat, solved, ROWS)
            if panel == panels - 1:
                low_rows[block] = totals[block]
                if plan.sure + block >= plan.held:
                    rows_out(block).start()

    each_out(lambda copy: copy.wait())
    for block in range(plan.wide):
        local = plan.sure + block
        if local < plan.held:
            mine = local * plan.group_count + me >= panels
            pl.when(mine)(rows_out(block).start)
            pl.when(mine)(rows_out(block).wait)
        else:
            rows_out(block).wait()


def per_device(right_side, factor_panels, inverses):
    group_count = lax.axis_size("row")
    chips = lax.axis_size("col") // 2
    panels, depth, rows = factor_panels.shape
    nb = inverses.shape[2]
    columns = right_side.shape[1]
    plan = Plan(group_count, chips, panels, nb, rows)
    swap = [(i, i ^ 1) for i in range(2 * chips)]
    shifts = [
        [((g + shift) % group_count, g) for g in range(group_count)] for shift in range(1, group_count)
    ]
    f32, bf16 = jnp.float32, jnp.bfloat16
    shape = jax.ShapeDtypeStruct
    bound = functools.partial

    factor, inv, own = kernel_call(
        load_kernel,
        [
            shape(factor_panels.shape, f32),
            shape(inverses.shape, f32),
            shape((plan.deep, depth, plan.held * nb), f32),
        ],
        [pltpu.SemaphoreType.DMA((3,))],
        [pltpu.with_memory_space_constraint(a, pltpu.HBM) for a in (factor_panels, inverses)],
        in_hbm=2,
    )
    inv_other = lax.ppermute(inv, "col", swap)
    factor_other = lax.ppermute(factor, "col", swap)
    tri = [own] + [lax.ppermute(own, "row", pairs) for pairs in shifts]
    above = right_side[: plan.held * nb]
    received = [lax.ppermute(above, "row", pairs) for pairs in shifts]
    half = kernel_call(bound(tri_kernel, plan), shape((len(plan.tri), depth, nb), f32), [], tri)
    half_other = lax.ppermute(half, "col", swap)

    pieces = []
    for chunk, blocks in enumerate(plan.chunks):
        heads = (half, half_other) if chunk == len(plan.chunks) - 1 else (inv, inv_other)
        packed = kernel_call(
            bound(pack_kernel, plan, chunk),
            shape((2, len(blocks), depth, nb), f32),
            [],
            (heads[0], factor, heads[1], factor_other),
        )
        pieces.append(ring(packed, chips))

    pairs = [[shape((len(blocks), nb, nb), bf16)] * 2 for blocks in plan.chunks]
    wholes = [whole_scratch(len(blocks), nb, depth) for blocks in plan.chunks]

    def place(chunk, count):
        return kernel_call(
            bound(place_kernel, plan), pairs[chunk], [wholes[chunk]], pieces[chunk][:count]
        )

    inv_high, inv_low, x_first, total = kernel_call(
        bound(prep_kernel, plan),
        [*pairs[0], shape((nb, columns), f32), shape((plan.wide * nb, columns), f32)],
        [wholes[0]],
        (*pieces[0], right_side, *received),
        flops=6 * 3 * nb * nb * columns,
    )
    below = place(1, chips + 1)
    if depth % 16 == 0:
        placed, late = place(2, chips - 1), pieces[2][chips - 1 :]
    else:
        placed, late = [jnp.zeros(s.shape, s.dtype) for s in pairs[2]], pieces[2]
    out, _, _ = kernel_call(
        bound(final_kernel, plan, len(late)),
        [shape(right_side.shape, f32), *pairs[2]],
        [
            pltpu.VMEM((panels, nb, columns), f32),
            pltpu.VMEM((plan.wide, nb, columns), f32),
            wholes[2],
            pltpu.SemaphoreType.DMA((rows // nb,)),
        ],
        (*late, *placed, inv_high, inv_low, *below, x_first, total, right_side, *received),
        flops=6 * 15 * nb * nb * columns,
        out_hbm=1,
        aliases={len(late): 1, len(late) + 1: 2},
    )
    return out


def solution(mesh):
    in_specs = (P("row", "col"), P(None, "col", "row"), P(None, "col", None))
    out_specs = P("row", "col")

    return jax.shard_map(per_device, mesh=mesh, in_specs=in_specs, out_specs=out_specs, check_vma=False)
```

```python
import functools

import jax
import jax.numpy as jnp
from jax import lax
from jax.experimental import pallas as pl
from jax.experimental.pallas import tpu as pltpu
from jax.sharding import PartitionSpec as P

ROWS = ((0,), (0,))
PLAIN = ((1,), (0,))
ABOVE = ((1,), (1,))


def ring_place(chip, chips):
    return jnp.where(chip % 2 == 0, chip // 2, chips - 1 - chip // 2)


def ring_chip(place, chips):
    up = 2 * place
    down = 2 * (chips - 1 - place) + 1
    if isinstance(place, int):
        return up if place < chips // 2 else down
    return jnp.where(place < chips // 2, up, down)


def split(value):
    high = value.astype(jnp.bfloat16)
    low = (value - high.astype(jnp.float32)).astype(jnp.bfloat16)
    return high, low


def dot3(left, right, dims):
    mult = functools.partial(
        lax.dot_general, dimension_numbers=(dims, ((), ())), preferred_element_type=jnp.float32
    )
    return mult(left[0], right[0]) + (mult(left[0], right[1]) + mult(left[1], right[0]))


def kernel_call(body, out_shapes, scratch, operands, flops=0, in_hbm=0, out_hbm=0, aliases={}):
    near, hbm = pl.BlockSpec(memory_space=pltpu.VMEM), pl.BlockSpec(memory_space=pltpu.HBM)
    return pl.pallas_call(
        body,
        out_shape=out_shapes,
        in_specs=[hbm] * in_hbm + [near] * (len(operands) - in_hbm),
        out_specs=jax.tree.map(lambda _: near, out_shapes)
        if not out_hbm
        else [hbm] * out_hbm + [near] * (len(out_shapes) - out_hbm),
        input_output_aliases=aliases,
        scratch_shapes=scratch,
        cost_estimate=pl.CostEstimate(flops=flops, bytes_accessed=4 << 20, transcendentals=0),
        compiler_params=pltpu.CompilerParams(vmem_limit_bytes=20 << 20),
    )(*operands)


def ring(first, chips):
    steps = chips // 2
    nearest = []
    for place in range(chips):
        here = ring_chip(place, chips)
        nearest.append((2 * here, 2 * ring_chip((place + 1) % chips, chips)))
        nearest.append((2 * here + 1, 2 * ring_chip((place - 1) % chips, chips) + 1))
    swap = [(i, i ^ 1) for i in range(2 * chips)]
    moving = first
    pieces = [first]
    for step in range(1, steps + 1):
        moving = lax.ppermute(moving, "col", nearest)
        pieces.append(moving)
        if step < steps:
            pieces.append(lax.ppermute(moving, "col", swap))
    return pieces


def streams(chips):
    core = lax.axis_index("col") % 2
    here = ring_place(lax.axis_index("col") // 2, chips)
    found = [(lax.axis_index("col") // 2, core)]
    for step in range(1, chips // 2 + 1):
        turn = step * (1 - 2 * core)
        found.append((ring_chip((here - turn + chips) % chips, chips), core))
        if step < chips // 2:
            found.append((ring_chip((here + turn + chips) % chips, chips), 1 - core))
    return found


def assemble(piece_refs, high_ref, low_ref, whole_ref, chips, chosen=slice(None)):
    depth = piece_refs[0].shape[-2]

    def put(row, value):
        rows = pl.ds(pl.multiple_of(row, value.shape[1]), value.shape[1])
        if depth % 16 == 0:
            high_ref[:, rows, :], low_ref[:, rows, :] = split(value)
        else:
            whole_ref[:, rows, :] = value

    for ref, (chip, core) in zip(piece_refs, streams(chips)[chosen]):
        if depth % 16 == 0:
            for half in range(2):
                put((2 * chip + half) * depth, ref[jnp.where(core == 0, half, 1 - half)])
        else:
            low = jnp.where(core == 0, ref[0], ref[1])
            high = jnp.where(core == 0, ref[1], ref[0])
            put(2 * chip * depth, jnp.concatenate([low, high], axis=1))
    if depth % 16 != 0:
        high_ref[...], low_ref[...] = split(whole_ref[...])


def whole_scratch(count, nb, depth):
    return pltpu.VMEM((count, nb, nb) if depth % 16 != 0 else (1, 8, nb), jnp.float32)


class Plan:
    def __init__(self, group_count, chips, panels, nb, rows):
        self.group_count, self.chips, self.panels, self.nb = group_count, chips, panels, nb
        self.held = -(-panels // group_count)
        self.sure = panels // group_count
        self.wide = rows // nb - self.sure
        self.tri = [(rank, panel) for rank in range(1, panels) for panel in range(rank)]
        self.deep = max(
            min(rank, panels - 1) for rank in range((self.held - 1) * group_count, self.held * group_count)
        )
        low = [("low", panel, block) for panel in range(panels) for block in range(self.wide)]
        self.chunks = [
            [("inv", panel) for panel in range(panels)] + low[: self.wide],
            low[self.wide :],
            [("tri", at) for at in range(len(self.tri))],
        ]
        self.where = {b: (c, at) for c, chunk in enumerate(self.chunks) for at, b in enumerate(chunk)}

    def mat(self, mats, *block):
        chunk, at = self.where[block]
        high, low = mats[chunk]
        return high[at], low[at]

    def chosen(self, owner, sources):
        me = lax.axis_index("row")
        value = sources[0]
        for shift in range(1, self.group_count):
            value = jnp.where((me + shift) % self.group_count == owner, sources[shift], value)
        return value

    def panel_rows(self, rank, right_ref, received):
        local, owner = divmod(rank, self.group_count)
        rows = slice(local * self.nb, (local + 1) * self.nb)
        return self.chosen(owner, [right_ref[rows]] + [r[rows] for r in received])


def load_kernel(factor_hbm, inv_hbm, factor_ref, inv_ref, own_ref, sems):
    deep, _, part = own_ref.shape
    copies = [
        pltpu.make_async_copy(factor_hbm.at[:deep, :, :part], own_ref, sems.at[0]),
        pltpu.make_async_copy(factor_hbm, factor_ref, sems.at[1]),
        pltpu.make_async_copy(inv_hbm, inv_ref, sems.at[2]),
    ]
    for copy in copies:
        copy.start()
    for copy in copies:
        copy.wait()


def pack_kernel(plan, chunk, *refs):
    out_ref = refs[-1]
    for side in range(2):
        head, factor = refs[2 * side : 2 * side + 2]
        for to, (kind, *which) in enumerate(plan.chunks[chunk]):
            if kind == "low":
                panel, block = which
                at = (plan.sure + block) * plan.nb
                out_ref[side, to] = factor[panel, :, at : at + plan.nb]
            else:
                out_ref[side, to] = head[which[0]]


def tri_kernel(plan, *refs):
    *sources, out_ref = refs
    for at, (rank, panel) in enumerate(plan.tri):
        local, owner = divmod(rank, plan.group_count)
        part = slice(local * plan.nb, (local + 1) * plan.nb)
        out_ref[at] = plan.chosen(owner, [source[panel, :, part] for source in sources])


def prep_kernel(plan, *refs):
    pieces, right_ref = refs[: plan.chips], refs[plan.chips]
    received = refs[plan.chips + 1 : -6]
    high_ref, low_ref, x_ref, wait_ref, total_ref, whole_ref = refs[-6:]
    assemble(pieces, high_ref, low_ref, whole_ref, plan.chips)
    mats, nb = [(high_ref, low_ref)], plan.nb
    answer = dot3(plan.mat(mats, "inv", 0), split(plan.panel_rows(0, right_ref, received)), PLAIN)
    x_ref[...] = answer
    for panel in range(1, plan.panels):
        wait_ref[panel - 1] = plan.panel_rows(panel, right_ref, received)
    solved = split(answer)
    for block in range(plan.wide):
        at = (plan.sure + block) * nb
        total = right_ref[at : at + nb] - dot3(plan.mat(mats, "low", 0, block), solved, ROWS)
        total_ref[block * nb : (block + 1) * nb] = total


def place_kernel(plan, *refs):
    high_ref, low_ref, whole_ref = refs[-3:]
    assemble(refs[:-3], high_ref, low_ref, whole_ref, plan.chips, slice(0, len(refs) - 3))


def late_pieces(plan, late):
    return slice(plan.chips - 1, None) if late == 1 else slice(None)


def final_kernel(plan, late, *refs):
    pieces, at = refs[:late], late + 2
    mats = [refs[at : at + 2], refs[at + 2 : at + 4]]
    x_first, wait_ref, total_ref = refs[at + 4 : at + 7]
    out_hbm, high_ref, low_ref, x_ref, low_rows, whole_ref, sems = refs[-7:]
    panels, nb = plan.panels, plan.nb
    me = lax.axis_index("row")
    assemble(pieces, high_ref, low_ref, whole_ref, plan.chips, late_pieces(plan, late))
    mats.append((high_ref, low_ref))
    totals = [total_ref[block * nb : (block + 1) * nb] for block in range(plan.wide)]

    def panel_out(local):
        rank = local * plan.group_count + me
        rows = pl.ds(local * nb, nb)
        return pltpu.make_async_copy(x_ref.at[rank], out_hbm.at[rows], sems.at[local])

    def rows_out(block):
        local = plan.sure + block
        rows = pl.ds(local * nb, nb)
        return pltpu.make_async_copy(low_rows.at[block], out_hbm.at[rows], sems.at[local])

    def each_out(act, locals_=range(plan.held)):
        for local in locals_:
            if local < plan.sure:
                act(panel_out(local))
            else:
                pl.when(local * plan.group_count + me < panels)(functools.partial(act, panel_out(local)))

    def tri(rank, panel):
        return plan.mat(mats, "tri", plan.tri.index((rank, panel)))

    def inverse(panel):
        return plan.mat(mats, "inv", panel)

    answer = x_first[...]
    rests = [None] + [wait_ref[panel - 1] for panel in range(1, panels)]
    steps = [None] * 2 + [split(dot3(inverse(p), tri(p, p - 1), ABOVE)) for p in range(2, panels)]
    for panel in range(panels):
        if panel == 1:
            rest = split(rests[1] - dot3(tri(1, 0), solved, ROWS))
            answer = dot3(inverse(1), rest, PLAIN)
        elif panel > 1:
            answer = dot3(inverse(panel), split(rests[panel]), PLAIN) - dot3(steps[panel], solved, PLAIN)
        x_ref[panel] = answer
        solved = split(answer)
        for after in range(panel + 2, panels):
            rests[after] = rests[after] - dot3(tri(after, panel), solved, ROWS)
        done = (panel + 1) // plan.group_count
        if (panel + 1) % plan.group_count == 0 and done <= plan.sure:
            each_out(lambda copy: copy.start(), [done - 1])
        if panel == panels - 1:
            each_out(lambda copy: copy.start(), range(plan.sure, plan.held))
        for block in range(plan.wide):
            if panel > 0:
                mat = plan.mat(mats, "low", panel, block)
                totals[block] = totals[block] - dot3(mat, solved, ROWS)
            if panel == panels - 1:
                low_rows[block] = totals[block]
                if plan.sure + block >= plan.held:
                    rows_out(block).start()

    each_out(lambda copy: copy.wait())
    for block in range(plan.wide):
        local = plan.sure + block
        if local < plan.held:
            mine = local * plan.group_count + me >= panels
            pl.when(mine)(rows_out(block).start)
            pl.when(mine)(rows_out(block).wait)
        else:
            rows_out(block).wait()


def per_device(right_side, factor_panels, inverses):
    group_count = lax.axis_size("row")
    chips = lax.axis_size("col") // 2
    panels, depth, rows = factor_panels.shape
    nb = inverses.shape[2]
    columns = right_side.shape[1]
    plan = Plan(group_count, chips, panels, nb, rows)
    swap = [(i, i ^ 1) for i in range(2 * chips)]
    shifts = [
        [((g + shift) % group_count, g) for g in range(group_count)] for shift in range(1, group_count)
    ]
    f32, bf16 = jnp.float32, jnp.bfloat16
    shape = jax.ShapeDtypeStruct
    bound = functools.partial

    factor, inv, own = kernel_call(
        load_kernel,
        [
            shape(factor_panels.shape, f32),
            shape(inverses.shape, f32),
            shape((plan.deep, depth, plan.held * nb), f32),
        ],
        [pltpu.SemaphoreType.DMA((3,))],
        [pltpu.with_memory_space_constraint(a, pltpu.HBM) for a in (factor_panels, inverses)],
        in_hbm=2,
    )
    inv_other = lax.ppermute(inv, "col", swap)
    factor_other = lax.ppermute(factor, "col", swap)
    tri = [own] + [lax.ppermute(own, "row", pairs) for pairs in shifts]
    above = right_side[: plan.held * nb]
    received = [lax.ppermute(above, "row", pairs) for pairs in shifts]
    half = kernel_call(bound(tri_kernel, plan), shape((len(plan.tri), depth, nb), f32), [], tri)
    half_other = lax.ppermute(half, "col", swap)

    pieces = []
    for chunk, blocks in enumerate(plan.chunks):
        heads = (half, half_other) if chunk == len(plan.chunks) - 1 else (inv, inv_other)
        packed = kernel_call(
            bound(pack_kernel, plan, chunk),
            shape((2, len(blocks), depth, nb), f32),
            [],
            (heads[0], factor, heads[1], factor_other),
        )
        pieces.append(ring(packed, chips))

    pairs = [[shape((len(blocks), nb, nb), bf16)] * 2 for blocks in plan.chunks]
    wholes = [whole_scratch(len(blocks), nb, depth) for blocks in plan.chunks]

    def place(chunk, count):
        return kernel_call(
            bound(place_kernel, plan), pairs[chunk], [wholes[chunk]], pieces[chunk][:count]
        )

    inv_high, inv_low, x_first, waiting, total = kernel_call(
        bound(prep_kernel, plan),
        [
            *pairs[0],
            shape((nb, columns), f32),
            shape((panels - 1, nb, columns), f32),
            shape((plan.wide * nb, columns), f32),
        ],
        [wholes[0]],
        (*pieces[0], right_side, *received),
        flops=6 * 3 * nb * nb * columns,
    )
    below = place(1, chips)
    if depth % 16 == 0:
        placed, late = place(2, chips - 1), pieces[2][chips - 1 :]
    else:
        placed, late = [jnp.zeros(s.shape, s.dtype) for s in pairs[2]], pieces[2]
    out, _, _ = kernel_call(
        bound(final_kernel, plan, len(late)),
        [shape(right_side.shape, f32), *pairs[2]],
        [
            pltpu.VMEM((panels, nb, columns), f32),
            pltpu.VMEM((plan.wide, nb, columns), f32),
            wholes[2],
            pltpu.SemaphoreType.DMA((rows // nb,)),
        ],
        (*late, *placed, inv_high, inv_low, *below, x_first, waiting, total),
        flops=6 * 15 * nb * nb * columns,
        out_hbm=1,
        aliases={len(late): 1, len(late) + 1: 2},
    )
    return out


def solution(mesh):
    in_specs = (P("row", "col"), P(None, "col", "row"), P(None, "col", None))
    out_specs = P("row", "col")

    return jax.shard_map(per_device, mesh=mesh, in_specs=in_specs, out_specs=out_specs, check_vma=False)
```

```python
import functools

import jax
import jax.numpy as jnp
from jax import lax
from jax.experimental import pallas as pl
from jax.experimental.pallas import tpu as pltpu
from jax.sharding import PartitionSpec as P

ROWS = ((0,), (0,))
PLAIN = ((1,), (0,))
ABOVE = ((1,), (1,))


def ring_place(chip, chips):
    return jnp.where(chip % 2 == 0, chip // 2, chips - 1 - chip // 2)


def ring_chip(place, chips):
    up = 2 * place
    down = 2 * (chips - 1 - place) + 1
    if isinstance(place, int):
        return up if place < chips // 2 else down
    return jnp.where(place < chips // 2, up, down)


def split(value):
    high = value.astype(jnp.bfloat16)
    low = (value - high.astype(jnp.float32)).astype(jnp.bfloat16)
    return high, low


def dot3(left, right, dims):
    mult = functools.partial(
        lax.dot_general, dimension_numbers=(dims, ((), ())), preferred_element_type=jnp.float32
    )
    return mult(left[0], right[0]) + (mult(left[0], right[1]) + mult(left[1], right[0]))


def kernel_call(body, out_shapes, scratch, operands, flops=0, in_hbm=0, out_hbm=0, aliases={}):
    near, hbm = pl.BlockSpec(memory_space=pltpu.VMEM), pl.BlockSpec(memory_space=pltpu.HBM)
    return pl.pallas_call(
        body,
        out_shape=out_shapes,
        in_specs=[hbm] * in_hbm + [near] * (len(operands) - in_hbm),
        out_specs=jax.tree.map(lambda _: near, out_shapes)
        if not out_hbm
        else [hbm] * out_hbm + [near] * (len(out_shapes) - out_hbm),
        input_output_aliases=aliases,
        scratch_shapes=scratch,
        cost_estimate=pl.CostEstimate(flops=flops, bytes_accessed=4 << 20, transcendentals=0),
        compiler_params=pltpu.CompilerParams(vmem_limit_bytes=20 << 20),
    )(*operands)


def ring(first, chips):
    steps = chips // 2
    nearest = []
    for place in range(chips):
        here = ring_chip(place, chips)
        nearest.append((2 * here, 2 * ring_chip((place + 1) % chips, chips)))
        nearest.append((2 * here + 1, 2 * ring_chip((place - 1) % chips, chips) + 1))
    swap = [(i, i ^ 1) for i in range(2 * chips)]
    moving = first
    pieces = [first]
    for step in range(1, steps + 1):
        moving = lax.ppermute(moving, "col", nearest)
        pieces.append(moving)
        if step < steps:
            pieces.append(lax.ppermute(moving, "col", swap))
    return pieces


def streams(chips):
    core = lax.axis_index("col") % 2
    here = ring_place(lax.axis_index("col") // 2, chips)
    found = [(lax.axis_index("col") // 2, core)]
    for step in range(1, chips // 2 + 1):
        turn = step * (1 - 2 * core)
        found.append((ring_chip((here - turn + chips) % chips, chips), core))
        if step < chips // 2:
            found.append((ring_chip((here + turn + chips) % chips, chips), 1 - core))
    return found


def assemble(piece_refs, high_ref, low_ref, whole_ref, chips, chosen=slice(None)):
    depth = piece_refs[0].shape[-2]

    def put(row, value):
        rows = pl.ds(pl.multiple_of(row, value.shape[1]), value.shape[1])
        if depth % 16 == 0:
            high_ref[:, rows, :], low_ref[:, rows, :] = split(value)
        else:
            whole_ref[:, rows, :] = value

    for ref, (chip, core) in zip(piece_refs, streams(chips)[chosen]):
        if depth % 16 == 0:
            for half in range(2):
                put((2 * chip + half) * depth, ref[jnp.where(core == 0, half, 1 - half)])
        else:
            low = jnp.where(core == 0, ref[0], ref[1])
            high = jnp.where(core == 0, ref[1], ref[0])
            put(2 * chip * depth, jnp.concatenate([low, high], axis=1))
    if depth % 16 != 0:
        high_ref[...], low_ref[...] = split(whole_ref[...])


def whole_scratch(count, nb, depth):
    return pltpu.VMEM((count, nb, nb) if depth % 16 != 0 else (1, 8, nb), jnp.float32)


class Plan:
    def __init__(self, group_count, chips, panels, nb, rows):
        self.group_count, self.chips, self.panels, self.nb = group_count, chips, panels, nb
        self.held = -(-panels // group_count)
        self.sure = panels // group_count
        self.wide = rows // nb - self.sure
        self.tri = [(rank, panel) for rank in range(1, panels) for panel in range(rank)]
        self.deep = max(
            min(rank, panels - 1) for rank in range((self.held - 1) * group_count, self.held * group_count)
        )
        low = [("low", panel, block) for panel in range(panels) for block in range(self.wide)]
        self.chunks = [
            [("inv", panel) for panel in range(panels)] + low[: self.wide],
            low[self.wide :],
            [("tri", at) for at in range(len(self.tri))],
        ]
        self.where = {b: (c, at) for c, chunk in enumerate(self.chunks) for at, b in enumerate(chunk)}

    def tri_of(self, rank):
        return slice(rank * (rank - 1) // 2, rank * (rank + 1) // 2)

    def mat(self, mats, *block):
        chunk, at = self.where[block]
        high, low = mats[chunk]
        return high[at], low[at]

    def chosen(self, owner, sources):
        me = lax.axis_index("row")
        value = sources[0]
        for shift in range(1, self.group_count):
            value = jnp.where((me + shift) % self.group_count == owner, sources[shift], value)
        return value

    def panel_rows(self, rank, right_ref, received):
        local, owner = divmod(rank, self.group_count)
        rows = slice(local * self.nb, (local + 1) * self.nb)
        return self.chosen(owner, [right_ref[rows]] + [r[rows] for r in received])


def load_kernel(factor_hbm, inv_hbm, factor_ref, inv_ref, own_ref, sems):
    deep, _, part = own_ref.shape
    copies = [
        pltpu.make_async_copy(factor_hbm.at[:deep, :, :part], own_ref, sems.at[0]),
        pltpu.make_async_copy(factor_hbm, factor_ref, sems.at[1]),
        pltpu.make_async_copy(inv_hbm, inv_ref, sems.at[2]),
    ]
    for copy in copies:
        copy.start()
    for copy in copies:
        copy.wait()


def pack_kernel(plan, chunk, *refs):
    out_ref = refs[-1]
    for side in range(2):
        head, factor = refs[2 * side : 2 * side + 2]
        for to, (kind, *which) in enumerate(plan.chunks[chunk]):
            if kind == "low":
                panel, block = which
                at = (plan.sure + block) * plan.nb
                out_ref[side, to] = factor[panel, :, at : at + plan.nb]
            else:
                out_ref[side, to] = head[which[0]]


def tri_kernel(plan, *refs):
    *sources, out_ref = refs
    for at, (rank, panel) in enumerate(plan.tri):
        local, owner = divmod(rank, plan.group_count)
        part = slice(local * plan.nb, (local + 1) * plan.nb)
        out_ref[at] = plan.chosen(owner, [source[panel, :, part] for source in sources])


def prep_kernel(plan, *refs):
    pieces, right_ref = refs[: plan.chips], refs[plan.chips]
    received = refs[plan.chips + 1 : -5]
    high_ref, low_ref, start_ref, total_ref, whole_ref = refs[-5:]
    assemble(pieces, high_ref, low_ref, whole_ref, plan.chips)
    mats, nb = [(high_ref, low_ref)], plan.nb
    for panel in range(plan.panels):
        rows = split(plan.panel_rows(panel, right_ref, received))
        answer = dot3(plan.mat(mats, "inv", panel), rows, PLAIN)
        start_ref[panel] = answer
        if panel == 0:
            solved = split(answer)
    for block in range(plan.wide):
        at = (plan.sure + block) * nb
        total = right_ref[at : at + nb] - dot3(plan.mat(mats, "low", 0, block), solved, ROWS)
        total_ref[block * nb : (block + 1) * nb] = total


def place_kernel(plan, *refs):
    high_ref, low_ref, whole_ref = refs[-3:]
    assemble(refs[:-3], high_ref, low_ref, whole_ref, plan.chips, slice(0, len(refs) - 3))


def triangle_kernel(plan, count, *refs):
    inv_high, inv_low, high_ref, low_ref, tri_high, tri_low, whole_ref = refs[count:]
    assemble(refs[:count], tri_high, tri_low, whole_ref, plan.chips, slice(0, count))
    for rank in range(1, plan.panels):
        rows = plan.tri_of(rank)
        flat = (rank * plan.nb, plan.nb)
        tri = tri_high[rows].reshape(flat), tri_low[rows].reshape(flat)
        step = dot3(tri, (inv_high[rank], inv_low[rank]), ABOVE).reshape(rank, plan.nb, plan.nb)
        high_ref[rows], low_ref[rows] = split(step)


def final_kernel(plan, late, *refs):
    pieces, at = refs[:late], late + 2
    mats = [refs[at : at + 2], refs[at + 2 : at + 4]]
    start_ref, total_ref = refs[at + 4 : at + 6]
    out_hbm, high_ref, low_ref, x_ref, low_rows, sems = refs[-6:]
    panels, nb = plan.panels, plan.nb
    me = lax.axis_index("row")
    for ref, (chip, core) in zip(pieces, streams(plan.chips)[plan.chips - late :]):
        depth = ref.shape[2]
        place = pl.ds(pl.multiple_of(2 * depth * chip, 2 * depth), 2 * depth)
        sides = [ref[jnp.where(core == 0, half, 1 - half)] for half in range(2)]
        both = jnp.concatenate(sides, axis=1)
        for rank in range(1, panels):
            rows = plan.tri_of(rank)
            flat = split(both[rows].reshape(rank * 2 * depth, nb))
            step = dot3(flat, plan.mat(mats, "inv", rank), ABOVE).reshape(rank, 2 * depth, nb)
            high_ref[rows, place, :], low_ref[rows, place, :] = split(step)
    totals = [total_ref[block * nb : (block + 1) * nb] for block in range(plan.wide)]

    def panel_out(local):
        rank = local * plan.group_count + me
        rows = pl.ds(local * nb, nb)
        return pltpu.make_async_copy(x_ref.at[rank], out_hbm.at[rows], sems.at[local])

    def rows_out(block):
        local = plan.sure + block
        rows = pl.ds(local * nb, nb)
        return pltpu.make_async_copy(low_rows.at[block], out_hbm.at[rows], sems.at[local])

    def each_out(act, locals_=range(plan.held)):
        for local in locals_:
            if local < plan.sure:
                act(panel_out(local))
            else:
                pl.when(local * plan.group_count + me < panels)(functools.partial(act, panel_out(local)))

    def step(rank, panel):
        at = plan.tri.index((rank, panel))
        return high_ref[at], low_ref[at]

    def take(panel):
        for block in range(plan.wide):
            mat = plan.mat(mats, "low", panel, block)
            totals[block] = totals[block] - dot3(mat, solved[panel], ROWS)

    rests = [start_ref[panel] for panel in range(panels)]
    solved = []
    for panel in range(panels):
        x_ref[panel] = rests[panel]
        solved.append(split(rests[panel]))
        for after in range(panel + 1, panels):
            rests[after] = rests[after] - dot3(step(after, panel), solved[panel], ROWS)
        done = (panel + 1) // plan.group_count
        if (panel + 1) % plan.group_count == 0 and done <= plan.sure:
            each_out(lambda copy: copy.start(), [done - 1])
    each_out(lambda copy: copy.start(), range(plan.sure, plan.held))
    for panel in range(1, panels - 1):
        take(panel)
    for block in range(plan.wide):
        mat = plan.mat(mats, "low", panels - 1, block)
        low_rows[block] = totals[block] - dot3(mat, solved[panels - 1], ROWS)
        if plan.sure + block >= plan.held:
            rows_out(block).start()

    each_out(lambda copy: copy.wait())
    for block in range(plan.wide):
        local = plan.sure + block
        if local < plan.held:
            mine = local * plan.group_count + me >= panels
            pl.when(mine)(rows_out(block).start)
            pl.when(mine)(rows_out(block).wait)
        else:
            rows_out(block).wait()


def per_device(right_side, factor_panels, inverses):
    group_count = lax.axis_size("row")
    chips = lax.axis_size("col") // 2
    panels, depth, rows = factor_panels.shape
    nb = inverses.shape[2]
    columns = right_side.shape[1]
    plan = Plan(group_count, chips, panels, nb, rows)
    swap = [(i, i ^ 1) for i in range(2 * chips)]
    shifts = [
        [((g + shift) % group_count, g) for g in range(group_count)] for shift in range(1, group_count)
    ]
    f32, bf16 = jnp.float32, jnp.bfloat16
    shape = jax.ShapeDtypeStruct
    bound = functools.partial

    factor, inv, own = kernel_call(
        load_kernel,
        [
            shape(factor_panels.shape, f32),
            shape(inverses.shape, f32),
            shape((plan.deep, depth, plan.held * nb), f32),
        ],
        [pltpu.SemaphoreType.DMA((3,))],
        [pltpu.with_memory_space_constraint(a, pltpu.HBM) for a in (factor_panels, inverses)],
        in_hbm=2,
    )
    inv_other = lax.ppermute(inv, "col", swap)
    factor_other = lax.ppermute(factor, "col", swap)
    tri = [own] + [lax.ppermute(own, "row", pairs) for pairs in shifts]
    above = right_side[: plan.held * nb]
    received = [lax.ppermute(above, "row", pairs) for pairs in shifts]
    half = kernel_call(bound(tri_kernel, plan), shape((len(plan.tri), depth, nb), f32), [], tri)
    half_other = lax.ppermute(half, "col", swap)

    pieces = []
    for chunk, blocks in enumerate(plan.chunks):
        heads = (half, half_other) if chunk == len(plan.chunks) - 1 else (inv, inv_other)
        packed = kernel_call(
            bound(pack_kernel, plan, chunk),
            shape((2, len(blocks), depth, nb), f32),
            [],
            (heads[0], factor, heads[1], factor_other),
        )
        pieces.append(ring(packed, chips))

    pairs = [[shape((len(blocks), nb, nb), bf16)] * 2 for blocks in plan.chunks]
    wholes = [whole_scratch(len(blocks), nb, depth) for blocks in plan.chunks]

    inv_high, inv_low, start, total = kernel_call(
        bound(prep_kernel, plan),
        [
            *pairs[0],
            shape((panels, nb, columns), f32),
            shape((plan.wide * nb, columns), f32),
        ],
        [wholes[0]],
        (*pieces[0], right_side, *received),
        flops=6 * 3 * nb * nb * columns,
    )
    count = chips - 1 if depth % 16 == 0 else chips
    early, late = pieces[2][:count], pieces[2][count:]
    steps = kernel_call(
        bound(triangle_kernel, plan, count),
        pairs[2],
        [pltpu.VMEM(s.shape, s.dtype) for s in pairs[2]] + [wholes[2]],
        (*early, inv_high, inv_low),
        flops=6 * 6 * nb * nb * nb,
    )
    below = kernel_call(bound(place_kernel, plan), pairs[1], [wholes[1]], pieces[1])
    out, _, _ = kernel_call(
        bound(final_kernel, plan, len(late)),
        [shape(right_side.shape, f32), *pairs[2]],
        [
            pltpu.VMEM((panels, nb, columns), f32),
            pltpu.VMEM((plan.wide, nb, columns), f32),
            pltpu.SemaphoreType.DMA((rows // nb,)),
        ],
        (*late, *steps, inv_high, inv_low, *below, start, total),
        flops=6 * 15 * nb * nb * columns,
        out_hbm=1,
        aliases={len(late): 1, len(late) + 1: 2},
    )
    return out


def solution(mesh):
    in_specs = (P("row", "col"), P(None, "col", "row"), P(None, "col", None))
    out_specs = P("row", "col")

    return jax.shard_map(per_device, mesh=mesh, in_specs=in_specs, out_specs=out_specs, check_vma=False)
```

```python
import functools

import jax
import jax.numpy as jnp
from jax import lax
from jax.experimental import pallas as pl
from jax.experimental.pallas import tpu as pltpu
from jax.sharding import PartitionSpec as P

ROWS = ((0,), (0,))
PLAIN = ((1,), (0,))
ABOVE = ((1,), (1,))


def ring_place(chip, chips):
    return jnp.where(chip % 2 == 0, chip // 2, chips - 1 - chip // 2)


def ring_chip(place, chips):
    up = 2 * place
    down = 2 * (chips - 1 - place) + 1
    if isinstance(place, int):
        return up if place < chips // 2 else down
    return jnp.where(place < chips // 2, up, down)


def split(value):
    high = value.astype(jnp.bfloat16)
    low = (value - high.astype(jnp.float32)).astype(jnp.bfloat16)
    return high, low


def dot3(left, right, dims):
    mult = functools.partial(
        lax.dot_general, dimension_numbers=(dims, ((), ())), preferred_element_type=jnp.float32
    )
    return mult(left[0], right[0]) + (mult(left[0], right[1]) + mult(left[1], right[0]))


def kernel_call(body, out_shapes, scratch, operands, flops=0, in_hbm=0, out_hbm=0, aliases={}):
    near, hbm = pl.BlockSpec(memory_space=pltpu.VMEM), pl.BlockSpec(memory_space=pltpu.HBM)
    return pl.pallas_call(
        body,
        out_shape=out_shapes,
        in_specs=[hbm] * in_hbm + [near] * (len(operands) - in_hbm),
        out_specs=jax.tree.map(lambda _: near, out_shapes)
        if not out_hbm
        else [hbm] * out_hbm + [near] * (len(out_shapes) - out_hbm),
        input_output_aliases=aliases,
        scratch_shapes=scratch,
        cost_estimate=pl.CostEstimate(flops=flops, bytes_accessed=4 << 20, transcendentals=0),
        compiler_params=pltpu.CompilerParams(vmem_limit_bytes=20 << 20),
    )(*operands)


def ring(first, chips, halves=False):
    steps = chips // 2
    nearest = []
    for place in range(chips):
        here = ring_chip(place, chips)
        nearest.append((2 * here, 2 * ring_chip((place + 1) % chips, chips)))
        nearest.append((2 * here + 1, 2 * ring_chip((place - 1) % chips, chips) + 1))
    swap = [(i, i ^ 1) for i in range(2 * chips)]
    moving = first
    pieces = [first]
    for step in range(1, steps + 1):
        last = step == steps
        moving = lax.ppermute(moving[0] if last and halves else moving, "col", nearest)
        pieces.append(moving)
        if not last or halves:
            pieces.append(lax.ppermute(moving, "col", swap))
    return pieces


def streams(chips):
    core = lax.axis_index("col") % 2
    here = ring_place(lax.axis_index("col") // 2, chips)
    found = [(lax.axis_index("col") // 2, core)]
    for step in range(1, chips // 2 + 1):
        turn = step * (1 - 2 * core)
        found.append((ring_chip((here - turn + chips) % chips, chips), core))
        found.append((ring_chip((here + turn + chips) % chips, chips), 1 - core))
    return found


def assemble(piece_refs, high_ref, low_ref, whole_ref, chips, chosen=slice(None)):
    depth = piece_refs[0].shape[-2]

    def put(row, value):
        rows = pl.ds(pl.multiple_of(row, value.shape[1]), value.shape[1])
        if depth % 16 == 0:
            high_ref[:, rows, :], low_ref[:, rows, :] = split(value)
        else:
            whole_ref[:, rows, :] = value

    for ref, (chip, core) in zip(piece_refs, streams(chips)[chosen]):
        if len(ref.shape) == 3:
            put((2 * chip + core) * depth, ref[...])
        elif depth % 16 == 0:
            for half in range(2):
                put((2 * chip + half) * depth, ref[jnp.where(core == 0, half, 1 - half)])
        else:
            low = jnp.where(core == 0, ref[0], ref[1])
            high = jnp.where(core == 0, ref[1], ref[0])
            put(2 * chip * depth, jnp.concatenate([low, high], axis=1))
    if depth % 16 != 0:
        high_ref[...], low_ref[...] = split(whole_ref[...])


def whole_scratch(count, nb, depth):
    return pltpu.VMEM((count, nb, nb) if depth % 16 != 0 else (1, 8, nb), jnp.float32)


class Plan:
    def __init__(self, group_count, chips, panels, nb, rows):
        self.group_count, self.chips, self.panels, self.nb = group_count, chips, panels, nb
        self.held = -(-panels // group_count)
        self.sure = panels // group_count
        self.wide = rows // nb - self.sure
        self.tri = [(rank, panel) for rank in range(1, panels) for panel in range(rank)]
        self.deep = [
            min(local * group_count + group_count, panels) - 1 for local in range(self.held)
        ]
        self.sent = [(local, panel) for local in range(self.held) for panel in range(self.deep[local])]
        low = [("low", panel, block) for panel in range(panels) for block in range(self.wide)]
        self.chunks = [
            [("inv", panel) for panel in range(panels)] + low[: self.wide],
            low[self.wide :],
            [("tri", at) for at in range(len(self.tri))],
        ]
        self.where = {b: (c, at) for c, chunk in enumerate(self.chunks) for at, b in enumerate(chunk)}

    def tri_of(self, rank):
        return slice(rank * (rank - 1) // 2, rank * (rank + 1) // 2)

    def mat(self, mats, *block):
        chunk, at = self.where[block]
        high, low = mats[chunk]
        return high[at], low[at]

    def chosen(self, owner, sources):
        me = lax.axis_index("row")
        value = sources[0]
        for shift in range(1, self.group_count):
            value = jnp.where((me + shift) % self.group_count == owner, sources[shift], value)
        return value

    def panel_rows(self, rank, right_ref, received):
        local, owner = divmod(rank, self.group_count)
        rows = slice(local * self.nb, (local + 1) * self.nb)
        return self.chosen(owner, [right_ref[rows]] + [r[rows] for r in received])


def load_kernel(plan, factor_hbm, inv_hbm, factor_ref, inv_ref, own_ref, sems):
    copies = [
        pltpu.make_async_copy(factor_hbm, factor_ref, sems.at[0]),
        pltpu.make_async_copy(inv_hbm, inv_ref, sems.at[1]),
    ]
    for local, deep in enumerate(plan.deep):
        source = factor_hbm.at[:deep, :, local * plan.nb : (local + 1) * plan.nb]
        target = own_ref.at[pl.ds(plan.sent.index((local, 0)), deep)]
        copies.append(pltpu.make_async_copy(source, target, sems.at[2 + local]))
    for copy in copies:
        copy.start()
    for copy in copies:
        copy.wait()


def pack_kernel(plan, chunk, *refs):
    out_ref = refs[-1]
    for side in range(2):
        head, factor = refs[2 * side : 2 * side + 2]
        for to, (kind, *which) in enumerate(plan.chunks[chunk]):
            if kind == "low":
                panel, block = which
                at = (plan.sure + block) * plan.nb
                out_ref[side, to] = factor[panel, :, at : at + plan.nb]
            else:
                out_ref[side, to] = head[which[0]]


def tri_kernel(plan, *refs):
    *sources, out_ref = refs
    for at, (rank, panel) in enumerate(plan.tri):
        local, owner = divmod(rank, plan.group_count)
        block = plan.sent.index((local, panel))
        out_ref[at] = plan.chosen(owner, [source[block] for source in sources])


def prep_kernel(plan, *refs):
    pieces, right_ref = refs[: plan.chips], refs[plan.chips]
    received = refs[plan.chips + 1 : -5]
    high_ref, low_ref, start_ref, total_ref, whole_ref = refs[-5:]
    assemble(pieces, high_ref, low_ref, whole_ref, plan.chips)
    mats, nb = [(high_ref, low_ref)], plan.nb
    for panel in range(plan.panels):
        rows = split(plan.panel_rows(panel, right_ref, received))
        answer = dot3(plan.mat(mats, "inv", panel), rows, PLAIN)
        start_ref[panel] = answer
        if panel == 0:
            solved = split(answer)
    for block in range(plan.wide):
        at = (plan.sure + block) * nb
        total = right_ref[at : at + nb] - dot3(plan.mat(mats, "low", 0, block), solved, ROWS)
        total_ref[block * nb : (block + 1) * nb] = total


def place_kernel(plan, *refs):
    high_ref, low_ref, whole_ref = refs[-3:]
    assemble(refs[:-3], high_ref, low_ref, whole_ref, plan.chips, slice(0, len(refs) - 3))


def triangle_kernel(plan, count, *refs):
    inv_high, inv_low, high_ref, low_ref, tri_high, tri_low, whole_ref = refs[count:]
    assemble(refs[:count], tri_high, tri_low, whole_ref, plan.chips, slice(0, count))
    for rank in range(1, plan.panels):
        rows = plan.tri_of(rank)
        flat = (rank * plan.nb, plan.nb)
        tri = tri_high[rows].reshape(flat), tri_low[rows].reshape(flat)
        step = dot3(tri, (inv_high[rank], inv_low[rank]), ABOVE).reshape(rank, plan.nb, plan.nb)
        high_ref[rows], low_ref[rows] = split(step)


def final_kernel(plan, late, *refs):
    pieces, at = refs[:late], late + 2
    mats = [refs[at : at + 2], refs[at + 2 : at + 4]]
    start_ref, total_ref = refs[at + 4 : at + 6]
    out_hbm, high_ref, low_ref, x_ref, low_rows, sems = refs[-6:]
    panels, nb = plan.panels, plan.nb
    me = lax.axis_index("row")
    for ref, (chip, core) in zip(pieces, streams(plan.chips)[plan.chips - late : plan.chips]):
        depth = ref.shape[2]
        place = pl.ds(pl.multiple_of(2 * depth * chip, 2 * depth), 2 * depth)
        sides = [ref[jnp.where(core == 0, half, 1 - half)] for half in range(2)]
        both = jnp.concatenate(sides, axis=1)
        for rank in range(1, panels):
            rows = plan.tri_of(rank)
            flat = split(both[rows].reshape(rank * 2 * depth, nb))
            step = dot3(flat, plan.mat(mats, "inv", rank), ABOVE).reshape(rank, 2 * depth, nb)
            high_ref[rows, place, :], low_ref[rows, place, :] = split(step)
    totals = [total_ref[block * nb : (block + 1) * nb] for block in range(plan.wide)]

    def panel_out(local):
        rank = local * plan.group_count + me
        rows = pl.ds(local * nb, nb)
        return pltpu.make_async_copy(x_ref.at[rank], out_hbm.at[rows], sems.at[local])

    def rows_out(block):
        local = plan.sure + block
        rows = pl.ds(local * nb, nb)
        return pltpu.make_async_copy(low_rows.at[block], out_hbm.at[rows], sems.at[local])

    def each_out(act, locals_=range(plan.held)):
        for local in locals_:
            if local < plan.sure:
                act(panel_out(local))
            else:
                pl.when(local * plan.group_count + me < panels)(functools.partial(act, panel_out(local)))

    def step(rank, panel):
        at = plan.tri.index((rank, panel))
        return high_ref[at], low_ref[at]

    def take(panel):
        for block in range(plan.wide):
            mat = plan.mat(mats, "low", panel, block)
            totals[block] = totals[block] - dot3(mat, solved[panel], ROWS)

    rests = [start_ref[panel] for panel in range(panels)]
    solved = []
    for panel in range(panels):
        x_ref[panel] = rests[panel]
        solved.append(split(rests[panel]))
        for after in range(panel + 1, panels):
            rests[after] = rests[after] - dot3(step(after, panel), solved[panel], ROWS)
        done = (panel + 1) // plan.group_count
        if (panel + 1) % plan.group_count == 0 and done <= plan.sure:
            each_out(lambda copy: copy.start(), [done - 1])
    each_out(lambda copy: copy.start(), range(plan.sure, plan.held))
    for panel in range(1, panels - 1):
        take(panel)
    for block in range(plan.wide):
        mat = plan.mat(mats, "low", panels - 1, block)
        low_rows[block] = totals[block] - dot3(mat, solved[panels - 1], ROWS)
        if plan.sure + block >= plan.held:
            rows_out(block).start()

    each_out(lambda copy: copy.wait())
    for block in range(plan.wide):
        local = plan.sure + block
        if local < plan.held:
            mine = local * plan.group_count + me >= panels
            pl.when(mine)(rows_out(block).start)
            pl.when(mine)(rows_out(block).wait)
        else:
            rows_out(block).wait()


def per_device(right_side, factor_panels, inverses):
    group_count = lax.axis_size("row")
    chips = lax.axis_size("col") // 2
    panels, depth, rows = factor_panels.shape
    nb = inverses.shape[2]
    columns = right_side.shape[1]
    plan = Plan(group_count, chips, panels, nb, rows)
    swap = [(i, i ^ 1) for i in range(2 * chips)]
    shifts = [
        [((g + shift) % group_count, g) for g in range(group_count)] for shift in range(1, group_count)
    ]
    f32, bf16 = jnp.float32, jnp.bfloat16
    shape = jax.ShapeDtypeStruct
    bound = functools.partial

    factor, inv, own = kernel_call(
        bound(load_kernel, plan),
        [
            shape(factor_panels.shape, f32),
            shape(inverses.shape, f32),
            shape((len(plan.sent), depth, nb), f32),
        ],
        [pltpu.SemaphoreType.DMA((2 + plan.held,))],
        [pltpu.with_memory_space_constraint(a, pltpu.HBM) for a in (factor_panels, inverses)],
        in_hbm=2,
    )
    inv_other = lax.ppermute(inv, "col", swap)
    factor_other = lax.ppermute(factor, "col", swap)
    tri = [own] + [lax.ppermute(own, "row", pairs) for pairs in shifts]
    above = right_side[: plan.held * nb]
    received = [lax.ppermute(above, "row", pairs) for pairs in shifts]
    half = kernel_call(bound(tri_kernel, plan), shape((len(plan.tri), depth, nb), f32), [], tri)
    half_other = lax.ppermute(half, "col", swap)

    pieces = []
    for chunk, blocks in enumerate(plan.chunks):
        heads = (half, half_other) if chunk == len(plan.chunks) - 1 else (inv, inv_other)
        packed = kernel_call(
            bound(pack_kernel, plan, chunk),
            shape((2, len(blocks), depth, nb), f32),
            [],
            (heads[0], factor, heads[1], factor_other),
        )
        pieces.append(ring(packed, chips, halves=chunk == 1 and depth % 16 == 0))

    pairs = [[shape((len(blocks), nb, nb), bf16)] * 2 for blocks in plan.chunks]
    wholes = [whole_scratch(len(blocks), nb, depth) for blocks in plan.chunks]

    inv_high, inv_low, start, total = kernel_call(
        bound(prep_kernel, plan),
        [
            *pairs[0],
            shape((panels, nb, columns), f32),
            shape((plan.wide * nb, columns), f32),
        ],
        [wholes[0]],
        (*pieces[0], right_side, *received),
        flops=6 * 3 * nb * nb * columns,
    )
    count = chips - 1 if depth % 16 == 0 else chips
    early, late = pieces[2][:count], pieces[2][count:]
    steps = kernel_call(
        bound(triangle_kernel, plan, count),
        pairs[2],
        [pltpu.VMEM(s.shape, s.dtype) for s in pairs[2]] + [wholes[2]],
        (*early, inv_high, inv_low),
        flops=6 * 6 * nb * nb * nb,
    )
    below = kernel_call(bound(place_kernel, plan), pairs[1], [wholes[1]], pieces[1])
    out, _, _ = kernel_call(
        bound(final_kernel, plan, len(late)),
        [shape(right_side.shape, f32), *pairs[2]],
        [
            pltpu.VMEM((panels, nb, columns), f32),
            pltpu.VMEM((plan.wide, nb, columns), f32),
            pltpu.SemaphoreType.DMA((rows // nb,)),
        ],
        (*late, *steps, inv_high, inv_low, *below, start, total),
        flops=6 * 15 * nb * nb * columns,
        out_hbm=1,
        aliases={len(late): 1, len(late) + 1: 2},
    )
    return out


def solution(mesh):
    in_specs = (P("row", "col"), P(None, "col", "row"), P(None, "col", None))
    out_specs = P("row", "col")

    return jax.shard_map(per_device, mesh=mesh, in_specs=in_specs, out_specs=out_specs, check_vma=False)
```

```python
import functools

import jax
import jax.numpy as jnp
from jax import lax
from jax.experimental import pallas as pl
from jax.experimental.pallas import tpu as pltpu
from jax.sharding import PartitionSpec as P

ROWS = ((0,), (0,))
PLAIN = ((1,), (0,))
ABOVE = ((1,), (1,))


def ring_place(chip, chips):
    return jnp.where(chip % 2 == 0, chip // 2, chips - 1 - chip // 2)


def ring_chip(place, chips):
    up = 2 * place
    down = 2 * (chips - 1 - place) + 1
    if isinstance(place, int):
        return up if place < chips // 2 else down
    return jnp.where(place < chips // 2, up, down)


def split(value):
    high = value.astype(jnp.bfloat16)
    low = (value - high.astype(jnp.float32)).astype(jnp.bfloat16)
    return high, low


def dot3(left, right, dims):
    mult = functools.partial(
        lax.dot_general, dimension_numbers=(dims, ((), ())), preferred_element_type=jnp.float32
    )
    return mult(left[0], right[0]) + (mult(left[0], right[1]) + mult(left[1], right[0]))


def kernel_call(body, out_shapes, scratch, operands, flops=0, in_hbm=0, out_hbm=0, aliases={}):
    near, hbm = pl.BlockSpec(memory_space=pltpu.VMEM), pl.BlockSpec(memory_space=pltpu.HBM)
    return pl.pallas_call(
        body,
        out_shape=out_shapes,
        in_specs=[hbm] * in_hbm + [near] * (len(operands) - in_hbm),
        out_specs=jax.tree.map(lambda _: near, out_shapes)
        if not out_hbm
        else [hbm] * out_hbm + [near] * (len(out_shapes) - out_hbm),
        input_output_aliases=aliases,
        scratch_shapes=scratch,
        cost_estimate=pl.CostEstimate(flops=flops, bytes_accessed=4 << 20, transcendentals=0),
        compiler_params=pltpu.CompilerParams(vmem_limit_bytes=20 << 20),
    )(*operands)


def ring(first, chips, halves=False):
    steps = chips // 2
    nearest = []
    for place in range(chips):
        here = ring_chip(place, chips)
        nearest.append((2 * here, 2 * ring_chip((place + 1) % chips, chips)))
        nearest.append((2 * here + 1, 2 * ring_chip((place - 1) % chips, chips) + 1))
    swap = [(i, i ^ 1) for i in range(2 * chips)]
    moving = first
    pieces = [first]
    for step in range(1, steps + 1):
        last = step == steps
        moving = lax.ppermute(moving[0] if last and halves else moving, "col", nearest)
        pieces.append(moving)
        if not last or halves:
            pieces.append(lax.ppermute(moving, "col", swap))
    return pieces


def streams(chips):
    core = lax.axis_index("col") % 2
    here = ring_place(lax.axis_index("col") // 2, chips)
    found = [(lax.axis_index("col") // 2, core)]
    for step in range(1, chips // 2 + 1):
        turn = step * (1 - 2 * core)
        found.append((ring_chip((here - turn + chips) % chips, chips), core))
        found.append((ring_chip((here + turn + chips) % chips, chips), 1 - core))
    return found


def assemble(piece_refs, high_ref, low_ref, whole_ref, chips, chosen=slice(None)):
    depth = piece_refs[0].shape[-2]

    def put(row, value):
        rows = pl.ds(pl.multiple_of(row, value.shape[1]), value.shape[1])
        if depth % 16 == 0:
            high_ref[:, rows, :], low_ref[:, rows, :] = split(value)
        else:
            whole_ref[:, rows, :] = value

    for ref, (chip, core) in zip(piece_refs, streams(chips)[chosen]):
        if len(ref.shape) == 3:
            put((2 * chip + core) * depth, ref[...])
        elif depth % 16 == 0:
            for half in range(2):
                put((2 * chip + half) * depth, ref[jnp.where(core == 0, half, 1 - half)])
        else:
            low = jnp.where(core == 0, ref[0], ref[1])
            high = jnp.where(core == 0, ref[1], ref[0])
            put(2 * chip * depth, jnp.concatenate([low, high], axis=1))
    if depth % 16 != 0:
        high_ref[...], low_ref[...] = split(whole_ref[...])


def whole_scratch(count, nb, depth):
    return pltpu.VMEM((count, nb, nb) if depth % 16 != 0 else (1, 8, nb), jnp.float32)


class Plan:
    def __init__(self, group_count, chips, panels, nb, rows):
        self.group_count, self.chips, self.panels, self.nb = group_count, chips, panels, nb
        self.held = -(-panels // group_count)
        self.sure = panels // group_count
        self.wide = rows // nb - self.sure
        self.tri = [(rank, panel) for rank in range(1, panels) for panel in range(rank)]
        self.deep = [
            min(local * group_count + group_count, panels) - 1 for local in range(self.held)
        ]
        self.sent = [(local, panel) for local in range(self.held) for panel in range(self.deep[local])]
        low = [("low", panel, block) for panel in range(panels) for block in range(self.wide)]
        self.chunks = [
            [("inv", panel) for panel in range(panels)] + low[: self.wide],
            low[self.wide :],
            [("tri", at) for at in range(len(self.tri))],
        ]
        self.mine = self.chunks[0][:panels]
        self.mine += [("low", panel, block) for block in range(self.wide) for panel in range(panels)]
        self.where = {b: (c, at) for c, chunk in enumerate(self.chunks) for at, b in enumerate(chunk)}

    def tri_of(self, rank):
        return slice(rank * (rank - 1) // 2, rank * (rank + 1) // 2)

    def mat(self, mats, *block):
        chunk, at = self.where[block]
        high, low = mats[chunk]
        return high[at], low[at]

    def chosen(self, owner, sources):
        me = lax.axis_index("row")
        value = sources[0]
        for shift in range(1, self.group_count):
            value = jnp.where((me + shift) % self.group_count == owner, sources[shift], value)
        return value

    def panel_rows(self, rank, right_ref, received):
        local, owner = divmod(rank, self.group_count)
        rows = slice(local * self.nb, (local + 1) * self.nb)
        return self.chosen(owner, [right_ref[rows]] + [r[rows] for r in received])


def load_kernel(plan, factor_hbm, inv_hbm, mine_ref, own_ref, sems):
    panels, nb = plan.panels, plan.nb
    copies = [(inv_hbm, mine_ref.at[:panels])]
    for local, deep in enumerate(plan.deep):
        source = factor_hbm.at[:deep, :, local * nb : (local + 1) * nb]
        copies.append((source, own_ref.at[pl.ds(plan.sent.index((local, 0)), deep)]))
    for block in range(plan.wide):
        at = (plan.sure + block) * nb
        to = plan.mine.index(("low", 0, block))
        copies.append((factor_hbm.at[:, :, at : at + nb], mine_ref.at[to : to + panels]))
    copies = [pltpu.make_async_copy(*pair, sems.at[n]) for n, pair in enumerate(copies)]
    for copy in copies:
        copy.start()
    for copy in copies:
        copy.wait()


def pack_kernel(held, chosen, own_ref, other_ref, out_ref):
    for to, block in enumerate(chosen):
        out_ref[0, to] = own_ref[held.index(block)]
        out_ref[1, to] = other_ref[held.index(block)]


def tri_kernel(plan, *refs):
    *sources, out_ref = refs
    for at, (rank, panel) in enumerate(plan.tri):
        local, owner = divmod(rank, plan.group_count)
        block = plan.sent.index((local, panel))
        out_ref[at] = plan.chosen(owner, [source[block] for source in sources])


def prep_kernel(plan, *refs):
    pieces, right_ref = refs[: plan.chips], refs[plan.chips]
    received = refs[plan.chips + 1 : -5]
    high_ref, low_ref, start_ref, total_ref, whole_ref = refs[-5:]
    assemble(pieces, high_ref, low_ref, whole_ref, plan.chips)
    mats, nb = [(high_ref, low_ref)], plan.nb
    for panel in range(plan.panels):
        rows = split(plan.panel_rows(panel, right_ref, received))
        answer = dot3(plan.mat(mats, "inv", panel), rows, PLAIN)
        start_ref[panel] = answer
        if panel == 0:
            solved = split(answer)
    for block in range(plan.wide):
        at = (plan.sure + block) * nb
        total = right_ref[at : at + nb] - dot3(plan.mat(mats, "low", 0, block), solved, ROWS)
        total_ref[block * nb : (block + 1) * nb] = total


def place_kernel(plan, *refs):
    high_ref, low_ref, whole_ref = refs[-3:]
    assemble(refs[:-3], high_ref, low_ref, whole_ref, plan.chips, slice(0, len(refs) - 3))


def triangle_kernel(plan, count, *refs):
    inv_high, inv_low, high_ref, low_ref, tri_high, tri_low, whole_ref = refs[count:]
    assemble(refs[:count], tri_high, tri_low, whole_ref, plan.chips, slice(0, count))
    for rank in range(1, plan.panels):
        rows = plan.tri_of(rank)
        flat = (rank * plan.nb, plan.nb)
        tri = tri_high[rows].reshape(flat), tri_low[rows].reshape(flat)
        step = dot3(tri, (inv_high[rank], inv_low[rank]), ABOVE).reshape(rank, plan.nb, plan.nb)
        high_ref[rows], low_ref[rows] = split(step)


def final_kernel(plan, late, *refs):
    pieces, at = refs[:late], late + 2
    mats = [refs[at : at + 2], refs[at + 2 : at + 4]]
    start_ref, total_ref = refs[at + 4 : at + 6]
    out_hbm, high_ref, low_ref, x_ref, low_rows, sems = refs[-6:]
    panels, nb = plan.panels, plan.nb
    me = lax.axis_index("row")
    for ref, (chip, core) in zip(pieces, streams(plan.chips)[plan.chips - late : plan.chips]):
        depth = ref.shape[2]
        place = pl.ds(pl.multiple_of(2 * depth * chip, 2 * depth), 2 * depth)
        sides = [ref[jnp.where(core == 0, half, 1 - half)] for half in range(2)]
        both = jnp.concatenate(sides, axis=1)
        for rank in range(1, panels):
            rows = plan.tri_of(rank)
            flat = split(both[rows].reshape(rank * 2 * depth, nb))
            step = dot3(flat, plan.mat(mats, "inv", rank), ABOVE).reshape(rank, 2 * depth, nb)
            high_ref[rows, place, :], low_ref[rows, place, :] = split(step)
    totals = [total_ref[block * nb : (block + 1) * nb] for block in range(plan.wide)]

    def panel_out(local):
        rank = local * plan.group_count + me
        rows = pl.ds(local * nb, nb)
        return pltpu.make_async_copy(x_ref.at[rank], out_hbm.at[rows], sems.at[local])

    def rows_out(block):
        local = plan.sure + block
        rows = pl.ds(local * nb, nb)
        return pltpu.make_async_copy(low_rows.at[block], out_hbm.at[rows], sems.at[local])

    def each_out(act, locals_=range(plan.held)):
        for local in locals_:
            if local < plan.sure:
                act(panel_out(local))
            else:
                pl.when(local * plan.group_count + me < panels)(functools.partial(act, panel_out(local)))

    def step(rank, panel):
        at = plan.tri.index((rank, panel))
        return high_ref[at], low_ref[at]

    def take(panel):
        for block in range(plan.wide):
            mat = plan.mat(mats, "low", panel, block)
            totals[block] = totals[block] - dot3(mat, solved[panel], ROWS)

    rests = [start_ref[panel] for panel in range(panels)]
    solved = []
    for panel in range(panels):
        x_ref[panel] = rests[panel]
        solved.append(split(rests[panel]))
        for after in range(panel + 1, panels):
            rests[after] = rests[after] - dot3(step(after, panel), solved[panel], ROWS)
        done = (panel + 1) // plan.group_count
        if (panel + 1) % plan.group_count == 0 and done <= plan.sure:
            each_out(lambda copy: copy.start(), [done - 1])
    each_out(lambda copy: copy.start(), range(plan.sure, plan.held))
    for panel in range(1, panels - 1):
        take(panel)
    for block in range(plan.wide):
        mat = plan.mat(mats, "low", panels - 1, block)
        low_rows[block] = totals[block] - dot3(mat, solved[panels - 1], ROWS)
        if plan.sure + block >= plan.held:
            rows_out(block).start()

    each_out(lambda copy: copy.wait())
    for block in range(plan.wide):
        local = plan.sure + block
        if local < plan.held:
            mine = local * plan.group_count + me >= panels
            pl.when(mine)(rows_out(block).start)
            pl.when(mine)(rows_out(block).wait)
        else:
            rows_out(block).wait()


def per_device(right_side, factor_panels, inverses):
    group_count = lax.axis_size("row")
    chips = lax.axis_size("col") // 2
    panels, depth, rows = factor_panels.shape
    nb = inverses.shape[2]
    columns = right_side.shape[1]
    plan = Plan(group_count, chips, panels, nb, rows)
    swap = [(i, i ^ 1) for i in range(2 * chips)]
    shifts = [
        [((g + shift) % group_count, g) for g in range(group_count)] for shift in range(1, group_count)
    ]
    f32, bf16 = jnp.float32, jnp.bfloat16
    shape = jax.ShapeDtypeStruct
    bound = functools.partial

    mine, own = kernel_call(
        bound(load_kernel, plan),
        [shape((len(plan.mine), depth, nb), f32), shape((len(plan.sent), depth, nb), f32)],
        [pltpu.SemaphoreType.DMA((1 + plan.held + plan.wide,))],
        [pltpu.with_memory_space_constraint(a, pltpu.HBM) for a in (factor_panels, inverses)],
        in_hbm=2,
    )
    other = lax.ppermute(mine, "col", swap)
    tri = [own] + [lax.ppermute(own, "row", pairs) for pairs in shifts]
    above = right_side[: plan.held * nb]
    received = [lax.ppermute(above, "row", pairs) for pairs in shifts]
    half = kernel_call(bound(tri_kernel, plan), shape((len(plan.tri), depth, nb), f32), [], tri)
    half_other = lax.ppermute(half, "col", swap)

    pieces = []
    for chunk, blocks in enumerate(plan.chunks):
        last = chunk == len(plan.chunks) - 1
        packed = kernel_call(
            bound(pack_kernel, blocks if last else plan.mine, blocks),
            shape((2, len(blocks), depth, nb), f32),
            [],
            (half, half_other) if last else (mine, other),
        )
        pieces.append(ring(packed, chips, halves=chunk == 1 and depth % 16 == 0))

    pairs = [[shape((len(blocks), nb, nb), bf16)] * 2 for blocks in plan.chunks]
    wholes = [whole_scratch(len(blocks), nb, depth) for blocks in plan.chunks]

    inv_high, inv_low, start, total = kernel_call(
        bound(prep_kernel, plan),
        [
            *pairs[0],
            shape((panels, nb, columns), f32),
            shape((plan.wide * nb, columns), f32),
        ],
        [wholes[0]],
        (*pieces[0], right_side, *received),
        flops=6 * 3 * nb * nb * columns,
    )
    count = chips - 1 if depth % 16 == 0 else chips
    early, late = pieces[2][:count], pieces[2][count:]
    steps = kernel_call(
        bound(triangle_kernel, plan, count),
        pairs[2],
        [pltpu.VMEM(s.shape, s.dtype) for s in pairs[2]] + [wholes[2]],
        (*early, inv_high, inv_low),
        flops=6 * 6 * nb * nb * nb,
    )
    below = kernel_call(bound(place_kernel, plan), pairs[1], [wholes[1]], pieces[1])
    out, _, _ = kernel_call(
        bound(final_kernel, plan, len(late)),
        [shape(right_side.shape, f32), *pairs[2]],
        [
            pltpu.VMEM((panels, nb, columns), f32),
            pltpu.VMEM((plan.wide, nb, columns), f32),
            pltpu.SemaphoreType.DMA((rows // nb,)),
        ],
        (*late, *steps, inv_high, inv_low, *below, start, total),
        flops=6 * 15 * nb * nb * columns,
        out_hbm=1,
        aliases={len(late): 1, len(late) + 1: 2},
    )
    return out


def solution(mesh):
    in_specs = (P("row", "col"), P(None, "col", "row"), P(None, "col", None))
    out_specs = P("row", "col")

    return jax.shard_map(per_device, mesh=mesh, in_specs=in_specs, out_specs=out_specs, check_vma=False)
```

```python
import functools

import jax
import jax.numpy as jnp
from jax import lax
from jax.experimental import pallas as pl
from jax.experimental.pallas import tpu as pltpu
from jax.sharding import PartitionSpec as P

ROWS = ((0,), (0,))
PLAIN = ((1,), (0,))
ABOVE = ((1,), (1,))


def ring_place(chip, chips):
    return jnp.where(chip % 2 == 0, chip // 2, chips - 1 - chip // 2)


def ring_chip(place, chips):
    up = 2 * place
    down = 2 * (chips - 1 - place) + 1
    if isinstance(place, int):
        return up if place < chips // 2 else down
    return jnp.where(place < chips // 2, up, down)


def split(value):
    high = value.astype(jnp.bfloat16)
    low = (value - high.astype(jnp.float32)).astype(jnp.bfloat16)
    return high, low


def dot3(left, right, dims):
    mult = functools.partial(
        lax.dot_general, dimension_numbers=(dims, ((), ())), preferred_element_type=jnp.float32
    )
    return mult(left[0], right[0]) + (mult(left[0], right[1]) + mult(left[1], right[0]))


def kernel_call(body, out_shapes, scratch, operands, flops=0, in_hbm=0, out_hbm=0, aliases={}):
    near, hbm = pl.BlockSpec(memory_space=pltpu.VMEM), pl.BlockSpec(memory_space=pltpu.HBM)
    return pl.pallas_call(
        body,
        out_shape=out_shapes,
        in_specs=[hbm] * in_hbm + [near] * (len(operands) - in_hbm),
        out_specs=jax.tree.map(lambda _: near, out_shapes)
        if not out_hbm
        else [hbm] * out_hbm + [near] * (len(out_shapes) - out_hbm),
        input_output_aliases=aliases,
        scratch_shapes=scratch,
        cost_estimate=pl.CostEstimate(flops=flops, bytes_accessed=4 << 20, transcendentals=0),
        compiler_params=pltpu.CompilerParams(vmem_limit_bytes=20 << 20),
    )(*operands)


def ring(first, chips, halves=False):
    steps = chips // 2
    nearest = []
    for place in range(chips):
        here = ring_chip(place, chips)
        nearest.append((2 * here, 2 * ring_chip((place + 1) % chips, chips)))
        nearest.append((2 * here + 1, 2 * ring_chip((place - 1) % chips, chips) + 1))
    swap = [(i, i ^ 1) for i in range(2 * chips)]
    moving = first
    pieces = [first]
    for step in range(1, steps + 1):
        last = step == steps
        moving = lax.ppermute(moving[0] if last and halves else moving, "col", nearest)
        pieces.append(moving)
        if not last or halves:
            pieces.append(lax.ppermute(moving, "col", swap))
    return pieces


def streams(chips):
    core = lax.axis_index("col") % 2
    here = ring_place(lax.axis_index("col") // 2, chips)
    found = [(lax.axis_index("col") // 2, core)]
    for step in range(1, chips // 2 + 1):
        turn = step * (1 - 2 * core)
        found.append((ring_chip((here - turn + chips) % chips, chips), core))
        found.append((ring_chip((here + turn + chips) % chips, chips), 1 - core))
    return found


def assemble(piece_refs, high_ref, low_ref, whole_ref, chips, chosen=slice(None)):
    depth = piece_refs[0].shape[-2]

    def put(row, value):
        rows = pl.ds(pl.multiple_of(row, value.shape[1]), value.shape[1])
        if depth % 16 == 0:
            high_ref[:, rows, :], low_ref[:, rows, :] = split(value)
        else:
            whole_ref[:, rows, :] = value

    for ref, (chip, core) in zip(piece_refs, streams(chips)[chosen]):
        if len(ref.shape) == 3:
            put((2 * chip + core) * depth, ref[...])
        elif depth % 16 == 0:
            for half in range(2):
                put((2 * chip + half) * depth, ref[jnp.where(core == 0, half, 1 - half)])
        else:
            low = jnp.where(core == 0, ref[0], ref[1])
            high = jnp.where(core == 0, ref[1], ref[0])
            put(2 * chip * depth, jnp.concatenate([low, high], axis=1))
    if depth % 16 != 0:
        high_ref[...], low_ref[...] = split(whole_ref[...])


def whole_scratch(count, nb, depth):
    return pltpu.VMEM((count, nb, nb) if depth % 16 != 0 else (1, 8, nb), jnp.float32)


class Plan:
    def __init__(self, group_count, chips, panels, nb, rows):
        self.group_count, self.chips, self.panels, self.nb = group_count, chips, panels, nb
        self.held = -(-panels // group_count)
        self.sure = panels // group_count
        self.wide = rows // nb - self.sure
        self.tri = [(rank, panel) for rank in range(1, panels) for panel in range(rank)]
        self.deep = [
            min(local * group_count + group_count, panels) - 1 for local in range(self.held)
        ]
        self.sent = [(local, panel) for local in range(self.held) for panel in range(self.deep[local])]
        low = [("low", panel, block) for panel in range(panels) for block in range(self.wide)]
        self.chunks = [
            [("inv", panel) for panel in range(panels)] + low[: self.wide],
            low[self.wide :],
            [("tri", at) for at in range(len(self.tri))],
        ]
        later = [("low", panel, block) for block in range(self.wide) for panel in range(1, panels)]
        self.held_as = [self.chunks[0], later, self.chunks[2]]
        self.where = {b: (c, at) for c, chunk in enumerate(self.chunks) for at, b in enumerate(chunk)}

    def tri_of(self, rank):
        return slice(rank * (rank - 1) // 2, rank * (rank + 1) // 2)

    def mat(self, mats, *block):
        chunk, at = self.where[block]
        high, low = mats[chunk]
        return high[at], low[at]

    def chosen(self, owner, sources):
        me = lax.axis_index("row")
        value = sources[0]
        for shift in range(1, self.group_count):
            value = jnp.where((me + shift) % self.group_count == owner, sources[shift], value)
        return value

    def panel_rows(self, rank, right_ref, received):
        local, owner = divmod(rank, self.group_count)
        rows = slice(local * self.nb, (local + 1) * self.nb)
        return self.chosen(owner, [right_ref[rows]] + [r[rows] for r in received])


def load_kernel(plan, factor_hbm, inv_hbm, inv_ref, low_ref, own_ref, sems):
    panels, nb = plan.panels, plan.nb
    copies = [(inv_hbm, inv_ref.at[:panels])]
    for local, deep in enumerate(plan.deep):
        source = factor_hbm.at[:deep, :, local * nb : (local + 1) * nb]
        copies.append((source, own_ref.at[pl.ds(plan.sent.index((local, 0)), deep)]))
    for block in range(plan.wide):
        at = (plan.sure + block) * nb
        copies.append((factor_hbm.at[:1, :, at : at + nb], inv_ref.at[panels + block : panels + block + 1]))
        to = pl.ds(block * (panels - 1), panels - 1)
        copies.append((factor_hbm.at[1:, :, at : at + nb], low_ref.at[to]))
    copies = [pltpu.make_async_copy(*pair, sems.at[n]) for n, pair in enumerate(copies)]
    for copy in copies:
        copy.start()
    for copy in copies:
        copy.wait()


def pack_kernel(held, chosen, own_ref, other_ref, out_ref):
    for to, block in enumerate(chosen):
        out_ref[0, to] = own_ref[held.index(block)]
        out_ref[1, to] = other_ref[held.index(block)]


def tri_kernel(plan, *refs):
    *sources, out_ref = refs
    for at, (rank, panel) in enumerate(plan.tri):
        local, owner = divmod(rank, plan.group_count)
        block = plan.sent.index((local, panel))
        out_ref[at] = plan.chosen(owner, [source[block] for source in sources])


def prep_kernel(plan, *refs):
    pieces, right_ref = refs[: plan.chips], refs[plan.chips]
    received = refs[plan.chips + 1 : -5]
    high_ref, low_ref, start_ref, total_ref, whole_ref = refs[-5:]
    assemble(pieces, high_ref, low_ref, whole_ref, plan.chips)
    mats, nb = [(high_ref, low_ref)], plan.nb
    for panel in range(plan.panels):
        rows = split(plan.panel_rows(panel, right_ref, received))
        answer = dot3(plan.mat(mats, "inv", panel), rows, PLAIN)
        start_ref[panel] = answer
        if panel == 0:
            solved = split(answer)
    for block in range(plan.wide):
        at = (plan.sure + block) * nb
        total = right_ref[at : at + nb] - dot3(plan.mat(mats, "low", 0, block), solved, ROWS)
        total_ref[block * nb : (block + 1) * nb] = total


def place_kernel(plan, *refs):
    high_ref, low_ref, whole_ref = refs[-3:]
    assemble(refs[:-3], high_ref, low_ref, whole_ref, plan.chips, slice(0, len(refs) - 3))


def triangle_kernel(plan, count, *refs):
    inv_high, inv_low, high_ref, low_ref, tri_high, tri_low, whole_ref = refs[count:]
    assemble(refs[:count], tri_high, tri_low, whole_ref, plan.chips, slice(0, count))
    for rank in range(1, plan.panels):
        rows = plan.tri_of(rank)
        flat = (rank * plan.nb, plan.nb)
        tri = tri_high[rows].reshape(flat), tri_low[rows].reshape(flat)
        step = dot3(tri, (inv_high[rank], inv_low[rank]), ABOVE).reshape(rank, plan.nb, plan.nb)
        high_ref[rows], low_ref[rows] = split(step)


def final_kernel(plan, late, *refs):
    pieces, at = refs[:late], late + 2
    mats = [refs[at : at + 2], refs[at + 2 : at + 4]]
    start_ref, total_ref = refs[at + 4 : at + 6]
    out_hbm, high_ref, low_ref, x_ref, low_rows, sems = refs[-6:]
    panels, nb = plan.panels, plan.nb
    me = lax.axis_index("row")
    for ref, (chip, core) in zip(pieces, streams(plan.chips)[plan.chips - late : plan.chips]):
        depth = ref.shape[2]
        place = pl.ds(pl.multiple_of(2 * depth * chip, 2 * depth), 2 * depth)
        sides = [ref[jnp.where(core == 0, half, 1 - half)] for half in range(2)]
        both = jnp.concatenate(sides, axis=1)
        for rank in range(1, panels):
            rows = plan.tri_of(rank)
            flat = split(both[rows].reshape(rank * 2 * depth, nb))
            step = dot3(flat, plan.mat(mats, "inv", rank), ABOVE).reshape(rank, 2 * depth, nb)
            high_ref[rows, place, :], low_ref[rows, place, :] = split(step)
    totals = [total_ref[block * nb : (block + 1) * nb] for block in range(plan.wide)]

    def panel_out(local):
        rank = local * plan.group_count + me
        rows = pl.ds(local * nb, nb)
        return pltpu.make_async_copy(x_ref.at[rank], out_hbm.at[rows], sems.at[local])

    def rows_out(block):
        local = plan.sure + block
        rows = pl.ds(local * nb, nb)
        return pltpu.make_async_copy(low_rows.at[block], out_hbm.at[rows], sems.at[local])

    def each_out(act, locals_=range(plan.held)):
        for local in locals_:
            if local < plan.sure:
                act(panel_out(local))
            else:
                pl.when(local * plan.group_count + me < panels)(functools.partial(act, panel_out(local)))

    def step(rank, panel):
        at = plan.tri.index((rank, panel))
        return high_ref[at], low_ref[at]

    def take(panel):
        for block in range(plan.wide):
            mat = plan.mat(mats, "low", panel, block)
            totals[block] = totals[block] - dot3(mat, solved[panel], ROWS)

    rests = [start_ref[panel] for panel in range(panels)]
    solved = []
    for panel in range(panels):
        x_ref[panel] = rests[panel]
        solved.append(split(rests[panel]))
        for after in range(panel + 1, panels):
            rests[after] = rests[after] - dot3(step(after, panel), solved[panel], ROWS)
        done = (panel + 1) // plan.group_count
        if (panel + 1) % plan.group_count == 0 and done <= plan.sure:
            each_out(lambda copy: copy.start(), [done - 1])
    each_out(lambda copy: copy.start(), range(plan.sure, plan.held))
    for panel in range(1, panels - 1):
        take(panel)
    for block in range(plan.wide):
        mat = plan.mat(mats, "low", panels - 1, block)
        low_rows[block] = totals[block] - dot3(mat, solved[panels - 1], ROWS)
        if plan.sure + block >= plan.held:
            rows_out(block).start()

    each_out(lambda copy: copy.wait())
    for block in range(plan.wide):
        local = plan.sure + block
        if local < plan.held:
            mine = local * plan.group_count + me >= panels
            pl.when(mine)(rows_out(block).start)
            pl.when(mine)(rows_out(block).wait)
        else:
            rows_out(block).wait()


def per_device(right_side, factor_panels, inverses):
    group_count = lax.axis_size("row")
    chips = lax.axis_size("col") // 2
    panels, depth, rows = factor_panels.shape
    nb = inverses.shape[2]
    columns = right_side.shape[1]
    plan = Plan(group_count, chips, panels, nb, rows)
    swap = [(i, i ^ 1) for i in range(2 * chips)]
    shifts = [
        [((g + shift) % group_count, g) for g in range(group_count)] for shift in range(1, group_count)
    ]
    f32, bf16 = jnp.float32, jnp.bfloat16
    shape = jax.ShapeDtypeStruct
    bound = functools.partial

    mine, later, own = kernel_call(
        bound(load_kernel, plan),
        [shape((len(b), depth, nb), f32) for b in (plan.chunks[0], plan.chunks[1], plan.sent)],
        [pltpu.SemaphoreType.DMA((1 + plan.held + 2 * plan.wide,))],
        [pltpu.with_memory_space_constraint(a, pltpu.HBM) for a in (factor_panels, inverses)],
        in_hbm=2,
    )
    mine_other = lax.ppermute(mine, "col", swap)
    later_other = lax.ppermute(later, "col", swap)
    tri = [own] + [lax.ppermute(own, "row", pairs) for pairs in shifts]
    above = right_side[: plan.held * nb]
    received = [lax.ppermute(above, "row", pairs) for pairs in shifts]
    half = kernel_call(bound(tri_kernel, plan), shape((len(plan.tri), depth, nb), f32), [], tri)
    half_other = lax.ppermute(half, "col", swap)

    pieces = []
    for chunk, blocks in enumerate(plan.chunks):
        packed = kernel_call(
            bound(pack_kernel, plan.held_as[chunk], blocks),
            shape((2, len(blocks), depth, nb), f32),
            [],
            ((mine, mine_other), (later, later_other), (half, half_other))[chunk],
        )
        pieces.append(ring(packed, chips, halves=chunk == 1 and depth % 16 == 0))

    pairs = [[shape((len(blocks), nb, nb), bf16)] * 2 for blocks in plan.chunks]
    wholes = [whole_scratch(len(blocks), nb, depth) for blocks in plan.chunks]

    inv_high, inv_low, start, total = kernel_call(
        bound(prep_kernel, plan),
        [
            *pairs[0],
            shape((panels, nb, columns), f32),
            shape((plan.wide * nb, columns), f32),
        ],
        [wholes[0]],
        (*pieces[0], right_side, *received),
        flops=6 * 3 * nb * nb * columns,
    )
    count = chips - 1 if depth % 16 == 0 else chips
    early, late = pieces[2][:count], pieces[2][count:]
    steps = kernel_call(
        bound(triangle_kernel, plan, count),
        pairs[2],
        [pltpu.VMEM(s.shape, s.dtype) for s in pairs[2]] + [wholes[2]],
        (*early, inv_high, inv_low),
        flops=6 * 6 * nb * nb * nb,
    )
    below = kernel_call(bound(place_kernel, plan), pairs[1], [wholes[1]], pieces[1])
    out, _, _ = kernel_call(
        bound(final_kernel, plan, len(late)),
        [shape(right_side.shape, f32), *pairs[2]],
        [
            pltpu.VMEM((panels, nb, columns), f32),
            pltpu.VMEM((plan.wide, nb, columns), f32),
            pltpu.SemaphoreType.DMA((rows // nb,)),
        ],
        (*late, *steps, inv_high, inv_low, *below, start, total),
        flops=6 * 15 * nb * nb * columns,
        out_hbm=1,
        aliases={len(late): 1, len(late) + 1: 2},
    )
    return out


def solution(mesh):
    in_specs = (P("row", "col"), P(None, "col", "row"), P(None, "col", None))
    out_specs = P("row", "col")

    return jax.shard_map(per_device, mesh=mesh, in_specs=in_specs, out_specs=out_specs, check_vma=False)
```

```python
import functools

import jax
import jax.numpy as jnp
from jax import lax
from jax.experimental import pallas as pl
from jax.experimental.pallas import tpu as pltpu
from jax.sharding import PartitionSpec as P

ROWS = ((0,), (0,))
PLAIN = ((1,), (0,))


def ring_place(chip, chips):
    return jnp.where(chip % 2 == 0, chip // 2, chips - 1 - chip // 2)


def ring_chip(place, chips):
    up = 2 * place
    down = 2 * (chips - 1 - place) + 1
    if isinstance(place, int):
        return up if place < chips // 2 else down
    return jnp.where(place < chips // 2, up, down)


def split(value):
    high = value.astype(jnp.bfloat16)
    low = (value - high.astype(jnp.float32)).astype(jnp.bfloat16)
    return high, low


def dot3(left, right, dims):
    mult = functools.partial(
        lax.dot_general, dimension_numbers=(dims, ((), ())), preferred_element_type=jnp.float32
    )
    return mult(left[0], right[0]) + (mult(left[0], right[1]) + mult(left[1], right[0]))


def kernel_call(body, out_shapes, scratch, operands, flops=0, in_hbm=0, out_hbm=0, aliases={}):
    near, hbm = pl.BlockSpec(memory_space=pltpu.VMEM), pl.BlockSpec(memory_space=pltpu.HBM)
    return pl.pallas_call(
        body,
        out_shape=out_shapes,
        in_specs=[hbm] * in_hbm + [near] * (len(operands) - in_hbm),
        out_specs=jax.tree.map(lambda _: near, out_shapes)
        if not out_hbm
        else [hbm] * out_hbm + [near] * (len(out_shapes) - out_hbm),
        input_output_aliases=aliases,
        scratch_shapes=scratch,
        cost_estimate=pl.CostEstimate(flops=flops, bytes_accessed=4 << 20, transcendentals=0),
        compiler_params=pltpu.CompilerParams(vmem_limit_bytes=20 << 20),
    )(*operands)


def ring(first, chips, halves=False):
    steps = chips // 2
    nearest = []
    for place in range(chips):
        here = ring_chip(place, chips)
        nearest.append((2 * here, 2 * ring_chip((place + 1) % chips, chips)))
        nearest.append((2 * here + 1, 2 * ring_chip((place - 1) % chips, chips) + 1))
    swap = [(i, i ^ 1) for i in range(2 * chips)]
    moving = first
    pieces = [first]
    for step in range(1, steps + 1):
        last = step == steps
        moving = lax.ppermute(moving[0] if last and halves else moving, "col", nearest)
        pieces.append(moving)
        if not last or halves:
            pieces.append(lax.ppermute(moving, "col", swap))
    return pieces


def streams(chips):
    core = lax.axis_index("col") % 2
    here = ring_place(lax.axis_index("col") // 2, chips)
    found = [(lax.axis_index("col") // 2, core)]
    for step in range(1, chips // 2 + 1):
        turn = step * (1 - 2 * core)
        found.append((ring_chip((here - turn + chips) % chips, chips), core))
        found.append((ring_chip((here + turn + chips) % chips, chips), 1 - core))
    return found


def assemble(piece_refs, high_ref, low_ref, whole_ref, chips, chosen=slice(None)):
    depth = piece_refs[0].shape[-2]

    def put(row, value):
        rows = pl.ds(pl.multiple_of(row, value.shape[1]), value.shape[1])
        if depth % 16 == 0:
            high_ref[:, rows, :], low_ref[:, rows, :] = split(value)
        else:
            whole_ref[:, rows, :] = value

    for ref, (chip, core) in zip(piece_refs, streams(chips)[chosen]):
        if len(ref.shape) == 3:
            put((2 * chip + core) * depth, ref[...])
        elif depth % 16 == 0:
            for half in range(2):
                put((2 * chip + half) * depth, ref[jnp.where(core == 0, half, 1 - half)])
        else:
            low = jnp.where(core == 0, ref[0], ref[1])
            high = jnp.where(core == 0, ref[1], ref[0])
            put(2 * chip * depth, jnp.concatenate([low, high], axis=1))
    if depth % 16 != 0:
        high_ref[...], low_ref[...] = split(whole_ref[...])


def whole_scratch(count, nb, depth):
    return pltpu.VMEM((count, nb, nb) if depth % 16 != 0 else (1, 8, nb), jnp.float32)


class Plan:
    def __init__(self, group_count, chips, panels, nb, rows):
        self.group_count, self.chips, self.panels, self.nb = group_count, chips, panels, nb
        self.held = -(-panels // group_count)
        self.sure = panels // group_count
        self.wide = rows // nb - self.sure
        self.tri = [(rank, panel) for rank in range(1, panels) for panel in range(rank)]
        self.deep = [
            min(local * group_count + group_count, panels) - 1 for local in range(self.held)
        ]
        self.sent = [(local, panel) for local in range(self.held) for panel in range(self.deep[local])]
        low = [("low", panel, block) for panel in range(panels) for block in range(self.wide)]
        self.chunks = [
            [("inv", panel) for panel in range(panels)] + low[: self.wide],
            low[self.wide :],
            [("tri", at) for at in range(len(self.tri))],
        ]
        later = [("low", panel, block) for block in range(self.wide) for panel in range(1, panels)]
        self.held_as = [self.chunks[0], later, self.chunks[2]]
        self.where = {b: (c, at) for c, chunk in enumerate(self.chunks) for at, b in enumerate(chunk)}

    def tri_of(self, rank):
        return slice(rank * (rank - 1) // 2, rank * (rank + 1) // 2)

    def mat(self, mats, *block):
        chunk, at = self.where[block]
        high, low = mats[chunk]
        return high[at], low[at]

    def chosen(self, owner, sources):
        me = lax.axis_index("row")
        value = sources[0]
        for shift in range(1, self.group_count):
            value = jnp.where((me + shift) % self.group_count == owner, sources[shift], value)
        return value

    def panel_rows(self, rank, right_ref, received):
        local, owner = divmod(rank, self.group_count)
        rows = slice(local * self.nb, (local + 1) * self.nb)
        return self.chosen(owner, [right_ref[rows]] + [r[rows] for r in received])


def load_kernel(plan, factor_hbm, inv_hbm, inv_ref, low_ref, own_ref, sems):
    panels, nb = plan.panels, plan.nb
    copies = [(inv_hbm, inv_ref.at[:panels])]
    for local, deep in enumerate(plan.deep):
        source = factor_hbm.at[:deep, :, local * nb : (local + 1) * nb]
        copies.append((source, own_ref.at[pl.ds(plan.sent.index((local, 0)), deep)]))
    for block in range(plan.wide):
        at = (plan.sure + block) * nb
        copies.append((factor_hbm.at[:1, :, at : at + nb], inv_ref.at[panels + block : panels + block + 1]))
        to = pl.ds(block * (panels - 1), panels - 1)
        copies.append((factor_hbm.at[1:, :, at : at + nb], low_ref.at[to]))
    copies = [pltpu.make_async_copy(*pair, sems.at[n]) for n, pair in enumerate(copies)]
    for copy in copies:
        copy.start()
    for copy in copies:
        copy.wait()


def pack_kernel(held, chosen, own_ref, other_ref, out_ref):
    for to, block in enumerate(chosen):
        out_ref[0, to] = own_ref[held.index(block)]
        out_ref[1, to] = other_ref[held.index(block)]


def tri_kernel(plan, *refs):
    *sources, out_ref = refs
    for at, (rank, panel) in enumerate(plan.tri):
        local, owner = divmod(rank, plan.group_count)
        block = plan.sent.index((local, panel))
        out_ref[at] = plan.chosen(owner, [source[block] for source in sources])


def prep_kernel(plan, *refs):
    pieces, right_ref = refs[: plan.chips], refs[plan.chips]
    received = refs[plan.chips + 1 : -5]
    high_ref, low_ref, start_ref, total_ref, whole_ref = refs[-5:]
    assemble(pieces, high_ref, low_ref, whole_ref, plan.chips)
    mats, nb = [(high_ref, low_ref)], plan.nb
    for panel in range(plan.panels):
        rows = split(plan.panel_rows(panel, right_ref, received))
        answer = dot3(plan.mat(mats, "inv", panel), rows, PLAIN)
        start_ref[panel] = answer
        if panel == 0:
            solved = split(answer)
        else:
            at = plan.where[("inv", panel)][1]
            high_ref[at], low_ref[at] = high_ref[at].T, low_ref[at].T
    for block in range(plan.wide):
        at = (plan.sure + block) * nb
        total = right_ref[at : at + nb] - dot3(plan.mat(mats, "low", 0, block), solved, ROWS)
        total_ref[block * nb : (block + 1) * nb] = total


def place_kernel(plan, *refs):
    high_ref, low_ref, whole_ref = refs[-3:]
    assemble(refs[:-3], high_ref, low_ref, whole_ref, plan.chips, slice(0, len(refs) - 3))


def triangle_kernel(plan, count, *refs):
    inv_high, inv_low, high_ref, low_ref, tri_high, tri_low, whole_ref = refs[count:]
    assemble(refs[:count], tri_high, tri_low, whole_ref, plan.chips, slice(0, count))
    for rank in range(1, plan.panels):
        rows = plan.tri_of(rank)
        flat = (rank * plan.nb, plan.nb)
        tri = tri_high[rows].reshape(flat), tri_low[rows].reshape(flat)
        step = dot3(tri, (inv_high[rank], inv_low[rank]), PLAIN).reshape(rank, plan.nb, plan.nb)
        high_ref[rows], low_ref[rows] = split(step)


def final_kernel(plan, late, *refs):
    pieces, at = refs[:late], late + 2
    mats = [refs[at : at + 2], refs[at + 2 : at + 4]]
    start_ref, total_ref = refs[at + 4 : at + 6]
    out_hbm, high_ref, low_ref, x_ref, low_rows, sems = refs[-6:]
    panels, nb = plan.panels, plan.nb
    me = lax.axis_index("row")
    for ref, (chip, core) in zip(pieces, streams(plan.chips)[plan.chips - late : plan.chips]):
        depth = ref.shape[2]
        place = pl.ds(pl.multiple_of(2 * depth * chip, 2 * depth), 2 * depth)
        sides = [ref[jnp.where(core == 0, half, 1 - half)] for half in range(2)]
        both = jnp.concatenate(sides, axis=1)
        for rank in range(1, panels):
            rows = plan.tri_of(rank)
            flat = split(both[rows].reshape(rank * 2 * depth, nb))
            step = dot3(flat, plan.mat(mats, "inv", rank), PLAIN).reshape(rank, 2 * depth, nb)
            high_ref[rows, place, :], low_ref[rows, place, :] = split(step)
    totals = [total_ref[block * nb : (block + 1) * nb] for block in range(plan.wide)]

    def panel_out(local):
        rank = local * plan.group_count + me
        rows = pl.ds(local * nb, nb)
        return pltpu.make_async_copy(x_ref.at[rank], out_hbm.at[rows], sems.at[local])

    def rows_out(block):
        local = plan.sure + block
        rows = pl.ds(local * nb, nb)
        return pltpu.make_async_copy(low_rows.at[block], out_hbm.at[rows], sems.at[local])

    def each_out(act, locals_=range(plan.held)):
        for local in locals_:
            if local < plan.sure:
                act(panel_out(local))
            else:
                pl.when(local * plan.group_count + me < panels)(functools.partial(act, panel_out(local)))

    def step(rank, panel):
        at = plan.tri.index((rank, panel))
        return high_ref[at], low_ref[at]

    def take(panel):
        for block in range(plan.wide):
            mat = plan.mat(mats, "low", panel, block)
            totals[block] = totals[block] - dot3(mat, solved[panel], ROWS)

    rests = [start_ref[panel] for panel in range(panels)]
    solved = []
    for panel in range(panels):
        x_ref[panel] = rests[panel]
        solved.append(split(rests[panel]))
        for after in range(panel + 1, panels):
            rests[after] = rests[after] - dot3(step(after, panel), solved[panel], ROWS)
        done = (panel + 1) // plan.group_count
        if (panel + 1) % plan.group_count == 0 and done <= plan.sure:
            each_out(lambda copy: copy.start(), [done - 1])
    each_out(lambda copy: copy.start(), range(plan.sure, plan.held))
    for panel in range(1, panels - 1):
        take(panel)
    for block in range(plan.wide):
        mat = plan.mat(mats, "low", panels - 1, block)
        low_rows[block] = totals[block] - dot3(mat, solved[panels - 1], ROWS)
        if plan.sure + block >= plan.held:
            rows_out(block).start()

    each_out(lambda copy: copy.wait())
    for block in range(plan.wide):
        local = plan.sure + block
        if local < plan.held:
            mine = local * plan.group_count + me >= panels
            pl.when(mine)(rows_out(block).start)
            pl.when(mine)(rows_out(block).wait)
        else:
            rows_out(block).wait()


def per_device(right_side, factor_panels, inverses):
    group_count = lax.axis_size("row")
    chips = lax.axis_size("col") // 2
    panels, depth, rows = factor_panels.shape
    nb = inverses.shape[2]
    columns = right_side.shape[1]
    plan = Plan(group_count, chips, panels, nb, rows)
    swap = [(i, i ^ 1) for i in range(2 * chips)]
    shifts = [
        [((g + shift) % group_count, g) for g in range(group_count)] for shift in range(1, group_count)
    ]
    f32, bf16 = jnp.float32, jnp.bfloat16
    shape = jax.ShapeDtypeStruct
    bound = functools.partial

    mine, later, own = kernel_call(
        bound(load_kernel, plan),
        [shape((len(b), depth, nb), f32) for b in (plan.chunks[0], plan.chunks[1], plan.sent)],
        [pltpu.SemaphoreType.DMA((1 + plan.held + 2 * plan.wide,))],
        [pltpu.with_memory_space_constraint(a, pltpu.HBM) for a in (factor_panels, inverses)],
        in_hbm=2,
    )
    mine_other = lax.ppermute(mine, "col", swap)
    later_other = lax.ppermute(later, "col", swap)
    tri = [own] + [lax.ppermute(own, "row", pairs) for pairs in shifts]
    above = right_side[: plan.held * nb]
    received = [lax.ppermute(above, "row", pairs) for pairs in shifts]
    half = kernel_call(bound(tri_kernel, plan), shape((len(plan.tri), depth, nb), f32), [], tri)
    half_other = lax.ppermute(half, "col", swap)

    pieces = []
    for chunk, blocks in enumerate(plan.chunks):
        packed = kernel_call(
            bound(pack_kernel, plan.held_as[chunk], blocks),
            shape((2, len(blocks), depth, nb), f32),
            [],
            ((mine, mine_other), (later, later_other), (half, half_other))[chunk],
        )
        pieces.append(ring(packed, chips, halves=chunk == 1 and depth % 16 == 0))

    pairs = [[shape((len(blocks), nb, nb), bf16)] * 2 for blocks in plan.chunks]
    wholes = [whole_scratch(len(blocks), nb, depth) for blocks in plan.chunks]

    inv_high, inv_low, start, total = kernel_call(
        bound(prep_kernel, plan),
        [
            *pairs[0],
            shape((panels, nb, columns), f32),
            shape((plan.wide * nb, columns), f32),
        ],
        [wholes[0]],
        (*pieces[0], right_side, *received),
        flops=6 * 3 * nb * nb * columns,
    )
    count = chips - 1 if depth % 16 == 0 else chips
    early, late = pieces[2][:count], pieces[2][count:]
    steps = kernel_call(
        bound(triangle_kernel, plan, count),
        pairs[2],
        [pltpu.VMEM(s.shape, s.dtype) for s in pairs[2]] + [wholes[2]],
        (*early, inv_high, inv_low),
        flops=6 * 6 * nb * nb * nb,
    )
    below = kernel_call(bound(place_kernel, plan), pairs[1], [wholes[1]], pieces[1])
    out, _, _ = kernel_call(
        bound(final_kernel, plan, len(late)),
        [shape(right_side.shape, f32), *pairs[2]],
        [
            pltpu.VMEM((panels, nb, columns), f32),
            pltpu.VMEM((plan.wide, nb, columns), f32),
            pltpu.SemaphoreType.DMA((rows // nb,)),
        ],
        (*late, *steps, inv_high, inv_low, *below, start, total),
        flops=6 * 15 * nb * nb * columns,
        out_hbm=1,
        aliases={len(late): 1, len(late) + 1: 2},
    )
    return out


def solution(mesh):
    in_specs = (P("row", "col"), P(None, "col", "row"), P(None, "col", None))
    out_specs = P("row", "col")

    return jax.shard_map(per_device, mesh=mesh, in_specs=in_specs, out_specs=out_specs, check_vma=False)
```

```python
import functools

import jax
import jax.numpy as jnp
from jax import lax
from jax.experimental import pallas as pl
from jax.experimental.pallas import tpu as pltpu
from jax.sharding import PartitionSpec as P

ROWS = ((0,), (0,))
PLAIN = ((1,), (0,))


def ring_place(chip, chips):
    return jnp.where(chip % 2 == 0, chip // 2, chips - 1 - chip // 2)


def ring_chip(place, chips):
    up = 2 * place
    down = 2 * (chips - 1 - place) + 1
    if isinstance(place, int):
        return up if place < chips // 2 else down
    return jnp.where(place < chips // 2, up, down)


def split(value):
    high = value.astype(jnp.bfloat16)
    low = (value - high.astype(jnp.float32)).astype(jnp.bfloat16)
    return high, low


def dot3(left, right, dims):
    mult = functools.partial(
        lax.dot_general, dimension_numbers=(dims, ((), ())), preferred_element_type=jnp.float32
    )
    return mult(left[0], right[0]) + (mult(left[0], right[1]) + mult(left[1], right[0]))


def kernel_call(body, out_shapes, scratch, operands, flops=0, in_hbm=0, out_hbm=0, aliases={}):
    near, hbm = pl.BlockSpec(memory_space=pltpu.VMEM), pl.BlockSpec(memory_space=pltpu.HBM)
    return pl.pallas_call(
        body,
        out_shape=out_shapes,
        in_specs=[hbm] * in_hbm + [near] * (len(operands) - in_hbm),
        out_specs=jax.tree.map(lambda _: near, out_shapes)
        if not out_hbm
        else [hbm] * out_hbm + [near] * (len(out_shapes) - out_hbm),
        input_output_aliases=aliases,
        scratch_shapes=scratch,
        cost_estimate=pl.CostEstimate(flops=flops, bytes_accessed=4 << 20, transcendentals=0),
        compiler_params=pltpu.CompilerParams(vmem_limit_bytes=20 << 20),
    )(*operands)


def ring(first, chips, halves=False):
    steps = chips // 2
    nearest = []
    for place in range(chips):
        here = ring_chip(place, chips)
        for up, turn in ((1, 1), (0, -1)):
            there = ring_chip((place + turn) % chips, chips)
            nearest.append((2 * here + (here % 2 ^ up), 2 * there + (there % 2 ^ up)))
    swap = [(i, i ^ 1) for i in range(2 * chips)]
    moving = first
    pieces = [first]
    for step in range(1, steps + 1):
        last = step == steps
        moving = lax.ppermute(moving[0] if last and halves else moving, "col", nearest)
        pieces.append(moving)
        if not last or halves:
            pieces.append(lax.ppermute(moving, "col", swap))
    return pieces


def streams(chips):
    chip, core = lax.axis_index("col") // 2, lax.axis_index("col") % 2
    here, up = ring_place(chip, chips), (chip + core) % 2
    found = [(chip, core)]
    for step in range(1, chips // 2 + 1):
        turn = step * (2 * up - 1)
        mine = ring_chip((here - turn + chips) % chips, chips)
        other = ring_chip((here + turn + chips) % chips, chips)
        found.append((mine, (mine + up) % 2))
        found.append((other, (other + 1 - up) % 2))
    return found


def assemble(piece_refs, high_ref, low_ref, whole_ref, chips, chosen=slice(None)):
    depth = piece_refs[0].shape[-2]

    def put(row, value):
        rows = pl.ds(pl.multiple_of(row, value.shape[1]), value.shape[1])
        if depth % 16 == 0:
            high_ref[:, rows, :], low_ref[:, rows, :] = split(value)
        else:
            whole_ref[:, rows, :] = value

    for ref, (chip, core) in zip(piece_refs, streams(chips)[chosen]):
        if len(ref.shape) == 3:
            put((2 * chip + core) * depth, ref[...])
        elif depth % 16 == 0:
            for half in range(2):
                put((2 * chip + half) * depth, ref[jnp.where(core == 0, half, 1 - half)])
        else:
            low = jnp.where(core == 0, ref[0], ref[1])
            high = jnp.where(core == 0, ref[1], ref[0])
            put(2 * chip * depth, jnp.concatenate([low, high], axis=1))
    if depth % 16 != 0:
        high_ref[...], low_ref[...] = split(whole_ref[...])


def whole_scratch(count, nb, depth):
    return pltpu.VMEM((count, nb, nb) if depth % 16 != 0 else (1, 8, nb), jnp.float32)


class Plan:
    def __init__(self, group_count, chips, panels, nb, rows):
        self.group_count, self.chips, self.panels, self.nb = group_count, chips, panels, nb
        self.held = -(-panels // group_count)
        self.sure = panels // group_count
        self.wide = rows // nb - self.sure
        self.tri = [(rank, panel) for rank in range(1, panels) for panel in range(rank)]
        self.deep = [
            min(local * group_count + group_count, panels) - 1 for local in range(self.held)
        ]
        self.sent = [(local, panel) for local in range(self.held) for panel in range(self.deep[local])]
        low = [("low", panel, block) for panel in range(panels) for block in range(self.wide)]
        self.chunks = [
            [("inv", panel) for panel in range(panels)] + low[: self.wide],
            low[self.wide :],
            [("tri", at) for at in range(len(self.tri))],
        ]
        later = [("low", panel, block) for block in range(self.wide) for panel in range(1, panels)]
        self.held_as = [self.chunks[0], later, self.chunks[2]]
        self.where = {b: (c, at) for c, chunk in enumerate(self.chunks) for at, b in enumerate(chunk)}

    def tri_of(self, rank):
        return slice(rank * (rank - 1) // 2, rank * (rank + 1) // 2)

    def mat(self, mats, *block):
        chunk, at = self.where[block]
        high, low = mats[chunk]
        return high[at], low[at]

    def chosen(self, owner, sources):
        me = lax.axis_index("row")
        value = sources[0]
        for shift in range(1, self.group_count):
            value = jnp.where((me + shift) % self.group_count == owner, sources[shift], value)
        return value

    def panel_rows(self, rank, right_ref, received):
        local, owner = divmod(rank, self.group_count)
        rows = slice(local * self.nb, (local + 1) * self.nb)
        return self.chosen(owner, [right_ref[rows]] + [r[rows] for r in received])


def load_kernel(plan, factor_hbm, inv_hbm, inv_ref, low_ref, own_ref, sems):
    panels, nb = plan.panels, plan.nb
    copies = [(inv_hbm, inv_ref.at[:panels])]
    for local, deep in enumerate(plan.deep):
        source = factor_hbm.at[:deep, :, local * nb : (local + 1) * nb]
        copies.append((source, own_ref.at[pl.ds(plan.sent.index((local, 0)), deep)]))
    for block in range(plan.wide):
        at = (plan.sure + block) * nb
        copies.append((factor_hbm.at[:1, :, at : at + nb], inv_ref.at[panels + block : panels + block + 1]))
        to = pl.ds(block * (panels - 1), panels - 1)
        copies.append((factor_hbm.at[1:, :, at : at + nb], low_ref.at[to]))
    copies = [pltpu.make_async_copy(*pair, sems.at[n]) for n, pair in enumerate(copies)]
    for copy in copies:
        copy.start()
    for copy in copies:
        copy.wait()


def pack_kernel(held, chosen, own_ref, other_ref, out_ref):
    for to, block in enumerate(chosen):
        out_ref[0, to] = own_ref[held.index(block)]
        out_ref[1, to] = other_ref[held.index(block)]


def tri_kernel(plan, *refs):
    *sources, out_ref = refs
    for at, (rank, panel) in enumerate(plan.tri):
        local, owner = divmod(rank, plan.group_count)
        block = plan.sent.index((local, panel))
        out_ref[at] = plan.chosen(owner, [source[block] for source in sources])


def prep_kernel(plan, *refs):
    count = len(refs) - 5 - plan.group_count
    pieces, right_ref = refs[:count], refs[count]
    received = refs[count + 1 : -5]
    high_ref, low_ref, start_ref, total_ref, whole_ref = refs[-5:]
    assemble(pieces, high_ref, low_ref, whole_ref, plan.chips)
    mats, nb = [(high_ref, low_ref)], plan.nb
    for panel in range(plan.panels):
        rows = split(plan.panel_rows(panel, right_ref, received))
        answer = dot3(plan.mat(mats, "inv", panel), rows, PLAIN)
        start_ref[panel] = answer
        if panel == 0:
            solved = split(answer)
        else:
            at = plan.where[("inv", panel)][1]
            high_ref[at], low_ref[at] = high_ref[at].T, low_ref[at].T
    for block in range(plan.wide):
        at = (plan.sure + block) * nb
        total = right_ref[at : at + nb] - dot3(plan.mat(mats, "low", 0, block), solved, ROWS)
        total_ref[block * nb : (block + 1) * nb] = total


def place_kernel(plan, *refs):
    high_ref, low_ref, whole_ref = refs[-3:]
    assemble(refs[:-3], high_ref, low_ref, whole_ref, plan.chips, slice(0, len(refs) - 3))


def late_kernel(plan, *refs):
    *pieces, _, _, high_ref, low_ref = refs
    assemble(pieces, high_ref, low_ref, None, plan.chips, slice(plan.chips - 1, None))


def triangle_kernel(plan, count, *refs):
    inv_high, inv_low, high_ref, low_ref, tri_high, tri_low, whole_ref = refs[count:]
    assemble(refs[:count], tri_high, tri_low, whole_ref, plan.chips, slice(0, count))
    for rank in range(1, plan.panels):
        rows = plan.tri_of(rank)
        flat = (rank * plan.nb, plan.nb)
        tri = tri_high[rows].reshape(flat), tri_low[rows].reshape(flat)
        step = dot3(tri, (inv_high[rank], inv_low[rank]), PLAIN).reshape(rank, plan.nb, plan.nb)
        high_ref[rows], low_ref[rows] = split(step)


def final_kernel(plan, late, *refs):
    pieces, at = refs[:late], late + 2
    mats = [refs[at : at + 2], refs[at + 2 : at + 4]]
    start_ref, total_ref = refs[at + 4 : at + 6]
    out_hbm, high_ref, low_ref, x_ref, low_rows, sems = refs[-6:]
    panels, nb = plan.panels, plan.nb
    me = lax.axis_index("row")
    for ref, (chip, core) in zip(pieces, streams(plan.chips)[plan.chips - late : plan.chips]):
        depth = ref.shape[2]
        place = pl.ds(pl.multiple_of(2 * depth * chip, 2 * depth), 2 * depth)
        sides = [ref[jnp.where(core == 0, half, 1 - half)] for half in range(2)]
        both = jnp.concatenate(sides, axis=1)
        for rank in range(1, panels):
            rows = plan.tri_of(rank)
            flat = split(both[rows].reshape(rank * 2 * depth, nb))
            step = dot3(flat, plan.mat(mats, "inv", rank), PLAIN).reshape(rank, 2 * depth, nb)
            high_ref[rows, place, :], low_ref[rows, place, :] = split(step)
    totals = [total_ref[block * nb : (block + 1) * nb] for block in range(plan.wide)]

    def panel_out(local):
        rank = local * plan.group_count + me
        rows = pl.ds(local * nb, nb)
        return pltpu.make_async_copy(x_ref.at[rank], out_hbm.at[rows], sems.at[local])

    def rows_out(block):
        local = plan.sure + block
        rows = pl.ds(local * nb, nb)
        return pltpu.make_async_copy(low_rows.at[block], out_hbm.at[rows], sems.at[local])

    def each_out(act, locals_=range(plan.held)):
        for local in locals_:
            if local < plan.sure:
                act(panel_out(local))
            else:
                pl.when(local * plan.group_count + me < panels)(functools.partial(act, panel_out(local)))

    def step(rank, panel):
        at = plan.tri.index((rank, panel))
        return high_ref[at], low_ref[at]

    def take(panel):
        for block in range(plan.wide):
            mat = plan.mat(mats, "low", panel, block)
            totals[block] = totals[block] - dot3(mat, solved[panel], ROWS)

    rests = [start_ref[panel] for panel in range(panels)]
    solved = []
    for panel in range(panels):
        x_ref[panel] = rests[panel]
        solved.append(split(rests[panel]))
        for after in range(panel + 1, panels):
            rests[after] = rests[after] - dot3(step(after, panel), solved[panel], ROWS)
        done = (panel + 1) // plan.group_count
        if (panel + 1) % plan.group_count == 0 and done <= plan.sure:
            each_out(lambda copy: copy.start(), [done - 1])
    each_out(lambda copy: copy.start(), range(plan.sure, plan.held))
    for panel in range(1, panels - 1):
        take(panel)
    for block in range(plan.wide):
        mat = plan.mat(mats, "low", panels - 1, block)
        low_rows[block] = totals[block] - dot3(mat, solved[panels - 1], ROWS)
        if plan.sure + block >= plan.held:
            rows_out(block).start()

    each_out(lambda copy: copy.wait())
    for block in range(plan.wide):
        local = plan.sure + block
        if local < plan.held:
            mine = local * plan.group_count + me >= panels
            pl.when(mine)(rows_out(block).start)
            pl.when(mine)(rows_out(block).wait)
        else:
            rows_out(block).wait()


def per_device(right_side, factor_panels, inverses):
    group_count = lax.axis_size("row")
    chips = lax.axis_size("col") // 2
    panels, depth, rows = factor_panels.shape
    nb = inverses.shape[2]
    columns = right_side.shape[1]
    plan = Plan(group_count, chips, panels, nb, rows)
    swap = [(i, i ^ 1) for i in range(2 * chips)]
    shifts = [
        [((g + shift) % group_count, g) for g in range(group_count)] for shift in range(1, group_count)
    ]
    f32, bf16 = jnp.float32, jnp.bfloat16
    shape = jax.ShapeDtypeStruct
    bound = functools.partial

    mine, later, own = kernel_call(
        bound(load_kernel, plan),
        [shape((len(b), depth, nb), f32) for b in (plan.chunks[0], plan.chunks[1], plan.sent)],
        [pltpu.SemaphoreType.DMA((1 + plan.held + 2 * plan.wide,))],
        [pltpu.with_memory_space_constraint(a, pltpu.HBM) for a in (factor_panels, inverses)],
        in_hbm=2,
    )
    mine_other = lax.ppermute(mine, "col", swap)
    later_other = lax.ppermute(later, "col", swap)
    tri = [own] + [lax.ppermute(own, "row", pairs) for pairs in shifts]
    above = right_side[: plan.held * nb]
    received = [lax.ppermute(above, "row", pairs) for pairs in shifts]
    half = kernel_call(bound(tri_kernel, plan), shape((len(plan.tri), depth, nb), f32), [], tri)
    half_other = lax.ppermute(half, "col", swap)

    pieces = []
    for chunk, blocks in enumerate(plan.chunks):
        packed = kernel_call(
            bound(pack_kernel, plan.held_as[chunk], blocks),
            shape((2, len(blocks), depth, nb), f32),
            [],
            ((mine, mine_other), (later, later_other), (half, half_other))[chunk],
        )
        pieces.append(ring(packed, chips, halves=chunk < 2 and depth % 16 == 0))

    pairs = [[shape((len(blocks), nb, nb), bf16)] * 2 for blocks in plan.chunks]
    wholes = [whole_scratch(len(blocks), nb, depth) for blocks in plan.chunks]

    inv_high, inv_low, start, total = kernel_call(
        bound(prep_kernel, plan),
        [
            *pairs[0],
            shape((panels, nb, columns), f32),
            shape((plan.wide * nb, columns), f32),
        ],
        [wholes[0]],
        (*pieces[0], right_side, *received),
        flops=6 * 3 * nb * nb * columns,
    )
    count = chips - 1 if depth % 16 == 0 else chips
    early, late = pieces[2][:count], pieces[2][count:]
    steps = kernel_call(
        bound(triangle_kernel, plan, count),
        pairs[2],
        [pltpu.VMEM(s.shape, s.dtype) for s in pairs[2]] + [wholes[2]],
        (*early, inv_high, inv_low),
        flops=6 * 6 * nb * nb * nb,
    )
    below = kernel_call(bound(place_kernel, plan), pairs[1], [wholes[1]], pieces[1][:count])
    if count < chips:
        ends = pieces[1][count:]
        below = kernel_call(bound(late_kernel, plan), pairs[1], [], (*ends, *below), aliases={2: 0, 3: 1})
    out, _, _ = kernel_call(
        bound(final_kernel, plan, len(late)),
        [shape(right_side.shape, f32), *pairs[2]],
        [
            pltpu.VMEM((panels, nb, columns), f32),
            pltpu.VMEM((plan.wide, nb, columns), f32),
            pltpu.SemaphoreType.DMA((rows // nb,)),
        ],
        (*late, *steps, inv_high, inv_low, *below, start, total),
        flops=6 * 15 * nb * nb * columns,
        out_hbm=1,
        aliases={len(late): 1, len(late) + 1: 2},
    )
    return out


def solution(mesh):
    in_specs = (P("row", "col"), P(None, "col", "row"), P(None, "col", None))
    out_specs = P("row", "col")

    return jax.shard_map(per_device, mesh=mesh, in_specs=in_specs, out_specs=out_specs, check_vma=False)
```

```python
import functools

import jax
import jax.numpy as jnp
from jax import lax
from jax.experimental import pallas as pl
from jax.experimental.pallas import tpu as pltpu
from jax.sharding import PartitionSpec as P

ROWS = ((0,), (0,))
PLAIN = ((1,), (0,))


def ring_place(chip, chips):
    return jnp.where(chip % 2 == 0, chip // 2, chips - 1 - chip // 2)


def ring_chip(place, chips):
    up = 2 * place
    down = 2 * (chips - 1 - place) + 1
    if isinstance(place, int):
        return up if place < chips // 2 else down
    return jnp.where(place < chips // 2, up, down)


def split(value):
    high = value.astype(jnp.bfloat16)
    low = (value - high.astype(jnp.float32)).astype(jnp.bfloat16)
    return high, low


def dot3(left, right, dims):
    mult = functools.partial(
        lax.dot_general, dimension_numbers=(dims, ((), ())), preferred_element_type=jnp.float32
    )
    return mult(left[0], right[0]) + (mult(left[0], right[1]) + mult(left[1], right[0]))


def kernel_call(body, out_shapes, scratch, operands, flops=0, in_hbm=0, out_hbm=0, aliases={}):
    near, hbm = pl.BlockSpec(memory_space=pltpu.VMEM), pl.BlockSpec(memory_space=pltpu.HBM)
    return pl.pallas_call(
        body,
        out_shape=out_shapes,
        in_specs=[hbm] * in_hbm + [near] * (len(operands) - in_hbm),
        out_specs=jax.tree.map(lambda _: near, out_shapes)
        if not out_hbm
        else [hbm] * out_hbm + [near] * (len(out_shapes) - out_hbm),
        input_output_aliases=aliases,
        scratch_shapes=scratch,
        cost_estimate=pl.CostEstimate(flops=flops, bytes_accessed=4 << 20, transcendentals=0),
        compiler_params=pltpu.CompilerParams(vmem_limit_bytes=20 << 20),
    )(*operands)


def ring(first, chips, halves=False):
    steps = chips // 2
    nearest = []
    for place in range(chips):
        here = ring_chip(place, chips)
        for up, turn in ((1, 1), (0, -1)):
            there = ring_chip((place + turn) % chips, chips)
            nearest.append((2 * here + (here % 2 ^ up), 2 * there + (there % 2 ^ up)))
    swap = [(i, i ^ 1) for i in range(2 * chips)]
    moving = first
    pieces = [first]
    for step in range(1, steps + 1):
        last = step == steps
        moving = lax.ppermute(moving[0] if last and halves else moving, "col", nearest)
        pieces.append(moving)
        if not last or halves:
            pieces.append(lax.ppermute(moving, "col", swap))
    return pieces


def streams(chips):
    chip, core = lax.axis_index("col") // 2, lax.axis_index("col") % 2
    here, up = ring_place(chip, chips), (chip + core) % 2
    found = [(chip, core)]
    for step in range(1, chips // 2 + 1):
        turn = step * (2 * up - 1)
        mine = ring_chip((here - turn + chips) % chips, chips)
        other = ring_chip((here + turn + chips) % chips, chips)
        found.append((mine, (mine + up) % 2))
        found.append((other, (other + 1 - up) % 2))
    return found


def assemble(piece_refs, high_ref, low_ref, whole_ref, chips, chosen=slice(None)):
    depth = piece_refs[0].shape[-2]

    def put(row, value):
        rows = pl.ds(pl.multiple_of(row, value.shape[1]), value.shape[1])
        if depth % 16 == 0:
            high_ref[:, rows, :], low_ref[:, rows, :] = split(value)
        else:
            whole_ref[:, rows, :] = value

    for ref, (chip, core) in zip(piece_refs, streams(chips)[chosen]):
        if len(ref.shape) == 3:
            put((2 * chip + core) * depth, ref[...])
        elif depth % 16 == 0:
            for half in range(2):
                put((2 * chip + half) * depth, ref[jnp.where(core == 0, half, 1 - half)])
        else:
            low = jnp.where(core == 0, ref[0], ref[1])
            high = jnp.where(core == 0, ref[1], ref[0])
            put(2 * chip * depth, jnp.concatenate([low, high], axis=1))
    if depth % 16 != 0:
        high_ref[...], low_ref[...] = split(whole_ref[...])


def whole_scratch(count, nb, depth):
    return pltpu.VMEM((count, nb, nb) if depth % 16 != 0 else (1, 8, nb), jnp.float32)


class Plan:
    def __init__(self, group_count, chips, panels, nb, rows):
        self.group_count, self.chips, self.panels, self.nb = group_count, chips, panels, nb
        self.held = -(-panels // group_count)
        self.sure = panels // group_count
        self.wide = rows // nb - self.sure
        self.tri = [(rank, panel) for rank in range(1, panels) for panel in range(rank)]
        self.deep = [
            min(local * group_count + group_count, panels) - 1 for local in range(self.held)
        ]
        self.sent = [(local, panel) for local in range(self.held) for panel in range(self.deep[local])]
        low = [("low", panel, block) for panel in range(panels) for block in range(self.wide)]
        self.chunks = [
            [("inv", panel) for panel in range(panels)] + low[: self.wide],
            low[self.wide :],
            [("tri", at) for at in range(len(self.tri))],
        ]
        later = [("low", panel, block) for block in range(self.wide) for panel in range(1, panels)]
        self.held_as = [self.chunks[0], later, self.chunks[2]]
        self.where = {b: (c, at) for c, chunk in enumerate(self.chunks) for at, b in enumerate(chunk)}

    def tri_of(self, rank):
        return slice(rank * (rank - 1) // 2, rank * (rank + 1) // 2)

    def mat(self, mats, *block):
        chunk, at = self.where[block]
        high, low = mats[chunk]
        return high[at], low[at]

    def chosen(self, owner, sources):
        me = lax.axis_index("row")
        value = sources[0]
        for shift in range(1, self.group_count):
            value = jnp.where((me + shift) % self.group_count == owner, sources[shift], value)
        return value

    def panel_rows(self, rank, right_ref, received):
        local, owner = divmod(rank, self.group_count)
        rows = slice(local * self.nb, (local + 1) * self.nb)
        return self.chosen(owner, [right_ref[rows]] + [r[rows] for r in received])


def load_kernel(plan, factor_hbm, inv_hbm, inv_ref, low_ref, own_ref, sems):
    panels, nb = plan.panels, plan.nb
    copies = [(inv_hbm, inv_ref.at[:panels])]
    for local, deep in enumerate(plan.deep):
        source = factor_hbm.at[:deep, :, local * nb : (local + 1) * nb]
        copies.append((source, own_ref.at[pl.ds(plan.sent.index((local, 0)), deep)]))
    for block in range(plan.wide):
        at = (plan.sure + block) * nb
        copies.append((factor_hbm.at[:1, :, at : at + nb], inv_ref.at[panels + block : panels + block + 1]))
    copies.append((factor_hbm.at[1:, :, plan.sure * nb :], low_ref))
    copies = [pltpu.make_async_copy(*pair, sems.at[n]) for n, pair in enumerate(copies)]
    for copy in copies:
        copy.start()
    for copy in copies:
        copy.wait()


def pack_kernel(held, chosen, own_ref, other_ref, out_ref):
    nb = out_ref.shape[3]
    for to, block in enumerate(chosen):
        for side, ref in enumerate((own_ref, other_ref)):
            if ref.shape[2] == nb:
                out_ref[side, to] = ref[held.index(block)]
            else:
                _, panel, at = block
                out_ref[side, to] = ref[panel - 1, :, at * nb : (at + 1) * nb]


def tri_kernel(plan, *refs):
    *sources, out_ref = refs
    for at, (rank, panel) in enumerate(plan.tri):
        local, owner = divmod(rank, plan.group_count)
        block = plan.sent.index((local, panel))
        out_ref[at] = plan.chosen(owner, [source[block] for source in sources])


def prep_kernel(plan, *refs):
    pieces, right_ref = refs[: plan.chips], refs[plan.chips]
    received = refs[plan.chips + 1 : -5]
    high_ref, low_ref, start_ref, total_ref, whole_ref = refs[-5:]
    assemble(pieces, high_ref, low_ref, whole_ref, plan.chips)
    mats, nb = [(high_ref, low_ref)], plan.nb
    for panel in range(plan.panels):
        rows = split(plan.panel_rows(panel, right_ref, received))
        answer = dot3(plan.mat(mats, "inv", panel), rows, PLAIN)
        start_ref[panel] = answer
        if panel == 0:
            solved = split(answer)
        else:
            at = plan.where[("inv", panel)][1]
            high_ref[at], low_ref[at] = high_ref[at].T, low_ref[at].T
    for block in range(plan.wide):
        at = (plan.sure + block) * nb
        total = right_ref[at : at + nb] - dot3(plan.mat(mats, "low", 0, block), solved, ROWS)
        total_ref[block * nb : (block + 1) * nb] = total


def place_kernel(plan, *refs):
    high_ref, low_ref, whole_ref = refs[-3:]
    assemble(refs[:-3], high_ref, low_ref, whole_ref, plan.chips, slice(0, len(refs) - 3))


def triangle_kernel(plan, count, *refs):
    inv_high, inv_low, high_ref, low_ref, tri_high, tri_low, whole_ref = refs[count:]
    assemble(refs[:count], tri_high, tri_low, whole_ref, plan.chips, slice(0, count))
    for rank in range(1, plan.panels):
        rows = plan.tri_of(rank)
        flat = (rank * plan.nb, plan.nb)
        tri = tri_high[rows].reshape(flat), tri_low[rows].reshape(flat)
        step = dot3(tri, (inv_high[rank], inv_low[rank]), PLAIN).reshape(rank, plan.nb, plan.nb)
        high_ref[rows], low_ref[rows] = split(step)


def final_kernel(plan, late, *refs):
    pieces, at = refs[:late], late + 2
    mats = [refs[at : at + 2], refs[at + 2 : at + 4]]
    start_ref, total_ref = refs[at + 4 : at + 6]
    out_hbm, high_ref, low_ref, x_ref, low_rows, sems = refs[-6:]
    panels, nb = plan.panels, plan.nb
    me = lax.axis_index("row")
    for ref, (chip, core) in zip(pieces, streams(plan.chips)[plan.chips - late : plan.chips]):
        depth = ref.shape[2]
        place = pl.ds(pl.multiple_of(2 * depth * chip, 2 * depth), 2 * depth)
        sides = [ref[jnp.where(core == 0, half, 1 - half)] for half in range(2)]
        both = jnp.concatenate(sides, axis=1)
        for rank in range(1, panels):
            rows = plan.tri_of(rank)
            flat = split(both[rows].reshape(rank * 2 * depth, nb))
            step = dot3(flat, plan.mat(mats, "inv", rank), PLAIN).reshape(rank, 2 * depth, nb)
            high_ref[rows, place, :], low_ref[rows, place, :] = split(step)
    totals = [total_ref[block * nb : (block + 1) * nb] for block in range(plan.wide)]

    def panel_out(local):
        rank = local * plan.group_count + me
        rows = pl.ds(local * nb, nb)
        return pltpu.make_async_copy(x_ref.at[rank], out_hbm.at[rows], sems.at[local])

    def rows_out(block):
        local = plan.sure + block
        rows = pl.ds(local * nb, nb)
        return pltpu.make_async_copy(low_rows.at[block], out_hbm.at[rows], sems.at[local])

    def each_out(act, locals_=range(plan.held)):
        for local in locals_:
            if local < plan.sure:
                act(panel_out(local))
            else:
                pl.when(local * plan.group_count + me < panels)(functools.partial(act, panel_out(local)))

    def step(rank, panel):
        at = plan.tri.index((rank, panel))
        return high_ref[at], low_ref[at]

    def take(panel):
        for block in range(plan.wide):
            mat = plan.mat(mats, "low", panel, block)
            totals[block] = totals[block] - dot3(mat, solved[panel], ROWS)

    rests = [start_ref[panel] for panel in range(panels)]
    solved = []
    for panel in range(panels):
        x_ref[panel] = rests[panel]
        solved.append(split(rests[panel]))
        for after in range(panel + 1, panels):
            rests[after] = rests[after] - dot3(step(after, panel), solved[panel], ROWS)
        done = (panel + 1) // plan.group_count
        if (panel + 1) % plan.group_count == 0 and done <= plan.sure:
            each_out(lambda copy: copy.start(), [done - 1])
    each_out(lambda copy: copy.start(), range(plan.sure, plan.held))
    for panel in range(1, panels - 1):
        take(panel)
    for block in range(plan.wide):
        mat = plan.mat(mats, "low", panels - 1, block)
        low_rows[block] = totals[block] - dot3(mat, solved[panels - 1], ROWS)
        if plan.sure + block >= plan.held:
            rows_out(block).start()

    each_out(lambda copy: copy.wait())
    for block in range(plan.wide):
        local = plan.sure + block
        if local < plan.held:
            mine = local * plan.group_count + me >= panels
            pl.when(mine)(rows_out(block).start)
            pl.when(mine)(rows_out(block).wait)
        else:
            rows_out(block).wait()


def per_device(right_side, factor_panels, inverses):
    group_count = lax.axis_size("row")
    chips = lax.axis_size("col") // 2
    panels, depth, rows = factor_panels.shape
    nb = inverses.shape[2]
    columns = right_side.shape[1]
    plan = Plan(group_count, chips, panels, nb, rows)
    swap = [(i, i ^ 1) for i in range(2 * chips)]
    shifts = [
        [((g + shift) % group_count, g) for g in range(group_count)] for shift in range(1, group_count)
    ]
    f32, bf16 = jnp.float32, jnp.bfloat16
    shape = jax.ShapeDtypeStruct
    bound = functools.partial

    mine, later, own = kernel_call(
        bound(load_kernel, plan),
        [
            shape((len(plan.chunks[0]), depth, nb), f32),
            shape((panels - 1, depth, plan.wide * nb), f32),
            shape((len(plan.sent), depth, nb), f32),
        ],
        [pltpu.SemaphoreType.DMA((2 + plan.held + plan.wide,))],
        [pltpu.with_memory_space_constraint(a, pltpu.HBM) for a in (factor_panels, inverses)],
        in_hbm=2,
    )
    mine_other = lax.ppermute(mine, "col", swap)
    later_other = lax.ppermute(later, "col", swap)
    tri = [own] + [lax.ppermute(own, "row", pairs) for pairs in shifts]
    above = right_side[: plan.held * nb]
    received = [lax.ppermute(above, "row", pairs) for pairs in shifts]
    half = kernel_call(bound(tri_kernel, plan), shape((len(plan.tri), depth, nb), f32), [], tri)
    half_other = lax.ppermute(half, "col", swap)

    pieces = []
    for chunk, blocks in enumerate(plan.chunks):
        packed = kernel_call(
            bound(pack_kernel, plan.held_as[chunk], blocks),
            shape((2, len(blocks), depth, nb), f32),
            [],
            ((mine, mine_other), (later, later_other), (half, half_other))[chunk],
        )
        pieces.append(ring(packed, chips, halves=chunk == 1 and depth % 16 == 0))

    pairs = [[shape((len(blocks), nb, nb), bf16)] * 2 for blocks in plan.chunks]
    wholes = [whole_scratch(len(blocks), nb, depth) for blocks in plan.chunks]

    inv_high, inv_low, start, total = kernel_call(
        bound(prep_kernel, plan),
        [
            *pairs[0],
            shape((panels, nb, columns), f32),
            shape((plan.wide * nb, columns), f32),
        ],
        [wholes[0]],
        (*pieces[0], right_side, *received),
        flops=6 * 3 * nb * nb * columns,
    )
    count = chips - 1 if depth % 16 == 0 else chips
    early, late = pieces[2][:count], pieces[2][count:]
    steps = kernel_call(
        bound(triangle_kernel, plan, count),
        pairs[2],
        [pltpu.VMEM(s.shape, s.dtype) for s in pairs[2]] + [wholes[2]],
        (*early, inv_high, inv_low),
        flops=6 * 6 * nb * nb * nb,
    )
    below = kernel_call(bound(place_kernel, plan), pairs[1], [wholes[1]], pieces[1])
    out, _, _ = kernel_call(
        bound(final_kernel, plan, len(late)),
        [shape(right_side.shape, f32), *pairs[2]],
        [
            pltpu.VMEM((panels, nb, columns), f32),
            pltpu.VMEM((plan.wide, nb, columns), f32),
            pltpu.SemaphoreType.DMA((rows // nb,)),
        ],
        (*late, *steps, inv_high, inv_low, *below, start, total),
        flops=6 * 15 * nb * nb * columns,
        out_hbm=1,
        aliases={len(late): 1, len(late) + 1: 2},
    )
    return out


def solution(mesh):
    in_specs = (P("row", "col"), P(None, "col", "row"), P(None, "col", None))
    out_specs = P("row", "col")

    return jax.shard_map(per_device, mesh=mesh, in_specs=in_specs, out_specs=out_specs, check_vma=False)
```

```python
import functools

import jax
import jax.numpy as jnp
from jax import lax
from jax.experimental import pallas as pl
from jax.experimental.pallas import tpu as pltpu
from jax.sharding import PartitionSpec as P

ROWS = ((0,), (0,))
PLAIN = ((1,), (0,))


def ring_place(chip, chips):
    return jnp.where(chip % 2 == 0, chip // 2, chips - 1 - chip // 2)


def ring_chip(place, chips):
    up = 2 * place
    down = 2 * (chips - 1 - place) + 1
    if isinstance(place, int):
        return up if place < chips // 2 else down
    return jnp.where(place < chips // 2, up, down)


def split(value):
    high = value.astype(jnp.bfloat16)
    low = (value - high.astype(jnp.float32)).astype(jnp.bfloat16)
    return high, low


def dot3(left, right, dims):
    mult = functools.partial(
        lax.dot_general, dimension_numbers=(dims, ((), ())), preferred_element_type=jnp.float32
    )
    return mult(left[0], right[0]) + (mult(left[0], right[1]) + mult(left[1], right[0]))


def kernel_call(body, out_shapes, scratch, operands, flops=0, in_hbm=0, out_hbm=0, aliases={}):
    near, hbm = pl.BlockSpec(memory_space=pltpu.VMEM), pl.BlockSpec(memory_space=pltpu.HBM)
    return pl.pallas_call(
        body,
        out_shape=out_shapes,
        in_specs=[hbm] * in_hbm + [near] * (len(operands) - in_hbm),
        out_specs=jax.tree.map(lambda _: near, out_shapes)
        if not out_hbm
        else [hbm] * out_hbm + [near] * (len(out_shapes) - out_hbm),
        input_output_aliases=aliases,
        scratch_shapes=scratch,
        cost_estimate=pl.CostEstimate(flops=flops, bytes_accessed=4 << 20, transcendentals=0),
        compiler_params=pltpu.CompilerParams(vmem_limit_bytes=20 << 20),
    )(*operands)


def ring(first, chips, halves=False):
    steps = chips // 2
    nearest = []
    for place in range(chips):
        here = ring_chip(place, chips)
        for up, turn in ((1, 1), (0, -1)):
            there = ring_chip((place + turn) % chips, chips)
            nearest.append((2 * here + (here % 2 ^ up), 2 * there + (there % 2 ^ up)))
    swap = [(i, i ^ 1) for i in range(2 * chips)]
    moving = first
    pieces = [first]
    for step in range(1, steps + 1):
        last = step == steps
        moving = lax.ppermute(moving[0] if last and halves else moving, "col", nearest)
        pieces.append(moving)
        if not last or halves:
            pieces.append(lax.ppermute(moving, "col", swap))
    return pieces


def streams(chips):
    chip, core = lax.axis_index("col") // 2, lax.axis_index("col") % 2
    here, up = ring_place(chip, chips), (chip + core) % 2
    found = [(chip, core)]
    for step in range(1, chips // 2 + 1):
        turn = step * (2 * up - 1)
        mine = ring_chip((here - turn + chips) % chips, chips)
        other = ring_chip((here + turn + chips) % chips, chips)
        found.append((mine, (mine + up) % 2))
        found.append((other, (other + 1 - up) % 2))
    return found


def assemble(piece_refs, high_ref, low_ref, whole_ref, chips, chosen=slice(None)):
    depth = piece_refs[0].shape[-2]

    def put(row, value):
        rows = pl.ds(pl.multiple_of(row, value.shape[1]), value.shape[1])
        if depth % 16 == 0:
            high_ref[:, rows, :], low_ref[:, rows, :] = split(value)
        else:
            whole_ref[:, rows, :] = value

    for ref, (chip, core) in zip(piece_refs, streams(chips)[chosen]):
        if len(ref.shape) == 3:
            put((2 * chip + core) * depth, ref[...])
        elif depth % 16 == 0:
            for half in range(2):
                put((2 * chip + half) * depth, ref[jnp.where(core == 0, half, 1 - half)])
        else:
            low = jnp.where(core == 0, ref[0], ref[1])
            high = jnp.where(core == 0, ref[1], ref[0])
            put(2 * chip * depth, jnp.concatenate([low, high], axis=1))
    if depth % 16 != 0:
        high_ref[...], low_ref[...] = split(whole_ref[...])


def whole_scratch(count, nb, depth):
    return pltpu.VMEM((count, nb, nb) if depth % 16 != 0 else (1, 8, nb), jnp.float32)


class Plan:
    def __init__(self, group_count, chips, panels, nb, rows):
        self.group_count, self.chips, self.panels, self.nb = group_count, chips, panels, nb
        self.held = -(-panels // group_count)
        self.sure = panels // group_count
        self.wide = rows // nb - self.sure
        self.tri = [(rank, panel) for rank in range(1, panels) for panel in range(rank)]
        self.deep = [
            min(local * group_count + group_count, panels) - 1 for local in range(self.held)
        ]
        self.sent = [(local, panel) for local in range(self.held) for panel in range(self.deep[local])]
        low = [("low", panel, block) for panel in range(panels) for block in range(self.wide)]
        self.chunks = [
            [("inv", panel) for panel in range(panels)] + low[: self.wide],
            low[self.wide :],
            [("tri", at) for at in range(len(self.tri))],
        ]
        later = [("low", panel, block) for block in range(self.wide) for panel in range(1, panels)]
        self.held_as = [self.chunks[0], later, self.chunks[2]]
        self.where = {b: (c, at) for c, chunk in enumerate(self.chunks) for at, b in enumerate(chunk)}

    def tri_of(self, rank):
        return slice(rank * (rank - 1) // 2, rank * (rank + 1) // 2)

    def mat(self, mats, *block):
        chunk, at = self.where[block]
        high, low = mats[chunk]
        return high[at], low[at]

    def chosen(self, owner, sources):
        me = lax.axis_index("row")
        value = sources[0]
        for shift in range(1, self.group_count):
            value = jnp.where((me + shift) % self.group_count == owner, sources[shift], value)
        return value

    def panel_rows(self, rank, right_ref, received):
        local, owner = divmod(rank, self.group_count)
        rows = slice(local * self.nb, (local + 1) * self.nb)
        return self.chosen(owner, [right_ref[rows]] + [r[rows] for r in received])


def load_kernel(plan, factor_hbm, inv_hbm, inv_ref, low_ref, own_ref, sems):
    panels, nb = plan.panels, plan.nb
    copies = [(inv_hbm, inv_ref.at[:panels])]
    for local, deep in enumerate(plan.deep):
        source = factor_hbm.at[:deep, :, local * nb : (local + 1) * nb]
        copies.append((source, own_ref.at[pl.ds(plan.sent.index((local, 0)), deep)]))
    for block in range(plan.wide):
        at = (plan.sure + block) * nb
        copies.append((factor_hbm.at[:1, :, at : at + nb], inv_ref.at[panels + block : panels + block + 1]))
        to = pl.ds(block * (panels - 1), panels - 1)
        copies.append((factor_hbm.at[1:, :, at : at + nb], low_ref.at[to]))
    copies = [pltpu.make_async_copy(*pair, sems.at[n]) for n, pair in enumerate(copies)]
    for copy in copies:
        copy.start()
    for copy in copies:
        copy.wait()


def pack_kernel(held, chosen, own_ref, other_ref, out_ref):
    for to, block in enumerate(chosen):
        out_ref[0, to] = own_ref[held.index(block)]
        out_ref[1, to] = other_ref[held.index(block)]


def tri_kernel(plan, *refs):
    *sources, out_ref = refs
    for at, (rank, panel) in enumerate(plan.tri):
        local, owner = divmod(rank, plan.group_count)
        block = plan.sent.index((local, panel))
        out_ref[at] = plan.chosen(owner, [source[block] for source in sources])


def prep_kernel(plan, *refs):
    pieces, right_ref = refs[: plan.chips], refs[plan.chips]
    received = refs[plan.chips + 1 : -5]
    high_ref, low_ref, start_ref, total_ref, whole_ref = refs[-5:]
    assemble(pieces, high_ref, low_ref, whole_ref, plan.chips)
    mats, nb = [(high_ref, low_ref)], plan.nb
    for panel in range(plan.panels):
        rows = split(plan.panel_rows(panel, right_ref, received))
        answer = dot3(plan.mat(mats, "inv", panel), rows, PLAIN)
        start_ref[panel] = answer
        if panel == 0:
            solved = split(answer)
        else:
            at = plan.where[("inv", panel)][1]
            high_ref[at], low_ref[at] = high_ref[at].T, low_ref[at].T
    for block in range(plan.wide):
        at = (plan.sure + block) * nb
        total = right_ref[at : at + nb] - dot3(plan.mat(mats, "low", 0, block), solved, ROWS)
        total_ref[block * nb : (block + 1) * nb] = total


def place_kernel(plan, *refs):
    high_ref, low_ref, whole_ref = refs[-3:]
    assemble(refs[:-3], high_ref, low_ref, whole_ref, plan.chips, slice(0, len(refs) - 3))


def triangle_kernel(plan, count, *refs):
    inv_high, inv_low, high_ref, low_ref, tri_high, tri_low, whole_ref = refs[count:]
    assemble(refs[:count], tri_high, tri_low, whole_ref, plan.chips, slice(0, count))
    for rank in range(1, plan.panels):
        rows = plan.tri_of(rank)
        flat = (rank * plan.nb, plan.nb)
        tri = tri_high[rows].reshape(flat), tri_low[rows].reshape(flat)
        step = dot3(tri, (inv_high[rank], inv_low[rank]), PLAIN).reshape(rank, plan.nb, plan.nb)
        high_ref[rows], low_ref[rows] = split(step)


def final_kernel(plan, late, *refs):
    pieces, at = refs[:late], late + 2
    mats = [refs[at : at + 2], refs[at + 2 : at + 4]]
    start_ref, total_ref = refs[at + 4 : at + 6]
    out_hbm, high_ref, low_ref, x_ref, low_rows, sems = refs[-6:]
    panels, nb = plan.panels, plan.nb
    me = lax.axis_index("row")
    for ref, (chip, core) in zip(pieces, streams(plan.chips)[plan.chips - late : plan.chips]):
        depth = ref.shape[2]
        place = pl.ds(pl.multiple_of(2 * depth * chip, 2 * depth), 2 * depth)
        sides = [ref[jnp.where(core == 0, half, 1 - half)] for half in range(2)]
        both = jnp.concatenate(sides, axis=1)
        for rank in range(1, panels):
            rows = plan.tri_of(rank)
            flat = split(both[rows].reshape(rank * 2 * depth, nb))
            step = dot3(flat, plan.mat(mats, "inv", rank), PLAIN).reshape(rank, 2 * depth, nb)
            high_ref[rows, place, :], low_ref[rows, place, :] = split(step)
    totals = [total_ref[block * nb : (block + 1) * nb] for block in range(plan.wide)]

    def panel_out(local):
        rank = local * plan.group_count + me
        rows = pl.ds(local * nb, nb)
        return pltpu.make_async_copy(x_ref.at[rank], out_hbm.at[rows], sems.at[local])

    def rows_out(block):
        local = plan.sure + block
        rows = pl.ds(local * nb, nb)
        return pltpu.make_async_copy(low_rows.at[block], out_hbm.at[rows], sems.at[local])

    def each_out(act, locals_=range(plan.held)):
        for local in locals_:
            if local < plan.sure:
                act(panel_out(local))
            else:
                pl.when(local * plan.group_count + me < panels)(functools.partial(act, panel_out(local)))

    def step(rank, panel):
        at = plan.tri.index((rank, panel))
        return high_ref[at], low_ref[at]

    def take(panel):
        for block in range(plan.wide):
            mat = plan.mat(mats, "low", panel, block)
            totals[block] = totals[block] - dot3(mat, solved[panel], ROWS)

    rests = [start_ref[panel] for panel in range(panels)]
    solved = []
    for panel in range(panels):
        x_ref[panel] = rests[panel]
        solved.append(split(rests[panel]))
        for after in range(panel + 1, panels):
            rests[after] = rests[after] - dot3(step(after, panel), solved[panel], ROWS)
        done = (panel + 1) // plan.group_count
        if (panel + 1) % plan.group_count == 0 and done <= plan.sure:
            each_out(lambda copy: copy.start(), [done - 1])
    each_out(lambda copy: copy.start(), range(plan.sure, plan.held))
    for panel in range(1, panels - 1):
        take(panel)
    for block in range(plan.wide):
        mat = plan.mat(mats, "low", panels - 1, block)
        low_rows[block] = totals[block] - dot3(mat, solved[panels - 1], ROWS)
        if plan.sure + block >= plan.held:
            rows_out(block).start()

    each_out(lambda copy: copy.wait())
    for block in range(plan.wide):
        local = plan.sure + block
        if local < plan.held:
            mine = local * plan.group_count + me >= panels
            pl.when(mine)(rows_out(block).start)
            pl.when(mine)(rows_out(block).wait)
        else:
            rows_out(block).wait()


def per_device(right_side, factor_panels, inverses):
    group_count = lax.axis_size("row")
    chips = lax.axis_size("col") // 2
    panels, depth, rows = factor_panels.shape
    nb = inverses.shape[2]
    columns = right_side.shape[1]
    plan = Plan(group_count, chips, panels, nb, rows)
    swap = [(i, i ^ 1) for i in range(2 * chips)]
    shifts = [
        [((g + shift) % group_count, g) for g in range(group_count)] for shift in range(1, group_count)
    ]
    f32, bf16 = jnp.float32, jnp.bfloat16
    shape = jax.ShapeDtypeStruct
    bound = functools.partial

    mine, later, own = kernel_call(
        bound(load_kernel, plan),
        [shape((len(b), depth, nb), f32) for b in (plan.chunks[0], plan.chunks[1], plan.sent)],
        [pltpu.SemaphoreType.DMA((1 + plan.held + 2 * plan.wide,))],
        [pltpu.with_memory_space_constraint(a, pltpu.HBM) for a in (factor_panels, inverses)],
        in_hbm=2,
    )
    mine_other = lax.ppermute(mine, "col", swap)
    later_other = lax.ppermute(later, "col", swap)
    tri = [own] + [lax.ppermute(own, "row", pairs) for pairs in shifts]
    above = right_side[: plan.held * nb]
    received = [lax.ppermute(above, "row", pairs) for pairs in shifts]
    half = kernel_call(bound(tri_kernel, plan), shape((len(plan.tri), depth, nb), f32), [], tri)
    half_other = lax.ppermute(half, "col", swap)

    pieces = []
    for chunk, blocks in enumerate(plan.chunks):
        packed = kernel_call(
            bound(pack_kernel, plan.held_as[chunk], blocks),
            shape((2, len(blocks), depth, nb), f32),
            [],
            ((mine, mine_other), (later, later_other), (half, half_other))[chunk],
        )
        pieces.append(ring(packed, chips, halves=chunk == 1 and depth % 16 == 0))

    pairs = [[shape((len(blocks), nb, nb), bf16)] * 2 for blocks in plan.chunks]
    wholes = [whole_scratch(len(blocks), nb, depth) for blocks in plan.chunks]

    inv_high, inv_low, start, total = kernel_call(
        bound(prep_kernel, plan),
        [
            *pairs[0],
            shape((panels, nb, columns), f32),
            shape((plan.wide * nb, columns), f32),
        ],
        [wholes[0]],
        (*pieces[0], right_side, *received),
        flops=6 * 3 * nb * nb * columns,
    )
    count = chips - 1 if depth % 16 == 0 else chips
    early, late = pieces[2][:count], pieces[2][count:]
    steps = kernel_call(
        bound(triangle_kernel, plan, count),
        pairs[2],
        [pltpu.VMEM(s.shape, s.dtype) for s in pairs[2]] + [wholes[2]],
        (*early, inv_high, inv_low),
        flops=6 * 6 * nb * nb * nb,
    )
    below = kernel_call(bound(place_kernel, plan), pairs[1], [wholes[1]], pieces[1])
    out, _, _ = kernel_call(
        bound(final_kernel, plan, len(late)),
        [shape(right_side.shape, f32), *pairs[2]],
        [
            pltpu.VMEM((panels, nb, columns), f32),
            pltpu.VMEM((plan.wide, nb, columns), f32),
            pltpu.SemaphoreType.DMA((rows // nb,)),
        ],
        (*late, *steps, inv_high, inv_low, *below, start, total),
        flops=6 * 15 * nb * nb * columns,
        out_hbm=1,
        aliases={len(late): 1, len(late) + 1: 2},
    )
    return out


def solution(mesh):
    in_specs = (P("row", "col"), P(None, "col", "row"), P(None, "col", None))
    out_specs = P("row", "col")

    return jax.shard_map(per_device, mesh=mesh, in_specs=in_specs, out_specs=out_specs, check_vma=False)
```
